32 devices in a mesh: row: 4 (over x, core), col: 8 (over z, y).
Axes of the slice: x: 2, y: 2, z: 4, core: 2. Of those that a mesh axis runs over, the one named last changes fastest.
Arguments:
- hidden_in: bfloat16 [6144, 2048], P('row', 'col'), may hold values from -6 to 6
- token_order: int32 [4, 1536], P('row'), may hold values from 0 to 1535, each once within a row
- lengths: int32 [4, 3], P('row'), may hold values from 1 to 1024, 1536 in all within a row
- key_mask: int32 [6144], P('row'), may hold values 0 or 1
- routes: int32 [6144, 8], P('row'), may hold values from 0 to 63, all different within a row; in each aligned block of 1536 rows (0 to 1535, 1536 to 3071, ...) at most 240 rows name the same one
- norm1_gain: float32 [2048], P('col'), may hold values from 0.5 to 1.5
- query_gain: float32 [128], replicated, may hold values from 1.1 to 2.2
- key_gain: float32 [128], replicated, may hold values from 1.1 to 2.2
- w_query: bfloat16 [2048, 2048], P('row', 'col'), may hold values from -0.125 to 0.125
- w_key: bfloat16 [2048, 2048], P('row', 'col'), may hold values from -0.125 to 0.125
- w_value: bfloat16 [2048, 2048], P('row', 'col'), may hold values from -0.125 to 0.125
- w_out: bfloat16 [2048, 2048], P('row', 'col'), may hold values from -1 to 1
- norm2_gain: float32 [2048], P('col'), may hold values from 0.5 to 1.5
- router: bfloat16 [64, 2048], P(None, 'row'), may hold values from -0.0625 to 0.0625
- w_gate: bfloat16 [64, 2048, 1024], P('col', 'row'), may hold values from -0.125 to 0.125
- w_up: bfloat16 [64, 2048, 1024], P('col', 'row'), may hold values from -0.125 to 0.125
- w_down: bfloat16 [64, 2048, 1024], P('col', 'row'), may hold values from -0.5 to 0.5
- cotangent: bfloat16 [6144, 2048], P('row', 'col'), may hold values from -6 to 6
Outputs:
- output: bfloat16 [6144, 2048], P('row', 'col')
- grad_input: float32 [6144, 2048], P('row', 'col')
- grad_norm1: float32 [2048], P('col')
- grad_query_gain: float32 [128], replicated
- grad_key_gain: float32 [128], replicated
- grad_w_query: float32 [2048, 2048], P('row', 'col')
- grad_w_key: float32 [2048, 2048], P('row', 'col')
- grad_w_value: float32 [2048, 2048], P('row', 'col')
- grad_w_out: float32 [2048, 2048], P('row', 'col')
- grad_norm2: float32 [2048], P('col')
- grad_router: float32 [64, 2048], P(None, 'row')
- grad_w_gate: float32 [64, 2048, 1024], P('col', 'row')
- grad_w_up: float32 [64, 2048, 1024], P('col', 'row')
- grad_w_down: float32 [64, 2048, 1024], P('col', 'row')
The draws below stay inside these ranges and needn't reach their ends.
Inputs may be any that keep to these rules, and one draw needn't show every extreme that they name: Each row of token_order holds every number of 0 to 1535 once. `lengths`: each row sums to 1536; its largest entry is 1024. `routes`: a row names 8 different experts; within the rows of one group no expert is named by more than 240 rows, a bound that some block reaches.
All inputs are finite; a program needn't handle non-finite values. No bound on the sum of `key_mask` on one device may be relied on, other than what follows from the above.
Results may differ from the reference program's by a relative error of at most 0.015.
The reference program's roundings to bfloat16 on the way count: a program that leaves them out, or rounds other values in their place, can miss the bound.
Values may be sent and summed in bfloat16 or wider, within the bound.
No kernel may reach another device: no remote copies, remote signals or barrier semaphores. Data moves between devices by JAX's collectives and lax.ppermute only.
A program may use at most 512 MiB of HBM per device.

```python
import math
import jax
import jax.numpy as jnp
import numpy as np
from jax import lax

D = 2048
H = 16
DH = 128
FF = 1024
E = 64
TOP = 8
SEQS = 3
GROUPS = 4
T_R = 1536
TOKENS = 6144
LMAX = 1024
CAP = 240
N_ROW = 4


def place_ends(values, stream_key, low, high):
    longest = values.shape.index(max(values.shape))
    spots = []
    for shift in (0, 1):
        where = [jax.random.randint(jax.random.fold_in(stream_key, axis), (), 0, length) for axis, length in enumerate(values.shape)]
        where[longest] = (where[longest] + shift) % values.shape[longest]
        spots.append(tuple(where))
    return values.at[spots[0]].set(low).at[spots[1]].set(high)


def block_scale(rng, dims, pieces, least, high):
    factor_of, own = 1.0, jax.random.fold_in(rng, 6)
    for dim, parts in pieces:
        heights = jnp.exp(jax.random.uniform(jax.random.fold_in(own, dim), (parts,), jnp.float32, least / len(pieces), high / len(pieces)))
        factor_of = factor_of * jnp.repeat(heights, dims[dim] // parts).reshape([-1 if axis == dim else 1 for axis in range(len(dims))])
    return factor_of


def length_profile(amount, total, reach, skew):
    weights = [(1 << 20) // math.isqrt(standing ** skew) + 1 for standing in range(2, amount + 1)]
    rest, counts = total - reach - (amount - 1), [1] * (amount - 1)
    while rest > 0:
        free = [i for i in range(amount - 1) if counts[i] < reach]
        whole, left = sum([weights[i] for i in free]), rest
        for i in free:
            more = min(reach - counts[i], max(1, left * weights[i] // whole), rest)
            counts[i] = counts[i] + more
            rest = rest - more
    return np.array([reach] + counts)


def ragged(own_key, number_of, total, reach, slope):
    if number_of == 2:
        one = jax.random.randint(own_key, (), max(1, total - reach), min(reach, total - 1) + 1)
        return jnp.stack([one, total - one])
    sizes = jnp.asarray(length_profile(number_of, total, reach, slope), jnp.int32)
    pairs = (number_of - 1) // 2
    source_of, taker = sizes[1:1 + 2 * pairs:2], sizes[2:2 + 2 * pairs:2]
    room = jnp.minimum(source_of - 1, reach - taker)
    shifted = jax.random.randint(jax.random.fold_in(own_key, 1), (pairs,), 0, 1 << 20) % (room + 1)
    sizes = sizes.at[1:1 + 2 * pairs:2].set(source_of - shifted).at[2:2 + 2 * pairs:2].set(taker + shifted)
    return sizes[jax.random.permutation(jax.random.fold_in(own_key, 2), number_of)]


def assign_block(rng, own, number, rows, count, top, limit, slope):
    order = jax.random.permutation(rng, count)
    crowded, common = shares(count, rows * top, limit, slope, True), shares(count, rows * top, limit, slope, False)
    places = jnp.arange(count)

    def named(tallies, rotation):
        used = int((tallies > 0).sum())
        fixed = max(1, used // 4)
        shifted = fixed + (places - fixed + rotation * (used - fixed)) % max(1, count - fixed)
        return jnp.zeros((count,), jnp.int32).at[order[jnp.where(places < fixed, places, shifted)]].set(jnp.asarray(tallies, jnp.int32))

    tallies = jnp.where(number % 4 == 0, named(crowded, number // 4), named(common, number - number // 4 - 1))
    mixed = jax.random.permutation(jax.random.fold_in(own, 3), count)
    giver, sink = mixed[0:count // 2 * 2:2], mixed[1:count // 2 * 2:2]
    slack = jnp.minimum(tallies[giver] - 1, limit - tallies[sink]) // 2
    slack = jnp.where((giver == order[0]) | (sink == order[0]) | (tallies[sink] == 0), 0, jnp.maximum(slack, 0))
    shifted = jax.random.randint(jax.random.fold_in(own, 4), (count // 2,), 0, 1 << 20) % (slack + 1)
    tallies = tallies.at[giver].add(-shifted).at[sink].add(shifted)
    members = jnp.searchsorted(jnp.cumsum(tallies), jnp.arange(rows * top), side="right").astype(jnp.int32)
    listing = members.reshape(top, rows).T
    listing = listing[jax.random.permutation(jax.random.fold_in(own, 1), rows)]
    rotation = jax.random.randint(jax.random.fold_in(own, 2), (rows, 1), 0, top)
    return jnp.take_along_axis(listing, (jnp.arange(top)[None, :] + rotation) % top, axis=1)


def shares(number_of, total, most, slope, full):
    weights = [(1 << 20) // math.isqrt(rank ** slope) + 1 for rank in range(1, number_of + 1)]
    largest = most if full else min(most, max(-(-total // number_of), total * weights[0] // sum(weights)))
    least = 1 if total - largest >= number_of - 1 else 0
    given, spare = [largest] + [least] * (number_of - 1), total - largest - least * (number_of - 1)
    while spare > 0:
        free = [i for i in range(1, number_of) if given[i] < largest] or [i for i in range(1, number_of) if given[i] < most]
        mass, budget = sum([weights[i] for i in free]), spare
        for i in free:
            more = min(most - given[i], max(1, budget * weights[i] // mass), spare)
            given[i] = given[i] + more
            spare = spare - more
    return np.array(given)


def noise(key, dims, spread, bound, pieces=(), kind=jnp.bfloat16):
    gain = block_scale(key, dims, pieces, -0.22, 0.18) if pieces else 1.0
    values = jax.random.normal(key, dims, jnp.float32) * spread * gain
    return jnp.minimum(jnp.maximum(values, -bound), bound).astype(kind)


def setup_inputs(seed: int = 0) -> dict:
    arg_keys = jax.random.split(jax.random.key(seed), 19)
    hidden_in = noise(arg_keys[0], (TOKENS, D), 1.0, 6.0, ((0, 4), (1, 8)))
    token_order = jax.vmap(lambda own: jax.random.permutation(own, T_R))(jax.random.split(arg_keys[1], GROUPS)).reshape((GROUPS, T_R)).astype(jnp.int32)
    lengths = jax.vmap(lambda own: ragged(own, SEQS, T_R, LMAX, 2))(jax.random.split(arg_keys[2], GROUPS)).reshape((GROUPS, SEQS)).astype(jnp.int32)
    key_mask = place_ends((jax.random.randint(arg_keys[3], (TOKENS,), 0, 8) < 7).astype(jnp.int32), jax.random.fold_in(arg_keys[3], 1), 0, 1)
    routes_keys = jax.random.split(jax.random.fold_in(arg_keys[4], 1), TOKENS // T_R)
    routes_turns = jax.random.permutation(jax.random.fold_in(arg_keys[4], 3), TOKENS // T_R)
    routes = jax.vmap(lambda own, number: assign_block(jax.random.fold_in(arg_keys[4], 2), own, number, T_R, E, TOP, CAP, 2))(routes_keys, routes_turns).reshape((TOKENS, TOP))
    norm1_gain = jnp.clip(1.0 + 0.1 * jax.random.normal(arg_keys[5], (D,), jnp.float32), 0.5, 1.5)
    query_gain = jnp.clip(jnp.exp(jax.random.uniform(arg_keys[6], (DH,), jnp.float32, math.log(1.1), math.log(2.2))), 1.1, 2.2)
    key_gain = jnp.clip(jnp.exp(jax.random.uniform(arg_keys[7], (DH,), jnp.float32, math.log(1.1), math.log(2.2))), 1.1, 2.2)
    w_query = noise(arg_keys[8], (D, H * DH), D ** -0.5, 0.125, ((0, 4), (1, 8)))
    w_key = noise(arg_keys[9], (D, H * DH), D ** -0.5, 0.125, ((0, 4), (1, 8)))
    w_value = noise(arg_keys[10], (D, H * DH), D ** -0.5, 0.125, ((0, 4), (1, 8)))
    w_out = noise(arg_keys[11], (D, H * DH), (D // 64) ** -0.5, 1.0, ((0, 4), (1, 8)))
    norm2_gain = jnp.clip(1.0 + 0.1 * jax.random.normal(arg_keys[12], (D,), jnp.float32), 0.5, 1.5)
    router = noise(arg_keys[13], (E, D), (4 * D) ** -0.5, 0.0625, ((1, 4),))
    w_gate = noise(arg_keys[14], (E, D, FF), D ** -0.5, 0.125, ((0, 8), (1, 4)))
    w_up = noise(arg_keys[15], (E, D, FF), D ** -0.5, 0.125, ((0, 8), (1, 4)))
    w_down = noise(arg_keys[16], (E, D, FF), (FF // 8) ** -0.5, 0.5, ((0, 8), (1, 4)))
    cotangent = noise(arg_keys[17], (TOKENS, D), 1.0, 6.0, ((0, 4), (1, 8)))
    return dict(hidden_in=hidden_in, token_order=token_order, lengths=lengths, key_mask=key_mask, routes=routes, norm1_gain=norm1_gain, query_gain=query_gain, key_gain=key_gain, w_query=w_query, w_key=w_key, w_value=w_value, w_out=w_out, norm2_gain=norm2_gain, router=router, w_gate=w_gate, w_up=w_up, w_down=w_down, cotangent=cotangent)


EPSILON = 1e-06
ROPE_BASE = 10000.0
HIGHEST = lax.Precision.HIGHEST

@jax.custom_vjp
def low(v):
    return lax.optimization_barrier(v.astype(jnp.bfloat16)).astype(jnp.float32)

@jax.custom_vjp
def low_back(v):
    return v

def low_keep(v):
    return (low(v), None)

def low_pass(kept, grad):
    return (grad,)

def back_keep(v):
    return (v, None)

def back_low(kept, grad):
    return (low(grad),)
low.defvjp(low_keep, low_pass)
low_back.defvjp(back_keep, back_low)

def matmul(left_op, right_op):
    return jnp.dot(left_op, right_op, precision=HIGHEST, preferred_element_type=jnp.float32)

def layout(seq_lengths, tok_count):
    seq_ends = jnp.cumsum(seq_lengths).astype(jnp.int32)
    seq_starts = (seq_ends - seq_lengths).astype(jnp.int32)
    places = jnp.arange(tok_count, dtype=jnp.int32)
    segment = lax.optimization_barrier(jnp.sum((places[:, None] >= seq_ends[None, :]).astype(jnp.int32), axis=1)).astype(jnp.int32)
    member = segment[:, None] == jnp.arange(seq_lengths.shape[0], dtype=jnp.int32)[None, :]
    offset = lax.optimization_barrier(jnp.sum(jnp.where(member, seq_starts[None, :], 0), axis=1)).astype(jnp.int32)
    return (segment, (places - offset).astype(jnp.int32))

def rotate(values, position):
    half_dim = values.shape[-1] // 2
    frequency = ROPE_BASE ** (-2.0 * jnp.arange(half_dim, dtype=jnp.float32) / values.shape[-1])
    angles = position.astype(jnp.float32)[:, None] * frequency[None, :]
    cosine = jnp.cos(angles)[:, None, :]
    sine_part = jnp.sin(angles)[:, None, :]
    first_half = values[..., :half_dim]
    second_half = values[..., half_dim:]
    return jnp.concatenate([first_half * cosine - second_half * sine_part, second_half * cosine + first_half * sine_part], axis=-1)

def head_norm(values, gain_vec):
    return values * lax.rsqrt(lax.optimization_barrier(jnp.mean(values * values, axis=-1, keepdims=True)) + EPSILON) * gain_vec

def slot_table(route_rows, experts, first_id, capacity):
    tok_count, top_count = route_rows.shape
    flat_routes = route_rows.reshape(-1)
    expert_ids = first_id + jnp.arange(experts, dtype=jnp.int32)
    hit_table = (flat_routes[:, None] == expert_ids[None, :]).astype(jnp.int32)
    rank_table = (jnp.cumsum(hit_table, axis=0) - 1).astype(jnp.int32)
    slot_place = lax.optimization_barrier(jnp.sum(rank_table * hit_table, axis=1)).astype(jnp.int32)
    local_id = flat_routes - first_id
    inside = (local_id >= 0) & (local_id < experts)
    target = jnp.where(inside, local_id, experts).astype(jnp.int32)
    entries = jnp.arange(tok_count * top_count, dtype=jnp.int32)
    slot_ids = jnp.full((experts, capacity), tok_count * top_count, jnp.int32)
    slot_ids = slot_ids.at[target, slot_place].set(entries, mode='drop')
    return (slot_ids // top_count, slot_ids % top_count)

def attend(queries, key_rot, values, segment, mask_row):
    tok_count, head_count, head_dim = queries.shape
    block_rows = 512 if tok_count % 512 == 0 else tok_count
    places = jnp.arange(tok_count, dtype=jnp.int32)
    score_scale = head_dim ** (-0.5)

    def one_block(block_start):
        query_rows = lax.dynamic_slice_in_dim(queries, block_start, block_rows, 0)
        rows_here = block_start + jnp.arange(block_rows, dtype=jnp.int32)
        segment_here = lax.dynamic_slice_in_dim(segment, block_start, block_rows, 0)
        allowed = (segment_here[:, None] == segment[None, :]) & ((mask_row[None, :] == 1) | (rows_here[:, None] == places[None, :]))
        scores = low_back(jnp.einsum('qhd,khd->hqk', query_rows, key_rot, precision=HIGHEST) * score_scale)
        scores = jnp.where(allowed[None], scores, -1e+30)
        weights = low(jax.nn.softmax(scores, axis=-1))
        return jnp.einsum('hqk,khd->qhd', weights, values, precision=HIGHEST)
    starts = jnp.arange(tok_count // block_rows, dtype=jnp.int32) * block_rows
    return lax.map(jax.checkpoint(one_block), starts).reshape(tok_count, head_count * head_dim)

def block_forward(packed, params, segment, position, mask_row, route_rows, slot_token, slot_pick):
    norm1_gain, query_gain, key_gain, w_query, w_key, w_value, w_out, norm2_gain, router, w_gate, w_up, w_down = params
    tok_count = packed.shape[0]
    scale_in = lax.rsqrt(lax.optimization_barrier(jnp.mean(packed * packed, axis=-1, keepdims=True)) + EPSILON)
    normed1 = low(packed * scale_in * norm1_gain)
    queries = low_back(matmul(normed1, w_query)).reshape(tok_count, -1, DH)
    keys_raw = low_back(matmul(normed1, w_key)).reshape(tok_count, -1, DH)
    values = low(low_back(matmul(normed1, w_value))).reshape(tok_count, -1, DH)
    query_rot = low(rotate(head_norm(queries, query_gain), position))
    key_rot = low(rotate(head_norm(keys_raw, key_gain), position))
    attended = low(low_back(attend(query_rot, key_rot, values, segment, mask_row)))
    branch = low_back(jnp.dot(attended, w_out.T, precision=HIGHEST, preferred_element_type=jnp.float32))
    mixed = packed + branch
    scale_mid = lax.rsqrt(lax.optimization_barrier(jnp.mean(mixed * mixed, axis=-1, keepdims=True)) + EPSILON)
    normed2 = low(mixed * scale_mid * norm2_gain)
    logits = low_back(jnp.dot(normed2, router.T, precision=HIGHEST, preferred_element_type=jnp.float32))
    chosen = jnp.take_along_axis(logits, route_rows, axis=1)
    gate_probs = jax.nn.softmax(chosen, axis=-1)
    padded = jnp.concatenate([normed2, jnp.zeros((1, D), jnp.float32)], axis=0)
    slot_rows = padded[slot_token]
    gate_pad = jnp.concatenate([gate_probs, jnp.zeros((1, TOP), jnp.float32)], axis=0)
    slot_gate = gate_pad[slot_token, slot_pick]
    gate_pre = low_back(jnp.einsum('ecd,edf->ecf', slot_rows, w_gate, precision=HIGHEST))
    up_pre = low_back(jnp.einsum('ecd,edf->ecf', slot_rows, w_up, precision=HIGHEST))
    activation = low(jax.nn.silu(gate_pre) * up_pre)
    expert_out = low_back(jnp.einsum('ecf,edf->ecd', activation, w_down, precision=HIGHEST))
    combined = jnp.zeros((tok_count + 1, D), jnp.float32).at[slot_token].add(slot_gate[..., None] * expert_out)[:tok_count]
    return mixed + low_back(combined)

def reference(hidden_in, token_order, lengths, key_mask, routes, norm1_gain, query_gain, key_gain, w_query, w_key, w_value, w_out, norm2_gain, router, w_gate, w_up, w_down, cotangent):
    params = tuple((param.astype(jnp.float32) for param in (norm1_gain, query_gain, key_gain, w_query, w_key, w_value, w_out, norm2_gain, router, w_gate, w_up, w_down)))
    hidden_groups = hidden_in.astype(jnp.float32).reshape(N_ROW, T_R, D)
    cot_groups = cotangent.astype(jnp.float32).reshape(N_ROW, T_R, D)
    mask_groups = key_mask.reshape(N_ROW, T_R)
    route_groups = routes.reshape(N_ROW, T_R, TOP)

    def one_group(totals, inputs):
        hidden_grp, cot_grp, order_grp, length_grp, mask_grp, route_grp = inputs
        inverse = jnp.zeros((T_R,), jnp.int32).at[order_grp].set(jnp.arange(T_R, dtype=jnp.int32))
        segment, position = layout(length_grp, T_R)
        slot_token, slot_pick = slot_table(route_grp, E, 0, CAP)

        def forward(packed, *weights_all):
            return block_forward(packed, weights_all, segment, position, mask_grp, route_grp, slot_token, slot_pick)
        result, pull = jax.vjp(forward, hidden_grp[order_grp], *params)
        gradients = pull(cot_grp[order_grp])
        totals = tuple((running + update for running, update in zip(totals, gradients[1:])))
        return (totals, (result[inverse], gradients[0][inverse]))
    zeros_init = tuple((jnp.zeros(param.shape, jnp.float32) for param in params))
    totals, (results, grad_rows) = lax.scan(one_group, zeros_init, (hidden_groups, cot_groups, token_order, lengths, mask_groups, route_groups))
    return (results.reshape(TOKENS, D).astype(jnp.bfloat16), grad_rows.reshape(TOKENS, D), totals[0], totals[1], totals[2], totals[3], totals[4], totals[5], totals[6], totals[7], totals[8], totals[9], totals[10], totals[11])
```

```python
import jax
import jax.numpy as jnp
from jax import lax
from jax.sharding import PartitionSpec as P

D = 2048
DH = 128
E = 64
TOP = 8


EPSILON = 1e-06
ROPE_BASE = 10000.0
BF16 = jnp.bfloat16
F32 = jnp.float32


def layout(seq_lengths, tok_count):
    seq_ends = jnp.cumsum(seq_lengths)
    seq_starts = seq_ends - seq_lengths
    places = jnp.arange(tok_count, dtype=jnp.int32)
    segment = jnp.sum((places[:, None] >= seq_ends[None, :]).astype(jnp.int32), axis=1)
    member = segment[:, None] == jnp.arange(seq_lengths.shape[0], dtype=jnp.int32)[None, :]
    offset = jnp.sum(jnp.where(member, seq_starts[None, :], 0), axis=1)
    return (segment, places - offset)


def rotate(values, position):
    half_dim = values.shape[-1] // 2
    frequency = ROPE_BASE ** (-2.0 * jnp.arange(half_dim, dtype=jnp.float32) / values.shape[-1])
    angles = position.astype(jnp.float32)[:, None] * frequency[None, :]
    cosine = jnp.cos(angles)[:, None, :]
    sine_part = jnp.sin(angles)[:, None, :]
    first_half = values[..., :half_dim]
    second_half = values[..., half_dim:]
    return jnp.concatenate(
        [
            first_half * cosine - second_half * sine_part,
            second_half * cosine + first_half * sine_part,
        ],
        axis=-1,
    )


def head_norm(values, gain_vec):
    return (
        values * lax.rsqrt(jnp.mean(values * values, axis=-1, keepdims=True) + EPSILON) * gain_vec
    )


def gather_features(local_rows):
    return lax.all_gather(local_rows, "col", axis=1, tiled=True)


def scatter_partial(partial_rows):
    return lax.psum_scatter(partial_rows, "col", scatter_dimension=1, tiled=True)


def swap_rows(pieces):
    return lax.all_to_all(pieces, "row", 0, 0, tiled=True)


def contract_last(left_op, right_op, kind=F32):
    return lax.dot_general(
        left_op, right_op, (((1,), (1,)), ((), ())), preferred_element_type=F32
    ).astype(kind)


def contract_first(left_op, right_op, kind=F32):
    return lax.dot_general(
        left_op, right_op, (((0,), (0,)), ((), ())), preferred_element_type=F32
    ).astype(kind)


def plain_dot(left_op, right_op, kind=F32):
    return jnp.dot(left_op, right_op, preferred_element_type=F32).astype(kind)


def after(value, *earlier):
    return lax.optimization_barrier((value, *earlier))[0]


def body(
    hidden_in,
    token_order,
    lengths,
    key_mask,
    routes,
    norm1_gain,
    query_gain,
    key_gain,
    w_query,
    w_key,
    w_value,
    w_out,
    norm2_gain,
    router,
    w_gate,
    w_up,
    w_down,
    cotangent,
):
    tok_count, feat_local = hidden_in.shape
    n_row = D // w_query.shape[0]
    local_experts, _, hidden_units = w_gate.shape
    per_device = max(1, local_experts // n_row)
    unit_split = max(1, n_row // local_experts)
    capacity = 5 * tok_count * TOP // (4 * E)
    col = lax.axis_index("col")
    core = lax.axis_index("row") % 2
    places = jnp.arange(tok_count, dtype=jnp.int32)
    order_row = token_order[0]
    inverse = jnp.zeros((tok_count,), jnp.int32).at[order_row].set(places)
    segment, position = layout(lengths[0], tok_count)

    packed_b = hidden_in[order_row]
    packed_all_b = gather_features(packed_b)
    cot_b = cotangent[order_row]

    width_local = w_query.shape[1]
    head_count = width_local // DH
    weight_rows = jnp.concatenate([w_query, w_key, w_value, w_out], axis=1)
    weight_heads = swap_rows(
        jnp.broadcast_to(weight_rows[None], (n_row,) + weight_rows.shape)
    ).reshape(D, 4 * width_local)
    w_qkv = weight_heads[:, : 3 * width_local]
    w_out_own = weight_heads[:, 3 * width_local :]

    def to_owner(weight, e):
        if unit_split == 1:
            pieces = weight.reshape(n_row, per_device, *weight.shape[1:])[:, e]
        else:
            pieces = weight.reshape(local_experts, -1, unit_split, hidden_units // unit_split)
            pieces = pieces.transpose(0, 2, 1, 3).reshape(
                n_row, -1, hidden_units // unit_split
            )
        return swap_rows(pieces).reshape(D, hidden_units // unit_split)

    experts = [
        tuple(to_owner(weight, e) for weight in (w_gate, w_up, w_down)) for e in range(per_device)
    ]

    gains = lax.all_gather(jnp.stack([norm1_gain, norm2_gain]), "col", axis=1, tiled=True)
    router_all = lax.all_gather(router, "row", axis=1, tiled=True)

    expert_ids = jnp.arange(E, dtype=jnp.int32)
    routes_t = routes.T
    chosen = jnp.any(routes_t[None] == expert_ids[:, None, None], axis=1)
    own_ids = col * local_experts + jnp.arange(local_experts, dtype=jnp.int32)
    own_chosen = jnp.any(routes_t[None] == own_ids[:, None, None], axis=1)
    earlier = (places[:, None] < places[None, :]).astype(BF16)
    rank = plain_dot(own_chosen.astype(BF16), earlier).astype(jnp.int32)
    slot_rank = jnp.where(own_chosen, rank, -1)
    slots = jnp.arange(capacity, dtype=jnp.int32)

    def slot_matrix(e):
        if unit_split == 1:
            mine = slot_rank.reshape(n_row, per_device, tok_count)[:, e]
        else:
            mine = jnp.repeat(slot_rank, unit_split, axis=0)
        hits = mine[:, None, :] == slots[None, :, None]
        return hits

    hits = [slot_matrix(e) for e in range(per_device)]
    picks = [h.astype(BF16).reshape(n_row * capacity, tok_count) for h in hits]

    packed_all = packed_all_b.astype(F32)
    scale_in = lax.rsqrt(jnp.mean(packed_all * packed_all, axis=1, keepdims=True) + EPSILON)
    normed1 = (packed_all * scale_in * gains[0]).astype(BF16)
    qkv = plain_dot(normed1, w_qkv)
    queries, keys_raw, values_raw = (
        qkv[:, i * width_local : (i + 1) * width_local].reshape(tok_count, head_count, DH)
        for i in range(3)
    )
    values_b = values_raw.astype(BF16)

    def post_heads(raw_rows, gain_vec):
        return rotate(head_norm(raw_rows, gain_vec), position)

    query_post, query_pull = jax.vjp(post_heads, queries, query_gain)
    key_post, key_pull = jax.vjp(post_heads, keys_raw, key_gain)
    query_rot = query_post.astype(BF16)
    key_rot = key_post.astype(BF16)
    score_scale = DH ** (-0.5)
    block_rows = 512
    starts = jnp.arange(tok_count // block_rows, dtype=jnp.int32) * block_rows

    def allowed_at(block_start):
        rows_here = block_start + jnp.arange(block_rows, dtype=jnp.int32)
        segment_here = lax.dynamic_slice_in_dim(segment, block_start, block_rows, 0)
        return (segment_here[:, None] == segment[None, :]) & (
            (key_mask[None, :] == 1) | (rows_here[:, None] == places[None, :])
        )

    def scores_at(block_start):
        query_rows = lax.dynamic_slice_in_dim(query_rot, block_start, block_rows, 0)
        scores = (
            jnp.einsum("qhd,khd->hqk", query_rows, key_rot, preferred_element_type=F32)
            * score_scale
        )
        return (query_rows, jnp.where(allowed_at(block_start)[None], scores, -1e30))

    def forward_block(block_start):
        query_rows, scores = scores_at(block_start)
        row_max = jnp.max(scores, axis=-1, keepdims=True)
        exp_terms = jnp.exp(scores - row_max)
        row_total = jnp.sum(exp_terms, axis=-1, keepdims=True)
        weights = (exp_terms / row_total).astype(BF16)
        attended = jnp.einsum("hqk,khd->qhd", weights, values_b, preferred_element_type=F32)
        return (attended, (row_max + jnp.log(row_total))[..., 0])

    attended_blocks, log_totals = lax.map(forward_block, starts)
    attended_b = attended_blocks.reshape(tok_count, width_local).astype(BF16)

    half = D // 2
    out_half = lax.dynamic_slice_in_dim(w_out_own, core * half, half, 0)
    out_half_all = gather_features(after(out_half, packed_all_b))
    other_half = lax.ppermute(out_half_all, "row", [(r, r ^ 1) for r in range(n_row)])
    first_core = core == 0
    w_out_all = jnp.concatenate(
        [
            jnp.where(first_core, out_half_all, other_half),
            jnp.where(first_core, other_half, out_half_all),
        ],
        axis=0,
    )
    attended_all = gather_features(after(attended_b, out_half_all))
    cot_all = gather_features(after(cot_b, attended_all))
    mixed_all = packed_all + contract_last(attended_all, w_out_all)
    scale_mid = lax.rsqrt(jnp.mean(mixed_all * mixed_all, axis=1, keepdims=True) + EPSILON)
    normed2 = (mixed_all * scale_mid * gains[1]).astype(BF16)
    column_start = col * feat_local
    mixed = lax.dynamic_slice_in_dim(mixed_all, column_start, feat_local, 1)

    logits = contract_last(router_all, normed2)
    top_logit = jnp.max(jnp.where(chosen, logits, -jnp.inf), axis=0, keepdims=True)
    raised = jnp.where(chosen, jnp.exp(logits - top_logit), 0.0)
    gate_probs = raised / jnp.sum(raised, axis=0, keepdims=True)
    own_probs = lax.dynamic_slice_in_dim(gate_probs, col * local_experts, local_experts, 0)

    def of_rows(table, e):
        if unit_split == 1:
            return table.reshape(n_row, per_device, *table.shape[1:])[:, e]
        return jnp.repeat(table, unit_split, axis=0)

    branch_back, grads_back, scalars_back, weight_grads = [], [], [], []
    for e in range(per_device):
        w_gate_e, w_up_e, w_down_e = experts[e]
        rows = swap_rows(plain_dot(picks[e], normed2, BF16).reshape(n_row, capacity, D))
        rows = rows.reshape(n_row * capacity, D)
        slot_gate = jnp.sum(jnp.where(hits[e], of_rows(own_probs, e)[:, None, :], 0.0), axis=2)
        slot_gate = swap_rows(slot_gate).reshape(n_row * capacity, 1)
        grad_rows = swap_rows(plain_dot(picks[e], cot_all, BF16).reshape(n_row, capacity, D))
        grad_rows = grad_rows.reshape(n_row * capacity, D)
        gate_pre = plain_dot(rows, w_gate_e)
        up_pre = plain_dot(rows, w_up_e)
        sigmoid_gate = jax.nn.sigmoid(gate_pre)
        silu_gate = gate_pre * sigmoid_gate
        activation = silu_gate * up_pre
        scaled_activation = (slot_gate * activation).astype(BF16)
        grad_unscaled = plain_dot(grad_rows, w_down_e)
        grad_gate = jnp.sum(activation * grad_unscaled, axis=1)
        grad_activation = slot_gate * grad_unscaled
        grad_gate_pre = (
            grad_activation * up_pre * sigmoid_gate * (1.0 + gate_pre * (1.0 - sigmoid_gate))
        ).astype(BF16)
        grad_up_pre = (grad_activation * silu_gate).astype(BF16)
        inner = jnp.sum(
            grad_gate_pre.astype(F32) * gate_pre + grad_up_pre.astype(F32) * up_pre, axis=1
        )
        scalars = jnp.stack([grad_gate, inner]).reshape(2, n_row, capacity).transpose(1, 0, 2)
        scalars_back.append(swap_rows(scalars))
        grad_slot_rows = (
            contract_last(grad_gate_pre, w_gate_e) + contract_last(grad_up_pre, w_up_e)
        ).astype(BF16)
        grads_back.append(swap_rows(grad_slot_rows.reshape(n_row, capacity, D)))
        expert_out = contract_last(scaled_activation, w_down_e, BF16)
        branch_back.append(swap_rows(expert_out.reshape(n_row, capacity, D)))
        weight_grads.append(
            (
                contract_first(rows, grad_gate_pre, BF16),
                contract_first(rows, grad_up_pre, BF16),
                contract_first(grad_rows, scaled_activation, BF16),
            )
        )

    def to_tokens(back):
        total = 0.0
        for e in range(per_device):
            total = total + contract_first(picks[e], back[e].reshape(n_row * capacity, D))
        return total.astype(BF16)

    grad_normed2 = scatter_partial(to_tokens(grads_back)).astype(F32)

    def of_experts(e, which):
        spread = jnp.where(hits[e], scalars_back[e][:, which, :, None], 0.0)
        return jnp.sum(spread, axis=1)

    def over_experts(which):
        table = jnp.stack([of_experts(e, which) for e in range(per_device)], axis=1)
        if unit_split == 1:
            return table.reshape(local_experts, tok_count)
        return jnp.sum(table.reshape(local_experts, unit_split, tok_count), axis=1)

    small = jnp.concatenate([over_experts(0), jnp.sum(over_experts(1), axis=0)[None]], axis=0)
    small = lax.all_gather(small, "col", axis=0)
    grad_gates = small[:, :local_experts].reshape(E, tok_count)
    grad_logits = gate_probs * (
        grad_gates - jnp.sum(gate_probs * grad_gates, axis=0, keepdims=True)
    )
    grad_logits = grad_logits.astype(BF16)
    inner_mid = jnp.sum(small[:, local_experts], axis=0) + jnp.sum(
        grad_logits.astype(F32) * logits, axis=0
    )
    inner_mid = (inner_mid / D)[:, None]
    grad_router = plain_dot(grad_logits, normed2)
    router_local = lax.dynamic_slice_in_dim(router_all, column_start, feat_local, 1)
    grad_unit_mid = grad_normed2 + contract_first(grad_logits, router_local)
    unit_mid = mixed * scale_mid
    grad_norm2 = jnp.sum(grad_unit_mid * unit_mid, axis=0)
    scaled_mid = grad_unit_mid * norm2_gain
    grad_mixed = cot_b.astype(F32) + scale_mid * (scaled_mid - unit_mid * inner_mid)
    grad_branch = gather_features(grad_mixed.astype(BF16))

    combined = scatter_partial(after(to_tokens(branch_back), grad_branch))
    output = (mixed + combined.astype(F32)).astype(BF16)[inverse]

    grad_w_out = contract_first(grad_branch, attended_b, BF16)
    grad_attended = plain_dot(grad_branch, w_out_own, BF16).reshape(tok_count, head_count, DH)

    def backward_block(carried, inputs):
        grad_keys, grad_values = carried
        block_start, log_total = inputs
        query_rows, scores = scores_at(block_start)
        prob_rows = jnp.exp(scores - log_total[..., None])
        grad_out_rows = lax.dynamic_slice_in_dim(grad_attended, block_start, block_rows, 0)
        grad_values = grad_values + jnp.einsum(
            "hqk,qhd->khd", prob_rows.astype(BF16), grad_out_rows, preferred_element_type=F32
        )
        grad_probs = jnp.einsum(
            "qhd,khd->hqk", grad_out_rows, values_b, preferred_element_type=F32
        )
        grad_scores = (
            prob_rows * (grad_probs - jnp.sum(prob_rows * grad_probs, axis=-1, keepdims=True))
        ).astype(BF16)
        grad_query_rows = (
            jnp.einsum("hqk,khd->qhd", grad_scores, key_rot, preferred_element_type=F32)
            * score_scale
        )
        grad_keys = (
            grad_keys
            + jnp.einsum("hqk,qhd->khd", grad_scores, query_rows, preferred_element_type=F32)
            * score_scale
        )
        return ((grad_keys, grad_values), grad_query_rows)

    zero_heads = jnp.zeros((tok_count, head_count, DH), F32)
    (grad_key_rot, grad_values), grad_query_rot = lax.scan(
        backward_block, (zero_heads, zero_heads), (starts, log_totals)
    )
    grad_queries, grad_query_gain = query_pull(grad_query_rot.reshape(tok_count, head_count, DH))
    grad_keys_raw, grad_key_gain = key_pull(grad_key_rot)
    grad_qkv = jnp.concatenate(
        [
            grad.reshape(tok_count, width_local).astype(BF16)
            for grad in (grad_queries, grad_keys_raw, grad_values)
        ],
        axis=1,
    )
    grad_normed1_part = contract_last(grad_qkv, w_qkv, BF16)
    grad_unit_in = scatter_partial(grad_normed1_part).astype(F32)
    inner_in = lax.psum(jnp.sum(grad_qkv.astype(F32) * qkv, axis=1), "col")[:, None] / D
    packed = packed_b.astype(F32)
    unit_in = packed * scale_in
    grad_norm1 = jnp.sum(grad_normed1_part.astype(F32) * (packed_all * scale_in), axis=0)
    scaled_in = grad_unit_in * norm1_gain
    grad_input = (grad_mixed + scale_in * (scaled_in - unit_in * inner_in))[inverse]

    grad_heads = jnp.concatenate(
        [contract_first(normed1, grad_qkv, BF16), grad_w_out], axis=1
    ).reshape(n_row, D // n_row, 4 * width_local)
    grad_heads = jnp.sum(swap_rows(grad_heads).astype(F32), axis=0)
    grad_w_query, grad_w_key, grad_w_value, grad_w_out = (
        grad_heads[:, i * width_local : (i + 1) * width_local] for i in range(4)
    )
    grad_router = grad_router.reshape(E, n_row, D // n_row).transpose(1, 0, 2)
    grad_router = jnp.sum(swap_rows(grad_router), axis=0)

    def to_rows(which):
        parts = []
        for e in range(per_device):
            grad = weight_grads[e][which].reshape(n_row, D // n_row, hidden_units // unit_split)
            parts.append(swap_rows(grad).astype(F32))
        if unit_split == 1:
            return jnp.stack(parts, axis=1).reshape(local_experts, D // n_row, hidden_units)
        grad = parts[0].reshape(local_experts, unit_split, D // n_row, -1)
        return grad.transpose(0, 2, 1, 3).reshape(local_experts, D // n_row, hidden_units)

    grad_w_gate, grad_w_up, grad_w_down = (to_rows(which) for which in range(3))

    vectors = jnp.concatenate(
        [
            grad_norm1,
            lax.dynamic_update_slice_in_dim(jnp.zeros((D,), F32), grad_norm2, column_start, 0),
            grad_query_gain,
            grad_key_gain,
        ]
    )
    vectors = lax.psum(vectors, ("row", "col"))
    grad_norm1 = lax.dynamic_slice_in_dim(vectors, column_start, feat_local, 0)
    grad_norm2 = lax.dynamic_slice_in_dim(vectors, D + column_start, feat_local, 0)
    grad_query_gain = vectors[2 * D : 2 * D + DH]
    grad_key_gain = vectors[2 * D + DH :]
    return (
        output,
        grad_input,
        grad_norm1,
        grad_query_gain,
        grad_key_gain,
        grad_w_query,
        grad_w_key,
        grad_w_value,
        grad_w_out,
        grad_norm2,
        grad_router,
        grad_w_gate,
        grad_w_up,
        grad_w_down,
    )


def solution(mesh):
    return jax.shard_map(
        body,
        mesh=mesh,
        in_specs=(
            P("row", "col"),
            P("row", None),
            P("row", None),
            P("row"),
            P("row", None),
            P("col"),
            P(),
            P(),
            P("row", "col"),
            P("row", "col"),
            P("row", "col"),
            P("row", "col"),
            P("col"),
            P(None, "row"),
            P("col", "row", None),
            P("col", "row", None),
            P("col", "row", None),
            P("row", "col"),
        ),
        out_specs=(
            P("row", "col"),
            P("row", "col"),
            P("col"),
            P(),
            P(),
            P("row", "col"),
            P("row", "col"),
            P("row", "col"),
            P("row", "col"),
            P("col"),
            P(None, "row"),
            P("col", "row", None),
            P("col", "row", None),
            P("col", "row", None),
        ),
        check_vma=False,
    )
```

```python
import jax
import jax.numpy as jnp
from jax import lax
from jax.experimental import pallas as pl
from jax.experimental.pallas import tpu as pltpu
from jax.sharding import PartitionSpec as P

D = 2048
DH = 128
E = 64
TOP = 8


EPSILON = 1e-06
ROPE_BASE = 10000.0
BF16 = jnp.bfloat16
F32 = jnp.float32


def layout(seq_lengths, tok_count):
    seq_ends = jnp.cumsum(seq_lengths)
    seq_starts = seq_ends - seq_lengths
    places = jnp.arange(tok_count, dtype=jnp.int32)
    segment = jnp.sum((places[:, None] >= seq_ends[None, :]).astype(jnp.int32), axis=1)
    member = segment[:, None] == jnp.arange(seq_lengths.shape[0], dtype=jnp.int32)[None, :]
    offset = jnp.sum(jnp.where(member, seq_starts[None, :], 0), axis=1)
    return (segment, places - offset)


def rope_tables(position):
    half_dim = DH // 2
    frequency = ROPE_BASE ** (-2.0 * jnp.arange(half_dim, dtype=F32) / DH)
    angles = position.astype(F32)[:, None] * frequency[None, :]
    cosine, sine = jnp.cos(angles), jnp.sin(angles)
    return jnp.concatenate([cosine, cosine], 1), jnp.concatenate([-sine, sine], 1)


def gather_features(local_rows):
    return lax.all_gather(local_rows, "col", axis=1, tiled=True)


def scatter_partial(partial_rows):
    return lax.psum_scatter(partial_rows, "col", scatter_dimension=1, tiled=True)


def trade(value, step, n_row):
    if step == 0:
        return value
    return lax.ppermute(value, "row", [(r, r ^ step) for r in range(n_row)])


def trade_all(pieces):
    return [trade(piece, step, len(pieces)) for step, piece in enumerate(pieces)]


def contract_last(left_op, right_op, kind=F32):
    return lax.dot_general(
        left_op, right_op, (((1,), (1,)), ((), ())), preferred_element_type=F32
    ).astype(kind)


def contract_first(left_op, right_op, kind=F32):
    return lax.dot_general(
        left_op, right_op, (((0,), (0,)), ((), ())), preferred_element_type=F32
    ).astype(kind)


def plain_dot(left_op, right_op, kind=F32):
    return jnp.dot(left_op, right_op, preferred_element_type=F32).astype(kind)


def after(value, *earlier):
    return lax.optimization_barrier((value, *earlier))[0]


def thirds(values):
    high = lax.reduce_precision(values, 8, 7)
    middle = lax.reduce_precision(values - high, 8, 7)
    return jnp.stack([high, middle, values - high - middle]).astype(BF16)


def cost(flops, moved):
    return pl.CostEstimate(flops=flops, bytes_accessed=moved, transcendentals=0)


def rope(values, cosine, sine):
    return values * cosine + pltpu.roll(values, DH // 2, 1) * sine


def rope_back(grad, cosine, sine):
    return grad * cosine + pltpu.roll(grad * sine, DH // 2, 1)


def project_kernel(x_ref, gain_ref, w_ref, qg_ref, kg_ref, cos_ref, sin_ref, *outs):
    normed_ref, scale_ref, raw_ref, q_ref, k_ref, v_ref = outs
    x = x_ref[...].astype(F32)
    scale = lax.rsqrt(jnp.mean(x * x, axis=1, keepdims=True) + EPSILON)
    normed = (x * scale * gain_ref[...]).astype(BF16)
    normed_ref[...] = normed
    scale_ref[...] = scale
    width = q_ref.shape[1]
    qkv = jnp.dot(normed, w_ref[:, : 3 * width], preferred_element_type=F32)
    raw_ref[...] = qkv[:, : 2 * width]
    v_ref[...] = qkv[:, 2 * width :].astype(BF16)
    cosine, sine = cos_ref[...], sin_ref[...]
    for part, gain, out in ((0, qg_ref, q_ref), (1, kg_ref, k_ref)):
        for h in range(width // DH):
            head = qkv[:, part * width + h * DH : part * width + (h + 1) * DH]
            size = lax.rsqrt(jnp.mean(head * head, axis=1, keepdims=True) + EPSILON)
            out[:, h * DH : (h + 1) * DH] = rope(head * size * gain[...], cosine, sine).astype(BF16)


def project(x, gain, w, q_gain, k_gain, cosine, sine, width, block=256):
    rows = cosine.shape[0]
    by_rows = lambda n: pl.BlockSpec((block, n), lambda i: (i, 0))
    whole = lambda a: pl.BlockSpec(a.shape, lambda i: (0, 0))
    return pl.pallas_call(
        project_kernel,
        name="project",
        grid=(rows // block,),
        in_specs=[
            by_rows(D),
            whole(gain),
            whole(w),
            whole(q_gain),
            whole(k_gain),
            by_rows(DH),
            by_rows(DH),
        ],
        out_specs=[by_rows(n) for n in (D, 1, 2 * width, width, width, width)],
        out_shape=[
            jax.ShapeDtypeStruct((rows, D), BF16),
            jax.ShapeDtypeStruct((rows, 1), F32),
            jax.ShapeDtypeStruct((rows, 2 * width), F32),
            jax.ShapeDtypeStruct((rows, width), BF16),
            jax.ShapeDtypeStruct((rows, width), BF16),
            jax.ShapeDtypeStruct((rows, width), BF16),
        ],
        cost_estimate=cost(1000, 1000),
    )(x, gain, w, q_gain, k_gain, cosine, sine)


def masked_scores(q, k, seg_q, seg_k, first):
    scores = lax.dot_general(q, k, (((1,), (1,)), ((), ())), preferred_element_type=F32)
    rows = first + lax.broadcasted_iota(jnp.int32, scores.shape, 0)
    columns = lax.broadcasted_iota(jnp.int32, scores.shape, 1)
    allowed = (seg_q == seg_k) | (rows == columns)
    return jnp.where(allowed, scores * DH ** (-0.5), -1e30)


def attend_kernel(q_ref, k_ref, v_ref, seg_q_ref, seg_k_ref, out_ref, log_ref):
    first = pl.program_id(1) * q_ref.shape[0]
    scores = masked_scores(q_ref[...], k_ref[...], seg_q_ref[...], seg_k_ref[...], first)
    top = jnp.max(scores, axis=1, keepdims=True)
    terms = jnp.exp(scores - top)
    total = jnp.sum(terms, axis=1, keepdims=True)
    weights = (terms * (1.0 / total)).astype(BF16)
    out_ref[...] = jnp.dot(weights, v_ref[...], preferred_element_type=F32).astype(BF16)
    log_ref[0] = top + jnp.log(total)


def attend(q, k, v, seg_q, seg_k, block=256):
    rows, width = q.shape
    heads = width // DH
    by_rows = pl.BlockSpec((block, DH), lambda h, i: (i, h))
    whole = pl.BlockSpec((rows, DH), lambda h, i: (0, h))
    return pl.pallas_call(
        attend_kernel,
        name="attend",
        grid=(heads, rows // block),
        in_specs=[
            by_rows,
            whole,
            whole,
            pl.BlockSpec((block, 1), lambda h, i: (i, 0)),
            pl.BlockSpec((1, rows), lambda h, i: (0, 0)),
        ],
        out_specs=[by_rows, pl.BlockSpec((1, block, 1), lambda h, i: (h, i, 0))],
        out_shape=[
            jax.ShapeDtypeStruct((rows, width), BF16),
            jax.ShapeDtypeStruct((heads, rows, 1), F32),
        ],
        cost_estimate=cost(1000, 1000),
    )(q, k, v, seg_q, seg_k)


def head_back(grad, raw, gain, cosine, sine):
    grad = rope_back(grad, cosine, sine)
    size = lax.rsqrt(jnp.mean(raw * raw, axis=1, keepdims=True) + EPSILON)
    unit = raw * size
    grad_gain = jnp.sum(grad * unit, axis=0, keepdims=True)
    grad = grad * gain
    return size * (grad - unit * jnp.mean(grad * unit, axis=1, keepdims=True)), grad_gain


def attend_back_kernel(
    q_ref, k_ref, v_ref, grad_ref, log_ref, seg_q_ref, seg_k_ref, raw_q_ref, raw_k_ref,
    qg_ref, kg_ref, cos_q_ref, sin_q_ref, cos_ref, sin_ref,
    dq_ref, dk_ref, dv_ref, dqg_ref, dkg_ref, sum_k, sum_v,
):
    head, i = pl.program_id(0), pl.program_id(1)

    @pl.when((head == 0) & (i == 0))
    def _():
        dqg_ref[...] = jnp.zeros_like(dqg_ref)
        dkg_ref[...] = jnp.zeros_like(dkg_ref)

    @pl.when(i == 0)
    def _():
        sum_k[...] = jnp.zeros_like(sum_k)
        sum_v[...] = jnp.zeros_like(sum_v)

    q, k, grad = q_ref[...], k_ref[...], grad_ref[...]
    scores = masked_scores(q, k, seg_q_ref[...], seg_k_ref[...], i * q.shape[0])
    probs = jnp.exp(scores - log_ref[0])
    sum_v[...] += lax.dot_general(
        probs.astype(BF16), grad, (((0,), (0,)), ((), ())), preferred_element_type=F32
    )
    grad_probs = lax.dot_general(
        grad, v_ref[...], (((1,), (1,)), ((), ())), preferred_element_type=F32
    )
    inner = jnp.sum(probs * grad_probs, axis=1, keepdims=True)
    grad_scores = (probs * (grad_probs - inner)).astype(BF16)
    sum_k[...] += lax.dot_general(
        grad_scores, q, (((0,), (0,)), ((), ())), preferred_element_type=F32
    )
    grad_q = jnp.dot(grad_scores, k, preferred_element_type=F32) * DH ** (-0.5)
    grad_q, grad_gain = head_back(
        grad_q, raw_q_ref[...], qg_ref[...], cos_q_ref[...], sin_q_ref[...]
    )
    dq_ref[...] = grad_q.astype(BF16)
    dqg_ref[...] += grad_gain

    @pl.when(i == pl.num_programs(1) - 1)
    def _():
        grad_k, gain_k = head_back(
            sum_k[...] * DH ** (-0.5), raw_k_ref[...], kg_ref[...], cos_ref[...], sin_ref[...]
        )
        dk_ref[...] = grad_k.astype(BF16)
        dkg_ref[...] += gain_k
        dv_ref[...] = sum_v[...].astype(BF16)


def attend_back(q, k, v, grad, logs, seg_q, seg_k, raw, q_gain, k_gain, cosine, sine, block=256):
    rows, width = q.shape
    heads = width // DH
    by_rows = pl.BlockSpec((block, DH), lambda h, i: (i, h))
    whole = pl.BlockSpec((rows, DH), lambda h, i: (0, h))
    gain = pl.BlockSpec((1, DH), lambda h, i: (0, 0))
    return pl.pallas_call(
        attend_back_kernel,
        name="attend_back",
        grid=(heads, rows // block),
        in_specs=[
            by_rows,
            whole,
            whole,
            by_rows,
            pl.BlockSpec((1, block, 1), lambda h, i: (h, i, 0)),
            pl.BlockSpec((block, 1), lambda h, i: (i, 0)),
            pl.BlockSpec((1, rows), lambda h, i: (0, 0)),
            by_rows,
            pl.BlockSpec((rows, DH), lambda h, i: (0, heads + h)),
            gain,
            gain,
            pl.BlockSpec((block, DH), lambda h, i: (i, 0)),
            pl.BlockSpec((block, DH), lambda h, i: (i, 0)),
            pl.BlockSpec((rows, DH), lambda h, i: (0, 0)),
            pl.BlockSpec((rows, DH), lambda h, i: (0, 0)),
        ],
        out_specs=[by_rows, whole, whole, gain, gain],
        out_shape=[
            jax.ShapeDtypeStruct((rows, width), BF16),
            jax.ShapeDtypeStruct((rows, width), BF16),
            jax.ShapeDtypeStruct((rows, width), BF16),
            jax.ShapeDtypeStruct((1, DH), F32),
            jax.ShapeDtypeStruct((1, DH), F32),
        ],
        scratch_shapes=[pltpu.VMEM((rows, DH), F32), pltpu.VMEM((rows, DH), F32)],
        cost_estimate=cost(1000, 1000),
    )(q, k, v, grad, logs, seg_q, seg_k, raw, raw, q_gain, k_gain, cosine, sine, cosine, sine)


def branch_kernel(
    at_ref, x_ref, att_ref, own_ref, other_ref, gain_ref, normed_ref, scale_ref, mixed_ref, total
):
    half = own_ref.shape[0]
    own = contract_last(att_ref[...], own_ref[...])
    other = contract_last(att_ref[...], other_ref[...])
    second = at_ref[0] == 1
    total[:, :half] = x_ref[:, :half].astype(F32) + jnp.where(second, other, own)
    total[:, half:] = x_ref[:, half:].astype(F32) + jnp.where(second, own, other)
    mixed = total[...]
    scale = lax.rsqrt(jnp.mean(mixed * mixed, axis=1, keepdims=True) + EPSILON)
    normed_ref[...] = (mixed * scale * gain_ref[...]).astype(BF16)
    scale_ref[...] = scale
    width = mixed_ref.shape[1]
    mixed_ref[...] = total[:, pl.ds(pl.multiple_of(at_ref[1] * width, 128), width)]


def run_branch(core, col, x, attended, own, other, gain, width, block=256):
    rows = attended.shape[0]
    by_rows = lambda n: pl.BlockSpec((block, n), lambda i, at: (i, 0))
    whole = lambda a: pl.BlockSpec(a.shape, lambda i, at: (0, 0))
    return pl.pallas_call(
        branch_kernel,
        name="branch",
        grid_spec=pltpu.PrefetchScalarGridSpec(
            num_scalar_prefetch=1,
            grid=(rows // block,),
            in_specs=[by_rows(D), by_rows(D), whole(own), whole(other), whole(gain)],
            out_specs=[by_rows(D), by_rows(1), by_rows(width)],
            scratch_shapes=[pltpu.VMEM((block, D), F32)],
        ),
        out_shape=[
            jax.ShapeDtypeStruct((rows, D), BF16),
            jax.ShapeDtypeStruct((rows, 1), F32),
            jax.ShapeDtypeStruct((rows, width), F32),
        ],
        cost_estimate=cost(1000, 1000),
    )(jnp.stack([core, col]), x, attended, own, other, gain)


def expert_kernel(x_ref, c_ref, gate_ref, w_ref, wd_ref, act_ref, grad_ref, sums_ref, dx_ref):
    width = act_ref.shape[1]
    slot_gate = gate_ref[...]
    pre = jnp.dot(x_ref[...], w_ref[...], preferred_element_type=F32)
    gate, up = pre[:, :width], pre[:, width:]
    grad = jnp.dot(c_ref[...], wd_ref[...], preferred_element_type=F32)
    opened = 1.0 / (1.0 + jnp.exp(-gate))
    silu = gate * opened
    act = silu * up
    act_ref[...] = (slot_gate * act).astype(BF16)
    grad_gate = jnp.sum(act * grad, axis=1, keepdims=True)
    grad = slot_gate * grad
    dgate = (grad * up * opened * (1.0 + gate * (1.0 - opened))).astype(BF16)
    dup = (grad * silu).astype(BF16)
    grad_ref[:, :width] = dgate
    grad_ref[:, width:] = dup
    inner = jnp.sum(dgate.astype(F32) * gate + dup.astype(F32) * up, axis=1, keepdims=True)
    sums_ref[:, 0:1] = grad_gate
    sums_ref[:, 1:2] = inner
    dx_ref[...] = contract_last(grad_ref[...], w_ref[...], BF16)


def run_expert(x, c, slot_gate, w, wd, block):
    rows, width = x.shape[0], wd.shape[1]
    by_rows = lambda n: pl.BlockSpec((block, n), lambda i: (i, 0))
    whole = lambda a: pl.BlockSpec(a.shape, lambda i: (0, 0), pipeline_mode=pl.Buffered(1))
    return pl.pallas_call(
        expert_kernel,
        name="expert",
        grid=(rows // block,),
        in_specs=[by_rows(D), by_rows(D), by_rows(1), whole(w), whole(wd)],
        out_specs=[by_rows(width), by_rows(2 * width), by_rows(2), by_rows(D)],
        out_shape=[
            jax.ShapeDtypeStruct((rows, width), BF16),
            jax.ShapeDtypeStruct((rows, 2 * width), BF16),
            jax.ShapeDtypeStruct((rows, 2), F32),
            jax.ShapeDtypeStruct((rows, D), BF16),
        ],
        cost_estimate=cost(1000, 1000),
    )(x, c, slot_gate, w, wd)


def body(
    hidden_in,
    token_order,
    lengths,
    key_mask,
    routes,
    norm1_gain,
    query_gain,
    key_gain,
    w_query,
    w_key,
    w_value,
    w_out,
    norm2_gain,
    router,
    w_gate,
    w_up,
    w_down,
    cotangent,
):
    tok_count, feat_local = hidden_in.shape
    n_row = D // w_query.shape[0]
    n_col = D // feat_local
    local_experts, _, hidden_units = w_gate.shape
    per_device = max(1, local_experts // n_row)
    unit_split = max(1, n_row // local_experts)
    capacity = 5 * tok_count * TOP // (4 * E)
    col = lax.axis_index("col")
    row = lax.axis_index("row")
    core = row % 2
    steps = range(n_row)
    peers = [row ^ step for step in steps]
    rows_local = D // n_row
    unit_count = hidden_units // unit_split
    places = jnp.arange(tok_count, dtype=jnp.int32)
    order_row = token_order[0]
    inverse = jnp.zeros((tok_count,), jnp.int32).at[order_row].set(places)
    segment, position = layout(lengths[0], tok_count)

    packed_b = hidden_in[order_row]
    gains_b = jnp.concatenate([thirds(norm1_gain), thirds(norm2_gain)])
    gathered = gather_features(jnp.concatenate([packed_b, jnp.pad(gains_b, ((0, 10), (0, 0)))]))
    cot_b = cotangent[order_row]

    width_local = w_query.shape[1]
    head_count = width_local // DH
    weight_rows = jnp.concatenate([w_query, w_key, w_value, w_out, router.T], axis=1)
    weight_pieces = {step: trade(weight_rows, step, n_row) for step in steps if step % 2 == 0}
    for step in steps:
        if step % 2 == 1:
            weight_pieces[step] = trade(weight_pieces[step ^ 1], 1, n_row)
    weight_heads = jnp.zeros((D, weight_rows.shape[1]), BF16)
    for step in steps:
        weight_heads = lax.dynamic_update_slice(
            weight_heads, weight_pieces[step], (peers[step] * rows_local, 0)
        )
    w_qkv = weight_heads[:, : 3 * width_local]
    w_out_own = weight_heads[:, 3 * width_local : 4 * width_local]
    router_all = weight_heads[:, 4 * width_local :]

    def owned_at(peer):
        return (peer * per_device // unit_split, 0, (peer % unit_split) * unit_count)

    all_weights = (w_gate, w_up, w_down)
    all_parts = [(which, e) for which in range(3) for e in range(per_device)]
    owned = {}
    w_in = [jnp.zeros((D, 2 * unit_count), BF16) for e in range(per_device)]
    w_back = [jnp.zeros((D, unit_count), BF16) for e in range(per_device)]

    def slices(parts):
        pieces = []
        for step in steps if parts else ():
            first, _, unit = owned_at(peers[step])
            held = [
                lax.dynamic_slice(
                    all_weights[which], (first + e, 0, unit), (1, rows_local, unit_count)
                )
                for which, e in parts
            ]
            pieces.append(jnp.concatenate(held))
        return pieces

    def to_owner(parts, pieces, *earlier):
        pieces = trade_all(after(pieces, *earlier))
        for i, (which, e) in enumerate(parts):
            for step in steps:
                at = (peers[step] * rows_local, unit_count if which == 1 else 0)
                if which < 2:
                    w_in[e] = lax.dynamic_update_slice(w_in[e], pieces[step][i], at)
                else:
                    w_back[e] = lax.dynamic_update_slice(w_back[e], pieces[step][i], at)

    def tied(value):
        value, w_in[:], w_back[:] = lax.optimization_barrier((value, w_in[:], w_back[:]))
        return value

    first_parts, second_parts = all_parts[:per_device], all_parts[per_device : per_device + 1]
    third_parts = all_parts[per_device + 1 : 2 * per_device + 1]
    last_parts = all_parts[2 * per_device + 1 :]
    to_owner(first_parts, slices(first_parts))
    second_pieces = after(slices(second_parts), *w_in)
    later = [slices(parts) for parts in (third_parts, last_parts)]
    gathered, second_pieces, later = tied((gathered, second_pieces, later))
    gains = gathered[tok_count : tok_count + 6].astype(F32).reshape(2, 3, D).sum(axis=1)

    expert_ids = jnp.arange(E, dtype=jnp.int32)
    routes_t = routes.T
    chosen = jnp.any(routes_t[None] == expert_ids[:, None, None], axis=1)
    own_ids = col * local_experts + jnp.arange(local_experts, dtype=jnp.int32)
    own_chosen = jnp.any(routes_t[None] == own_ids[:, None, None], axis=1)
    earlier = (places[:, None] < places[None, :]).astype(BF16)
    rank = plain_dot(own_chosen.astype(BF16), earlier).astype(jnp.int32)
    slot_rank = jnp.where(own_chosen, rank, -1)
    slots = jnp.arange(capacity, dtype=jnp.int32)

    def of_peer(table, step, e):
        return lax.dynamic_slice_in_dim(table, owned_at(peers[step])[0] + e, 1, 0)

    hits = [
        [of_peer(slot_rank, step, e) == slots[:, None] for step in steps]
        for e in range(per_device)
    ]
    picks = [[hit.astype(BF16) for hit in hits[e]] for e in range(per_device)]

    def swap_small(pieces):
        table = jnp.zeros((n_row,) + pieces[0].shape, pieces[0].dtype)
        for step in steps:
            table = jnp.where(
                jnp.arange(n_row).reshape((-1,) + (1,) * pieces[0].ndim) == peers[step],
                pieces[step][None],
                table,
            )
        table = lax.all_to_all(table, "row", 0, 0, tiled=True)
        return [lax.dynamic_index_in_dim(table, peers[step], 0, False) for step in steps]

    cosine, sine = rope_tables(position)
    q_gain, k_gain = query_gain[None], key_gain[None]
    normed1, scale_in, raw_qk, query_rot, key_rot, values_b = project(
        gathered, gains[:1], weight_heads, q_gain, k_gain, cosine, sine, width_local
    )
    seg_q, seg_k = segment[:, None], jnp.where(key_mask == 1, segment, -1)[None]
    attended_b, log_totals = attend(query_rot, key_rot, values_b, seg_q, seg_k)

    half = D // 2
    out_half = lax.dynamic_slice_in_dim(w_out_own, core * half, half, 0)
    out_half_all = gather_features(after(out_half, *w_in))

    to_owner(second_parts, second_pieces)
    attended_b = tied(attended_b)
    attended_all = gather_features(attended_b)
    to_owner(third_parts, later[0], attended_b)
    other_half = trade(after(out_half_all, *w_back), 1, n_row)
    cot_all = gather_features(after(cot_b, attended_all))
    attended_all = tied(attended_all)
    if last_parts:
        to_owner(last_parts, later[1], w_back[0])
    normed2, scale_mid, mixed = run_branch(
        core, col, gathered, attended_all, out_half_all, other_half, gains[1:], feat_local
    )
    column_start = col * feat_local

    def chosen_rows(e, values):
        return [plain_dot(picks[e][step], values, BF16) for step in steps]

    sent_rows = [chosen_rows(e, normed2) for e in range(per_device)]
    sent_rows[0] = tied(sent_rows[0])
    all_rows = [trade_all(pieces) for pieces in sent_rows]
    sent_grads = [chosen_rows(e, cot_all) for e in range(per_device)]
    all_rows, sent_grads = lax.optimization_barrier((all_rows, sent_grads))
    all_grad_rows = [trade_all(pieces) for pieces in sent_grads]

    logits = lax.dot_general(
        router_all, normed2, (((0,), (1,)), ((), ())), preferred_element_type=F32
    )
    top_logit = jnp.max(jnp.where(chosen, logits, -jnp.inf), axis=0, keepdims=True)
    raised = jnp.where(chosen, jnp.exp(logits - top_logit), 0.0)
    gate_probs = raised / jnp.sum(raised, axis=0, keepdims=True)
    own_probs = lax.dynamic_slice_in_dim(gate_probs, col * local_experts, local_experts, 0)

    slot_gates = []
    for step in steps:
        held = [
            jnp.sum(jnp.where(hits[e][step], of_peer(own_probs, step, e), 0.0), axis=1)
            for e in range(per_device)
        ]
        slot_gates.append(jnp.stack(held))
    slot_gates = swap_small(slot_gates)

    near, far = list(steps)[:2], list(steps)[2:]
    branch_back, grads_back, scalars, weight_grads = [], [], [], []
    for e in range(per_device):
        rows, grad_rows, act, grad_pre, sums, grad_slot_rows = [], [], [], [], [], []
        for held in (near, far):
            rows.append(jnp.concatenate([all_rows[e][step] for step in held]))
            grad_rows.append(jnp.concatenate([all_grad_rows[e][step] for step in held]))
            slot_gate = jnp.concatenate([slot_gates[step][e] for step in held])[:, None]
            results = run_expert(
                rows[-1], grad_rows[-1], slot_gate, w_in[e], w_back[e], 2 * capacity
            )
            for total, result in zip((act, grad_pre, sums), results):
                total.append(result)
            grad_slot_rows += [
                results[3][i * capacity : (i + 1) * capacity] for i in range(len(held))
            ]
        rows, grad_rows, act, grad_pre, sums = (
            jnp.concatenate(parts) for parts in (rows, grad_rows, act, grad_pre, sums)
        )
        scalars.append(sums)
        grads_back.append(trade_all(grad_slot_rows))
        branch_back.append(contract_last(act, w_back[e], BF16))
        grad_in = contract_first(rows, grad_pre, BF16)
        weight_grads.append(
            (
                grad_in[:, :unit_count],
                grad_in[:, unit_count:],
                contract_first(grad_rows, act, BF16),
            )
        )
    scalars = jnp.stack(scalars)
    scalars_back = swap_small(
        [scalars[:, step * capacity : (step + 1) * capacity] for step in steps]
    )
    branch_back = jnp.stack(branch_back)
    out_pieces = [branch_back[:, step * capacity : (step + 1) * capacity] for step in steps]

    def to_tokens(back, which):
        return contract_first(
            jnp.concatenate([picks[e][step] for e, step in which]),
            jnp.concatenate([back[e][step] for e, step in which]),
        )

    every = [(e, step) for e in range(per_device) for step in steps]
    late = [(per_device - 1, step) for step in far]
    early = [pair for pair in every if pair not in late]
    grad_normed2_part = to_tokens(grads_back, early)
    grads_back, out_pieces, grad_normed2_part = lax.optimization_barrier(
        (grads_back, out_pieces, grad_normed2_part)
    )
    grad_normed2_part = (grad_normed2_part + to_tokens(grads_back, late)).astype(BF16)
    branch_back = trade_all(out_pieces)
    branch_back = [[piece[e] for piece in branch_back] for e in range(per_device)]
    grad_normed2 = scatter_partial(grad_normed2_part).astype(F32)

    grad_own = jnp.zeros((local_experts, tok_count), F32)
    inner_own = jnp.zeros((1, tok_count), F32)
    own_rows = jnp.arange(local_experts, dtype=jnp.int32)[:, None]
    for e in range(per_device):
        for step in steps:
            expert = owned_at(peers[step])[0] + e
            back = scalars_back[step][e]
            spread = jnp.sum(jnp.where(hits[e][step], back[:, :1], 0.0), axis=0, keepdims=True)
            grad_own = grad_own + jnp.where(own_rows == expert, spread, 0.0)
            inner_own = inner_own + jnp.sum(
                jnp.where(hits[e][step], back[:, 1:], 0.0), axis=0, keepdims=True
            )
    small = jnp.concatenate([grad_own, inner_own], axis=0)
    small = lax.all_to_all(
        jnp.broadcast_to(small[None], (n_col,) + small.shape), "col", 0, 0, tiled=True
    )
    grad_gates = small[:, :local_experts].reshape(E, tok_count)
    grad_logits = gate_probs * (
        grad_gates - jnp.sum(gate_probs * grad_gates, axis=0, keepdims=True)
    )
    grad_logits = grad_logits.astype(BF16)
    inner_mid = jnp.sum(small[:, local_experts], axis=0) + jnp.sum(
        grad_logits.astype(F32) * logits, axis=0
    )
    inner_mid = (inner_mid / D)[:, None]
    grad_router = lax.dot_general(
        normed2, grad_logits, (((0,), (1,)), ((), ())), preferred_element_type=F32
    )
    router_local = lax.dynamic_slice_in_dim(router_all, column_start, feat_local, 0)
    grad_unit_mid = grad_normed2 + lax.dot_general(
        grad_logits, router_local, (((0,), (1,)), ((), ())), preferred_element_type=F32
    )
    unit_mid = mixed * scale_mid
    grad_norm2 = jnp.sum(grad_unit_mid * unit_mid, axis=0)
    scaled_mid = grad_unit_mid * norm2_gain
    grad_mixed = cot_b.astype(F32) + scale_mid * (scaled_mid - unit_mid * inner_mid)
    def held_slices(which):
        return [
            jnp.stack(
                [
                    lax.dynamic_slice_in_dim(
                        weight_grads[e][which], peers[step] * rows_local, rows_local, 0
                    )
                    for e in range(per_device)
                ]
            )
            for step in steps
        ]

    gate_slices, up_slices = held_slices(0), held_slices(1)
    grad_mixed_b, branch_back, gate_slices, up_slices = lax.optimization_barrier(
        (grad_mixed.astype(BF16), branch_back, gate_slices, up_slices)
    )
    grad_branch = gather_features(grad_mixed_b)

    def to_holders(pieces, *earlier):
        return trade_all(after(pieces, *earlier))

    def to_rows(pieces):
        grad = jnp.zeros((local_experts, rows_local, hidden_units), F32)
        for step in steps:
            grad = lax.dynamic_update_slice(grad, pieces[step].astype(F32), owned_at(peers[step]))
        return grad

    def sum_groups(grad, *earlier):
        parts = [
            lax.dynamic_slice_in_dim(grad, peers[step] * rows_local, rows_local, 0)
            for step in steps
        ]
        return sum(part.astype(F32) for part in to_holders(parts, *earlier))

    gate_pieces = to_holders(gate_slices)
    combined_part = to_tokens(branch_back, every).astype(BF16)
    grad_branch, gate_pieces, combined_part = lax.optimization_barrier(
        (grad_branch, gate_pieces, combined_part)
    )
    up_pieces = to_holders(up_slices, gate_pieces)

    combined = scatter_partial(combined_part)

    grad_w_out = contract_first(grad_branch, attended_b, BF16)
    grad_attended = plain_dot(grad_branch, w_out_own, BF16)
    grad_q, grad_k, grad_v, grad_query_gain, grad_key_gain = attend_back(
        query_rot, key_rot, values_b, grad_attended, log_totals, seg_q, seg_k, raw_qk,
        q_gain, k_gain, cosine, sine,
    )
    grad_qkv = jnp.concatenate([grad_q, grad_k, grad_v], axis=1)
    grad_w_out = sum_groups(grad_w_out, up_pieces)
    grad_router = sum_groups(grad_router, up_pieces).T
    down_pieces = held_slices(2)
    grad_qkv, up_pieces, combined, down_pieces, grad_w_out, grad_router = (
        lax.optimization_barrier(
            (grad_qkv, up_pieces, combined, down_pieces, grad_w_out, grad_router)
        )
    )
    grad_normed1_part = contract_last(grad_qkv, w_qkv, BF16)
    grad_unit_in = scatter_partial(grad_normed1_part)
    inner_in = jnp.sum(
        grad_qkv.astype(F32) * jnp.concatenate([raw_qk, values_b.astype(F32)], axis=1), axis=1
    )
    packed = packed_b.astype(F32)
    unit_in = packed * scale_in
    unit_all = gathered[:tok_count].astype(F32) * scale_in
    grad_norm1 = jnp.sum(grad_normed1_part.astype(F32) * unit_all, axis=0)
    down_pieces = to_holders(down_pieces, grad_normed1_part)
    def for_all(vector):
        return jnp.broadcast_to(vector[None], (n_col,) + vector.shape)

    vectors = jnp.concatenate(
        [
            for_all(inner_in),
            for_all(grad_query_gain[0]),
            for_all(grad_key_gain[0]),
            grad_norm1.reshape(n_col, feat_local),
        ],
        axis=1,
    )
    vectors = jnp.sum(lax.all_to_all(vectors, "col", 0, 0, tiled=True), axis=0)
    inner_in = vectors[:tok_count, None] / D
    vectors = jnp.concatenate([vectors[tok_count:], grad_norm2])
    vectors = sum(trade(vectors, step, n_row) for step in steps)
    grad_unit_in, vectors, inner_in = lax.optimization_barrier(
        (grad_unit_in, vectors, inner_in)
    )
    grad_unit_in = grad_unit_in.astype(F32)
    scaled_in = grad_unit_in * norm1_gain
    grad_input = (grad_mixed + scale_in * (scaled_in - unit_in * inner_in))[inverse]

    output = (mixed + combined.astype(F32)).astype(BF16)[inverse]

    grad_heads = sum_groups(contract_first(normed1, grad_qkv, BF16), down_pieces)
    grad_w_query, grad_w_key, grad_w_value = (
        grad_heads[:, i * width_local : (i + 1) * width_local] for i in range(3)
    )
    grad_w_gate, grad_w_up, grad_w_down = (
        to_rows(pieces) for pieces in (gate_pieces, up_pieces, down_pieces)
    )

    grad_query_gain, grad_key_gain = vectors[:DH], vectors[DH : 2 * DH]
    grad_norm1 = vectors[2 * DH : 2 * DH + feat_local]
    grad_norm2 = vectors[2 * DH + feat_local :]
    return (
        output,
        grad_input,
        grad_norm1,
        grad_query_gain,
        grad_key_gain,
        grad_w_query,
        grad_w_key,
        grad_w_value,
        grad_w_out,
        grad_norm2,
        grad_router,
        grad_w_gate,
        grad_w_up,
        grad_w_down,
    )


def solution(mesh):
    return jax.shard_map(
        body,
        mesh=mesh,
        in_specs=(
            P("row", "col"),
            P("row", None),
            P("row", None),
            P("row"),
            P("row", None),
            P("col"),
            P(),
            P(),
            P("row", "col"),
            P("row", "col"),
            P("row", "col"),
            P("row", "col"),
            P("col"),
            P(None, "row"),
            P("col", "row", None),
            P("col", "row", None),
            P("col", "row", None),
            P("row", "col"),
        ),
        out_specs=(
            P("row", "col"),
            P("row", "col"),
            P("col"),
            P(),
            P(),
            P("row", "col"),
            P("row", "col"),
            P("row", "col"),
            P("row", "col"),
            P("col"),
            P(None, "row"),
            P("col", "row", None),
            P("col", "row", None),
            P("col", "row", None),
        ),
        check_vma=False,
    )
```

```python
import jax
import jax.numpy as jnp
from jax import lax
from jax.experimental import pallas as pl
from jax.experimental.pallas import tpu as pltpu
from jax.sharding import PartitionSpec as P

D = 2048
DH = 128
E = 64
TOP = 8


EPSILON = 1e-06
ROPE_BASE = 10000.0
BF16 = jnp.bfloat16
F32 = jnp.float32


def layout(seq_lengths, tok_count):
    seq_ends = jnp.cumsum(seq_lengths)
    seq_starts = seq_ends - seq_lengths
    places = jnp.arange(tok_count, dtype=jnp.int32)
    segment = jnp.sum((places[:, None] >= seq_ends[None, :]).astype(jnp.int32), axis=1)
    member = segment[:, None] == jnp.arange(seq_lengths.shape[0], dtype=jnp.int32)[None, :]
    offset = jnp.sum(jnp.where(member, seq_starts[None, :], 0), axis=1)
    return (segment, places - offset)


def rope_tables(position):
    half_dim = DH // 2
    frequency = ROPE_BASE ** (-2.0 * jnp.arange(half_dim, dtype=F32) / DH)
    angles = position.astype(F32)[:, None] * frequency[None, :]
    cosine, sine = jnp.cos(angles), jnp.sin(angles)
    return jnp.concatenate([cosine, cosine], 1), jnp.concatenate([-sine, sine], 1)


def gather_features(local_rows):
    return lax.all_gather(local_rows, "col", axis=1, tiled=True)


def scatter_partial(partial_rows):
    return lax.psum_scatter(partial_rows, "col", scatter_dimension=1, tiled=True)


def trade(value, step, n_row):
    if step == 0:
        return value
    return lax.ppermute(value, "row", [(r, r ^ step) for r in range(n_row)])


def trade_all(pieces):
    return [trade(piece, step, len(pieces)) for step, piece in enumerate(pieces)]


def contract_last(left_op, right_op, kind=F32):
    return lax.dot_general(
        left_op, right_op, (((1,), (1,)), ((), ())), preferred_element_type=F32
    ).astype(kind)


def contract_first(left_op, right_op, kind=F32):
    return lax.dot_general(
        left_op, right_op, (((0,), (0,)), ((), ())), preferred_element_type=F32
    ).astype(kind)


def plain_dot(left_op, right_op, kind=F32):
    return jnp.dot(left_op, right_op, preferred_element_type=F32).astype(kind)


def after(value, *earlier):
    return lax.optimization_barrier((value, *earlier))[0]


def thirds(values):
    high = lax.reduce_precision(values, 8, 7)
    middle = lax.reduce_precision(values - high, 8, 7)
    return jnp.stack([high, middle, values - high - middle]).astype(BF16)


def cost(flops, moved):
    return pl.CostEstimate(flops=flops, bytes_accessed=moved, transcendentals=0)


def rope(values, cosine, sine):
    return values * cosine + pltpu.roll(values, DH // 2, 1) * sine


def rope_back(grad, cosine, sine):
    return grad * cosine + pltpu.roll(grad * sine, DH // 2, 1)


def project_kernel(x_ref, gain_ref, w_ref, qg_ref, kg_ref, cos_ref, sin_ref, *outs):
    normed_ref, scale_ref, raw_ref, q_ref, k_ref, v_ref = outs
    x = x_ref[...].astype(F32)
    scale = lax.rsqrt(jnp.mean(x * x, axis=1, keepdims=True) + EPSILON)
    normed = (x * scale * gain_ref[...]).astype(BF16)
    normed_ref[...] = normed
    scale_ref[...] = scale
    width = q_ref.shape[1]
    qkv = jnp.dot(normed, w_ref[:, : 3 * width], preferred_element_type=F32)
    raw_ref[...] = qkv[:, : 2 * width]
    v_ref[...] = qkv[:, 2 * width :].astype(BF16)
    cosine, sine = cos_ref[...], sin_ref[...]
    for part, gain, out in ((0, qg_ref, q_ref), (1, kg_ref, k_ref)):
        for h in range(width // DH):
            head = qkv[:, part * width + h * DH : part * width + (h + 1) * DH]
            size = lax.rsqrt(jnp.mean(head * head, axis=1, keepdims=True) + EPSILON)
            out[:, h * DH : (h + 1) * DH] = rope(head * size * gain[...], cosine, sine).astype(BF16)


def project(x, gain, w, q_gain, k_gain, cosine, sine, width, block=256):
    rows = cosine.shape[0]
    by_rows = lambda n: pl.BlockSpec((block, n), lambda i: (i, 0))
    whole = lambda a: pl.BlockSpec(a.shape, lambda i: (0, 0))
    return pl.pallas_call(
        project_kernel,
        name="project",
        grid=(rows // block,),
        in_specs=[
            by_rows(D),
            whole(gain),
            whole(w),
            whole(q_gain),
            whole(k_gain),
            by_rows(DH),
            by_rows(DH),
        ],
        out_specs=[by_rows(n) for n in (D, 1, 2 * width, width, width, width)],
        out_shape=[
            jax.ShapeDtypeStruct((rows, D), BF16),
            jax.ShapeDtypeStruct((rows, 1), F32),
            jax.ShapeDtypeStruct((rows, 2 * width), F32),
            jax.ShapeDtypeStruct((rows, width), BF16),
            jax.ShapeDtypeStruct((rows, width), BF16),
            jax.ShapeDtypeStruct((rows, width), BF16),
        ],
        cost_estimate=cost(1000, 1000),
    )(x, gain, w, q_gain, k_gain, cosine, sine)


def masked_scores(q, k, seg_q, seg_k, first):
    scores = lax.dot_general(q, k, (((1,), (1,)), ((), ())), preferred_element_type=F32)
    rows = first + lax.broadcasted_iota(jnp.int32, scores.shape, 0)
    columns = lax.broadcasted_iota(jnp.int32, scores.shape, 1)
    allowed = (seg_q == seg_k) | (rows == columns)
    return jnp.where(allowed, scores * DH ** (-0.5), -1e30)


def attend_kernel(q_ref, k_ref, v_ref, seg_q_ref, seg_k_ref, out_ref, log_ref):
    first = pl.program_id(1) * q_ref.shape[0]
    scores = masked_scores(q_ref[...], k_ref[...], seg_q_ref[...], seg_k_ref[...], first)
    top = jnp.max(scores, axis=1, keepdims=True)
    terms = jnp.exp(scores - top)
    total = jnp.sum(terms, axis=1, keepdims=True)
    weights = (terms * (1.0 / total)).astype(BF16)
    out_ref[...] = jnp.dot(weights, v_ref[...], preferred_element_type=F32).astype(BF16)
    log_ref[0] = top + jnp.log(total)


def attend(q, k, v, seg_q, seg_k, block=256):
    rows, width = q.shape
    heads = width // DH
    by_rows = pl.BlockSpec((block, DH), lambda h, i: (i, h))
    whole = pl.BlockSpec((rows, DH), lambda h, i: (0, h))
    return pl.pallas_call(
        attend_kernel,
        name="attend",
        grid=(heads, rows // block),
        in_specs=[
            by_rows,
            whole,
            whole,
            pl.BlockSpec((block, 1), lambda h, i: (i, 0)),
            pl.BlockSpec((1, rows), lambda h, i: (0, 0)),
        ],
        out_specs=[by_rows, pl.BlockSpec((1, block, 1), lambda h, i: (h, i, 0))],
        out_shape=[
            jax.ShapeDtypeStruct((rows, width), BF16),
            jax.ShapeDtypeStruct((heads, rows, 1), F32),
        ],
        cost_estimate=cost(1000, 1000),
    )(q, k, v, seg_q, seg_k)


def head_back(grad, raw, gain, cosine, sine):
    grad = rope_back(grad, cosine, sine)
    size = lax.rsqrt(jnp.mean(raw * raw, axis=1, keepdims=True) + EPSILON)
    unit = raw * size
    grad_gain = jnp.sum(grad * unit, axis=0, keepdims=True)
    grad = grad * gain
    return size * (grad - unit * jnp.mean(grad * unit, axis=1, keepdims=True)), grad_gain


def attend_back_kernel(
    q_ref, k_ref, v_ref, grad_ref, log_ref, seg_q_ref, seg_k_ref, raw_q_ref, raw_k_ref,
    qg_ref, kg_ref, cos_q_ref, sin_q_ref, cos_ref, sin_ref,
    dq_ref, dk_ref, dv_ref, dqg_ref, dkg_ref, sum_k, sum_v,
):
    head, i = pl.program_id(0), pl.program_id(1)

    @pl.when((head == 0) & (i == 0))
    def _():
        dqg_ref[...] = jnp.zeros_like(dqg_ref)
        dkg_ref[...] = jnp.zeros_like(dkg_ref)

    @pl.when(i == 0)
    def _():
        sum_k[...] = jnp.zeros_like(sum_k)
        sum_v[...] = jnp.zeros_like(sum_v)

    q, k, grad = q_ref[...], k_ref[...], grad_ref[...]
    scores = masked_scores(q, k, seg_q_ref[...], seg_k_ref[...], i * q.shape[0])
    probs = jnp.exp(scores - log_ref[0])
    sum_v[...] += lax.dot_general(
        probs.astype(BF16), grad, (((0,), (0,)), ((), ())), preferred_element_type=F32
    )
    grad_probs = lax.dot_general(
        grad, v_ref[...], (((1,), (1,)), ((), ())), preferred_element_type=F32
    )
    inner = jnp.sum(probs * grad_probs, axis=1, keepdims=True)
    grad_scores = (probs * (grad_probs - inner)).astype(BF16)
    sum_k[...] += lax.dot_general(
        grad_scores, q, (((0,), (0,)), ((), ())), preferred_element_type=F32
    )
    grad_q = jnp.dot(grad_scores, k, preferred_element_type=F32) * DH ** (-0.5)
    grad_q, grad_gain = head_back(
        grad_q, raw_q_ref[...], qg_ref[...], cos_q_ref[...], sin_q_ref[...]
    )
    dq_ref[...] = grad_q.astype(BF16)
    dqg_ref[...] += grad_gain

    @pl.when(i == pl.num_programs(1) - 1)
    def _():
        grad_k, gain_k = head_back(
            sum_k[...] * DH ** (-0.5), raw_k_ref[...], kg_ref[...], cos_ref[...], sin_ref[...]
        )
        dk_ref[...] = grad_k.astype(BF16)
        dkg_ref[...] += gain_k
        dv_ref[...] = sum_v[...].astype(BF16)


def attend_back(q, k, v, grad, logs, seg_q, seg_k, raw, q_gain, k_gain, cosine, sine, block=256):
    rows, width = q.shape
    heads = width // DH
    by_rows = pl.BlockSpec((block, DH), lambda h, i: (i, h))
    whole = pl.BlockSpec((rows, DH), lambda h, i: (0, h))
    gain = pl.BlockSpec((1, DH), lambda h, i: (0, 0))
    return pl.pallas_call(
        attend_back_kernel,
        name="attend_back",
        grid=(heads, rows // block),
        in_specs=[
            by_rows,
            whole,
            whole,
            by_rows,
            pl.BlockSpec((1, block, 1), lambda h, i: (h, i, 0)),
            pl.BlockSpec((block, 1), lambda h, i: (i, 0)),
            pl.BlockSpec((1, rows), lambda h, i: (0, 0)),
            by_rows,
            pl.BlockSpec((rows, DH), lambda h, i: (0, heads + h)),
            gain,
            gain,
            pl.BlockSpec((block, DH), lambda h, i: (i, 0)),
            pl.BlockSpec((block, DH), lambda h, i: (i, 0)),
            pl.BlockSpec((rows, DH), lambda h, i: (0, 0)),
            pl.BlockSpec((rows, DH), lambda h, i: (0, 0)),
        ],
        out_specs=[by_rows, whole, whole, gain, gain],
        out_shape=[
            jax.ShapeDtypeStruct((rows, width), BF16),
            jax.ShapeDtypeStruct((rows, width), BF16),
            jax.ShapeDtypeStruct((rows, width), BF16),
            jax.ShapeDtypeStruct((1, DH), F32),
            jax.ShapeDtypeStruct((1, DH), F32),
        ],
        scratch_shapes=[pltpu.VMEM((rows, DH), F32), pltpu.VMEM((rows, DH), F32)],
        cost_estimate=cost(1000, 1000),
    )(q, k, v, grad, logs, seg_q, seg_k, raw, raw, q_gain, k_gain, cosine, sine, cosine, sine)


def branch_kernel(
    at_ref, x_ref, att_ref, own_ref, other_ref, gain_ref, normed_ref, scale_ref, mixed_ref, total
):
    half = own_ref.shape[0]
    own = contract_last(att_ref[...], own_ref[...])
    other = contract_last(att_ref[...], other_ref[...])
    second = at_ref[0] == 1
    total[:, :half] = x_ref[:, :half].astype(F32) + jnp.where(second, other, own)
    total[:, half:] = x_ref[:, half:].astype(F32) + jnp.where(second, own, other)
    mixed = total[...]
    scale = lax.rsqrt(jnp.mean(mixed * mixed, axis=1, keepdims=True) + EPSILON)
    normed_ref[...] = (mixed * scale * gain_ref[...]).astype(BF16)
    scale_ref[...] = scale
    width = mixed_ref.shape[1]
    mixed_ref[...] = total[:, pl.ds(pl.multiple_of(at_ref[1] * width, 128), width)]


def run_branch(core, col, x, attended, own, other, gain, width, block=256):
    rows = attended.shape[0]
    by_rows = lambda n: pl.BlockSpec((block, n), lambda i, at: (i, 0))
    whole = lambda a: pl.BlockSpec(a.shape, lambda i, at: (0, 0))
    return pl.pallas_call(
        branch_kernel,
        name="branch",
        grid_spec=pltpu.PrefetchScalarGridSpec(
            num_scalar_prefetch=1,
            grid=(rows // block,),
            in_specs=[by_rows(D), by_rows(D), whole(own), whole(other), whole(gain)],
            out_specs=[by_rows(D), by_rows(1), by_rows(width)],
            scratch_shapes=[pltpu.VMEM((block, D), F32)],
        ),
        out_shape=[
            jax.ShapeDtypeStruct((rows, D), BF16),
            jax.ShapeDtypeStruct((rows, 1), F32),
            jax.ShapeDtypeStruct((rows, width), F32),
        ],
        cost_estimate=cost(1000, 1000),
    )(jnp.stack([core, col]), x, attended, own, other, gain)


def expert_kernel(x_ref, c_ref, gate_ref, w_ref, wd_ref, act_ref, grad_ref, sums_ref, dx_ref):
    width = act_ref.shape[1]
    slot_gate = gate_ref[...]
    pre = jnp.dot(x_ref[...], w_ref[...], preferred_element_type=F32)
    gate, up = pre[:, :width], pre[:, width:]
    grad = jnp.dot(c_ref[...], wd_ref[...], preferred_element_type=F32)
    opened = 1.0 / (1.0 + jnp.exp(-gate))
    silu = gate * opened
    act = silu * up
    act_ref[...] = (slot_gate * act).astype(BF16)
    grad_gate = jnp.sum(act * grad, axis=1, keepdims=True)
    grad = slot_gate * grad
    dgate = (grad * up * opened * (1.0 + gate * (1.0 - opened))).astype(BF16)
    dup = (grad * silu).astype(BF16)
    grad_ref[:, :width] = dgate
    grad_ref[:, width:] = dup
    inner = jnp.sum(dgate.astype(F32) * gate + dup.astype(F32) * up, axis=1, keepdims=True)
    sums_ref[:, 0:1] = grad_gate
    sums_ref[:, 1:2] = inner
    dx_ref[...] = contract_last(grad_ref[...], w_ref[...], BF16)


def run_expert(x, c, slot_gate, w, wd, block):
    rows, width = x.shape[0], wd.shape[1]
    by_rows = lambda n: pl.BlockSpec((block, n), lambda i: (i, 0))
    whole = lambda a: pl.BlockSpec(a.shape, lambda i: (0, 0), pipeline_mode=pl.Buffered(1))
    return pl.pallas_call(
        expert_kernel,
        name="expert",
        grid=(rows // block,),
        in_specs=[by_rows(D), by_rows(D), by_rows(1), whole(w), whole(wd)],
        out_specs=[by_rows(width), by_rows(2 * width), by_rows(2), by_rows(D)],
        out_shape=[
            jax.ShapeDtypeStruct((rows, width), BF16),
            jax.ShapeDtypeStruct((rows, 2 * width), BF16),
            jax.ShapeDtypeStruct((rows, 2), F32),
            jax.ShapeDtypeStruct((rows, D), BF16),
        ],
        cost_estimate=cost(1000, 1000),
    )(x, c, slot_gate, w, wd)


def combine_kernel(*refs):
    rank_ref, out_ref = refs[0], refs[-1]
    pieces = refs[1:-1]
    total = 0.0
    for i, piece in enumerate(pieces):
        shape = (piece.shape[0], out_ref.shape[0])
        slots = lax.broadcasted_iota(jnp.int32, shape, 0)
        hits = (slots == rank_ref[i : i + 1, :]).astype(BF16)
        total = total + contract_first(hits, piece[...])
    out_ref[...] = total.astype(BF16)


def combine(ranks, pieces, block=256):
    rows = ranks.shape[1]
    width = 1024
    whole = lambda a: pl.BlockSpec((a.shape[0], width), lambda j, i: (0, j))
    return pl.pallas_call(
        combine_kernel,
        name="combine",
        grid=(D // width, rows // block),
        in_specs=[pl.BlockSpec((len(pieces), block), lambda j, i: (0, i))]
        + [whole(piece) for piece in pieces],
        out_specs=pl.BlockSpec((block, width), lambda j, i: (i, j)),
        out_shape=jax.ShapeDtypeStruct((rows, D), BF16),
        cost_estimate=cost(1000, 1000),
    )(ranks, *pieces)


def place_kernel(at_ref, *refs):
    out_ref = refs[-1]
    for i, piece in enumerate(refs[:-1]):
        experts, _, units = piece.shape
        first, unit = at_ref[2 * i], pl.multiple_of(at_ref[2 * i + 1], 128)
        for e in range(experts):
            out_ref[first + e, :, pl.ds(unit, units)] = piece[e].astype(F32)


def place(places, pieces, experts, units, block=64):
    rows = pieces[0].shape[1]
    spec = lambda a: pl.BlockSpec((a.shape[0], block, a.shape[2]), lambda i, at: (0, i, 0))
    return pl.pallas_call(
        place_kernel,
        name="place",
        grid_spec=pltpu.PrefetchScalarGridSpec(
            num_scalar_prefetch=1,
            grid=(rows // block,),
            in_specs=[spec(piece) for piece in pieces],
            out_specs=pl.BlockSpec((experts, block, units), lambda i, at: (0, i, 0)),
        ),
        out_shape=jax.ShapeDtypeStruct((experts, rows, units), F32),
        cost_estimate=cost(1000, 1000),
    )(places, *pieces)


def body(
    hidden_in,
    token_order,
    lengths,
    key_mask,
    routes,
    norm1_gain,
    query_gain,
    key_gain,
    w_query,
    w_key,
    w_value,
    w_out,
    norm2_gain,
    router,
    w_gate,
    w_up,
    w_down,
    cotangent,
):
    tok_count, feat_local = hidden_in.shape
    n_row = D // w_query.shape[0]
    n_col = D // feat_local
    local_experts, _, hidden_units = w_gate.shape
    per_device = max(1, local_experts // n_row)
    unit_split = max(1, n_row // local_experts)
    capacity = 5 * tok_count * TOP // (4 * E)
    col = lax.axis_index("col")
    row = lax.axis_index("row")
    core = row % 2
    steps = range(n_row)
    peers = [row ^ step for step in steps]
    near, far = list(steps)[:2], list(steps)[2:]
    rows_local = D // n_row
    unit_count = hidden_units // unit_split
    places = jnp.arange(tok_count, dtype=jnp.int32)
    order_row = token_order[0]
    inverse = jnp.zeros((tok_count,), jnp.int32).at[order_row].set(places)
    segment, position = layout(lengths[0], tok_count)

    packed_b = hidden_in[order_row]
    gains_b = jnp.concatenate([thirds(norm1_gain), thirds(norm2_gain)])
    gathered = gather_features(jnp.concatenate([packed_b, jnp.pad(gains_b, ((0, 10), (0, 0)))]))
    cot_b = cotangent[order_row]

    width_local = w_query.shape[1]
    head_count = width_local // DH
    weight_rows = jnp.concatenate([w_query, w_key, w_value, w_out, router.T], axis=1)
    weight_pieces = {step: trade(weight_rows, step, n_row) for step in steps if step % 2 == 0}
    for step in steps:
        if step % 2 == 1:
            weight_pieces[step] = trade(weight_pieces[step ^ 1], 1, n_row)
    weight_heads = jnp.zeros((D, weight_rows.shape[1]), BF16)
    for step in steps:
        weight_heads = lax.dynamic_update_slice(
            weight_heads, weight_pieces[step], (peers[step] * rows_local, 0)
        )
    w_qkv = weight_heads[:, : 3 * width_local]
    w_out_own = weight_heads[:, 3 * width_local : 4 * width_local]
    router_all = weight_heads[:, 4 * width_local :]

    def owned_at(peer):
        return (peer * per_device // unit_split, 0, (peer % unit_split) * unit_count)

    all_weights = (w_gate, w_up, w_down)
    all_parts = [(which, e) for which in range(3) for e in range(per_device)]
    owned = {}
    w_in = [jnp.zeros((D, 2 * unit_count), BF16) for e in range(per_device)]
    w_back = [jnp.zeros((D, unit_count), BF16) for e in range(per_device)]

    def slices(parts):
        pieces = []
        for step in steps if parts else ():
            first, _, unit = owned_at(peers[step])
            held = [
                lax.dynamic_slice(
                    all_weights[which], (first + e, 0, unit), (1, rows_local, unit_count)
                )
                for which, e in parts
            ]
            pieces.append(jnp.concatenate(held))
        return pieces

    def to_owner(parts, pieces, *earlier):
        pieces = trade_all(after(pieces, *earlier))
        for i, (which, e) in enumerate(parts):
            for step in steps:
                at = (peers[step] * rows_local, unit_count if which == 1 else 0)
                if which < 2:
                    w_in[e] = lax.dynamic_update_slice(w_in[e], pieces[step][i], at)
                else:
                    w_back[e] = lax.dynamic_update_slice(w_back[e], pieces[step][i], at)
        return pieces

    def tied(value):
        value, w_in[:], w_back[:] = lax.optimization_barrier((value, w_in[:], w_back[:]))
        return value

    first_parts, second_parts = all_parts[:per_device], all_parts[per_device : per_device + 1]
    third_parts = all_parts[per_device + 1 : 2 * per_device + 1]
    last_parts = all_parts[2 * per_device + 1 :]
    first_pieces = to_owner(first_parts, slices(first_parts))
    second_pieces = after(slices(second_parts), *w_in)
    later = [slices(parts) for parts in (third_parts, last_parts)]
    far_bases = far[::2]
    gathered, second_pieces, later, cot_b = tied((gathered, second_pieces, later, cot_b))
    gains = gathered[tok_count : tok_count + 6].astype(F32).reshape(2, 3, D).sum(axis=1)

    expert_ids = jnp.arange(E, dtype=jnp.int32)
    routes_t = routes.T
    chosen = jnp.any(routes_t[None] == expert_ids[:, None, None], axis=1)
    own_ids = col * local_experts + jnp.arange(local_experts, dtype=jnp.int32)
    own_chosen = jnp.any(routes_t[None] == own_ids[:, None, None], axis=1)
    earlier = (places[:, None] < places[None, :]).astype(BF16)
    rank = plain_dot(own_chosen.astype(BF16), earlier).astype(jnp.int32)
    slot_rank = jnp.where(own_chosen, rank, -1)
    slots = jnp.arange(capacity, dtype=jnp.int32)

    def of_peer(table, step, e):
        return lax.dynamic_slice_in_dim(table, owned_at(peers[step])[0] + e, 1, 0)

    hits = [
        [of_peer(slot_rank, step, e) == slots[:, None] for step in steps]
        for e in range(per_device)
    ]
    picks = [[hit.astype(BF16) for hit in hits[e]] for e in range(per_device)]

    far_ranks = {base: trade(slot_rank.astype(F32), base, n_row) for base in far_bases}

    def swap_small(pieces):
        table = jnp.zeros((n_row,) + pieces[0].shape, pieces[0].dtype)
        for step in steps:
            table = jnp.where(
                jnp.arange(n_row).reshape((-1,) + (1,) * pieces[0].ndim) == peers[step],
                pieces[step][None],
                table,
            )
        table = lax.all_to_all(table, "row", 0, 0, tiled=True)
        return [lax.dynamic_index_in_dim(table, peers[step], 0, False) for step in steps]

    cosine, sine = rope_tables(position)
    q_gain, k_gain = query_gain[None], key_gain[None]
    normed1, scale_in, raw_qk, query_rot, key_rot, values_b = project(
        gathered, gains[:1], weight_heads, q_gain, k_gain, cosine, sine, width_local
    )
    seg_q, seg_k = segment[:, None], jnp.where(key_mask == 1, segment, -1)[None]
    attended_b, log_totals = attend(query_rot, key_rot, values_b, seg_q, seg_k)

    half = D // 2
    out_half = lax.dynamic_slice_in_dim(w_out_own, core * half, half, 0)
    out_half_all = gather_features(after(out_half, *first_pieces[:-1]))

    to_owner(second_parts, second_pieces)
    attended_b = tied(attended_b)
    attended_all = gather_features(after(attended_b, out_half_all))
    far_cots = [trade(after(cot_b, *w_in), base, n_row) for base in far_bases]
    to_owner(third_parts, later[0], attended_b, far_cots)
    other_half = trade(after(out_half_all, *w_back), 1, n_row)
    cot_alls = {
        base: gather_features(after(cot, w_back[0])) for base, cot in zip(far_bases, far_cots)
    }
    attended_all = tied(attended_all)
    if last_parts:
        to_owner(last_parts, later[1], w_back[0])
    normed2, scale_mid, mixed = run_branch(
        core, col, gathered, attended_all, out_half_all, other_half, gains[1:], feat_local
    )
    cot_alls[0] = gather_features(after(cot_b, normed2))
    column_start = col * feat_local

    def chosen_rows(e, values):
        return [plain_dot(picks[e][step], values, BF16) for step in steps]

    sent_rows = [chosen_rows(e, normed2) for e in range(per_device)]
    sent_rows[0] = tied(sent_rows[0])
    all_rows = [trade_all(pieces) for pieces in sent_rows]

    def grad_rows_of(base, cots):
        table = far_ranks[base] if base else slot_rank.astype(F32)
        halves = []
        for step in near:
            held = []
            for e in range(per_device):
                pick = (of_peer(table, step, e) == slots[:, None].astype(F32)).astype(BF16)
                held.append(plain_dot(pick, cots, BF16))
            halves.append(jnp.stack(held))
        return halves

    grad_rows_at = {}

    def hand_on(base, halves):
        grad_rows_at[base], grad_rows_at[base + 1] = halves[0], trade(halves[1], 1, n_row)

    for base in far_bases:
        hand_on(base, grad_rows_of(base, after(cot_alls[base], sent_rows)))

    logits = lax.dot_general(
        router_all, normed2, (((0,), (1,)), ((), ())), preferred_element_type=F32
    )
    top_logit = jnp.max(jnp.where(chosen, logits, -jnp.inf), axis=0, keepdims=True)
    raised = jnp.where(chosen, jnp.exp(logits - top_logit), 0.0)
    gate_probs = raised / jnp.sum(raised, axis=0, keepdims=True)
    own_probs = lax.dynamic_slice_in_dim(gate_probs, col * local_experts, local_experts, 0)

    slot_gates = []
    for step in steps:
        held = [
            jnp.sum(jnp.where(hits[e][step], of_peer(own_probs, step, e), 0.0), axis=1)
            for e in range(per_device)
        ]
        slot_gates.append(jnp.stack(held))
    slot_gates = swap_small(slot_gates)

    both = range(per_device)
    calls, grads_back = {}, [[None] * n_row for e in range(per_device)]

    def expert_call(e, held):
        rows = jnp.concatenate([all_rows[e][step] for step in held])
        grad_rows = jnp.concatenate([grad_rows_at[step][e] for step in held])
        slot_gate = jnp.concatenate([slot_gates[step][e] for step in held])[:, None]
        results = run_expert(rows, grad_rows, slot_gate, w_in[e], w_back[e], 2 * capacity)
        calls[e, held[0]] = [rows, grad_rows, *results]

    def send_back(e, held):
        grads = calls[e, held[0]][-1]
        for i, step in enumerate(held):
            piece = grads[i * capacity : (i + 1) * capacity]
            grads_back[e][step] = trade(piece, step, n_row)

    expert_call(0, far)
    send_back(0, far)
    for e in range(1, per_device):
        all_rows[e] = after(all_rows[e], calls[0, 2])
        expert_call(e, far)
    near_halves = grad_rows_of(0, after(cot_alls[0], [calls[e, 2] for e in both]))
    for e in range(1, per_device):
        calls[e, 2], grads_back[e - 1], near_halves = lax.optimization_barrier(
            (calls[e, 2], grads_back[e - 1], near_halves)
        )
        send_back(e, far)
    hand_on(0, near_halves)
    for e in range(per_device):
        expert_call(e, near)
        send_back(e, near)
    last_near = (per_device - 1, 0)
    calls[last_near], grads_back[-1] = lax.optimization_barrier((calls[last_near], grads_back[-1]))
    scalars = [jnp.concatenate([calls[e, 0][4], calls[e, 2][4]]) for e in range(per_device)]
    scalars = jnp.stack(scalars)
    scalars_back = swap_small(
        [scalars[:, step * capacity : (step + 1) * capacity] for step in steps]
    )
    every = [(e, step) for e in range(per_device) for step in steps]
    ranks = jnp.concatenate([of_peer(slot_rank, step, e) for e, step in every])
    grad_normed2_part = combine(ranks, [grads_back[e][step] for e, step in every])

    calls = after(calls, grad_normed2_part)
    branch_back, weight_grads = [], []
    for e in range(per_device):
        rows, grad_rows, act, grad_pre = (
            jnp.concatenate([calls[e, 0][i], calls[e, 2][i]]) for i in range(4)
        )
        out = contract_last(act, w_back[e], BF16)
        branch_back.append(
            trade_all([out[step * capacity : (step + 1) * capacity] for step in steps])
        )
        grad_in = contract_first(rows, grad_pre, BF16)
        weight_grads.append(
            (
                grad_in[:, :unit_count],
                grad_in[:, unit_count:],
                contract_first(grad_rows, act, BF16),
            )
        )
    grad_normed2 = scatter_partial(grad_normed2_part).astype(F32)

    grad_own = jnp.zeros((local_experts, tok_count), F32)
    inner_own = jnp.zeros((1, tok_count), F32)
    own_rows = jnp.arange(local_experts, dtype=jnp.int32)[:, None]
    for e in range(per_device):
        for step in steps:
            expert = owned_at(peers[step])[0] + e
            back = scalars_back[step][e]
            spread = jnp.sum(jnp.where(hits[e][step], back[:, :1], 0.0), axis=0, keepdims=True)
            grad_own = grad_own + jnp.where(own_rows == expert, spread, 0.0)
            inner_own = inner_own + jnp.sum(
                jnp.where(hits[e][step], back[:, 1:], 0.0), axis=0, keepdims=True
            )
    small = jnp.concatenate([grad_own, inner_own], axis=0)
    small, branch_back[0] = lax.optimization_barrier((small, branch_back[0]))
    small = lax.all_to_all(
        jnp.broadcast_to(small[None], (n_col,) + small.shape), "col", 0, 0, tiled=True
    )
    small, branch_back = lax.optimization_barrier((small, branch_back))
    grad_gates = small[:, :local_experts].reshape(E, tok_count)
    grad_logits = gate_probs * (
        grad_gates - jnp.sum(gate_probs * grad_gates, axis=0, keepdims=True)
    )
    grad_logits = grad_logits.astype(BF16)
    inner_mid = jnp.sum(small[:, local_experts], axis=0) + jnp.sum(
        grad_logits.astype(F32) * logits, axis=0
    )
    inner_mid = (inner_mid / D)[:, None]
    grad_router = lax.dot_general(
        normed2, grad_logits, (((0,), (1,)), ((), ())), preferred_element_type=F32
    )
    router_local = lax.dynamic_slice_in_dim(router_all, column_start, feat_local, 0)
    grad_unit_mid = grad_normed2 + lax.dot_general(
        grad_logits, router_local, (((0,), (1,)), ((), ())), preferred_element_type=F32
    )
    unit_mid = mixed * scale_mid
    grad_norm2 = jnp.sum(grad_unit_mid * unit_mid, axis=0)
    scaled_mid = grad_unit_mid * norm2_gain
    grad_mixed = cot_b.astype(F32) + scale_mid * (scaled_mid - unit_mid * inner_mid)
    def held_slices(which, experts):
        return [
            jnp.stack(
                [
                    lax.dynamic_slice_in_dim(
                        weight_grads[e][which], peers[step] * rows_local, rows_local, 0
                    )
                    for e in experts
                ]
            )
            for step in steps
        ]

    def to_holders(pieces, *earlier):
        return trade_all(after(pieces, *earlier))

    gate_slices, up_slices = held_slices(0, both), held_slices(1, both)
    grad_mixed_b, gate_slices, up_slices, inverse = lax.optimization_barrier(
        (grad_mixed.astype(BF16), gate_slices, up_slices, inverse)
    )
    grad_branch = gather_features(grad_mixed_b)
    gate_pieces = to_holders(gate_slices)

    def to_rows(pieces):
        flat, places = [], []
        for e, held in enumerate(pieces):
            for step in steps:
                first, _, unit = owned_at(peers[step])
                flat.append(held[step])
                places += [first + e, unit]
        return place(jnp.stack(places), flat, local_experts, hidden_units)

    def sum_groups(grad, *earlier):
        grad = after(grad, *earlier)
        parts = [
            lax.dynamic_slice_in_dim(grad, peers[step] * rows_local, rows_local, 0)
            for step in steps
        ]
        other = trade(jnp.stack(parts[1::2]), 1, n_row).astype(F32)
        sums = [part.astype(F32) + other[i] for i, part in enumerate(parts[::2])]
        total = sums[0]
        for i, base in enumerate(far_bases):
            total = total + trade(sums[i + 1].astype(grad.dtype), base, n_row).astype(F32)
        return total

    combined_part = combine(ranks, [branch_back[e][step] for e, step in every])
    grad_branch, gate_pieces, combined_part = lax.optimization_barrier(
        (grad_branch, gate_pieces, combined_part)
    )
    up_pieces = to_holders(up_slices, gate_pieces)

    combined = scatter_partial(combined_part)

    grad_w_out = contract_first(grad_branch, attended_b, BF16)
    grad_w_gate = to_rows([gate_pieces])
    grad_attended = plain_dot(after(grad_branch, grad_w_gate), w_out_own, BF16)
    grad_q, grad_k, grad_v, grad_query_gain, grad_key_gain = attend_back(
        query_rot, key_rot, values_b, grad_attended, log_totals, seg_q, seg_k, raw_qk,
        q_gain, k_gain, cosine, sine,
    )
    grad_qkv = jnp.concatenate([grad_q, grad_k, grad_v], axis=1)
    grad_w_out = sum_groups(grad_w_out)
    grad_router = sum_groups(grad_router, grad_branch).T
    down_slices = [held_slices(2, [e]) for e in range(per_device)]
    grad_qkv, up_pieces, combined, down_slices, grad_w_out, grad_router = (
        lax.optimization_barrier(
            (grad_qkv, up_pieces, combined, down_slices, grad_w_out, grad_router)
        )
    )
    down_pieces = [to_holders(down_slices[0])]
    grad_normed1_part = contract_last(grad_qkv, w_qkv, BF16)
    grad_unit_in = scatter_partial(grad_normed1_part)
    output = (mixed + combined.astype(F32)).astype(BF16)[inverse]
    grad_w_up = to_rows([up_pieces])
    grad_normed1_part, down_pieces, output, grad_w_up = lax.optimization_barrier(
        (grad_normed1_part, down_pieces, output, grad_w_up)
    )
    down_pieces += [to_holders(held, down_pieces) for held in down_slices[1:]]
    inner_in = jnp.sum(
        grad_qkv.astype(F32) * jnp.concatenate([raw_qk, values_b.astype(F32)], axis=1), axis=1
    )
    packed = packed_b.astype(F32)
    unit_in = packed * scale_in
    unit_all = gathered[:tok_count].astype(F32) * scale_in
    grad_norm1 = jnp.sum(grad_normed1_part.astype(F32) * unit_all, axis=0)
    def for_all(vector):
        return jnp.broadcast_to(vector[None], (n_col,) + vector.shape)

    vectors = jnp.concatenate(
        [
            for_all(inner_in),
            for_all(grad_query_gain[0]),
            for_all(grad_key_gain[0]),
            grad_norm1.reshape(n_col, feat_local),
        ],
        axis=1,
    )
    heads_grad = contract_first(normed1, grad_qkv, BF16)
    vectors, down_pieces, heads_grad = lax.optimization_barrier(
        (vectors, down_pieces, heads_grad)
    )
    vectors = jnp.sum(lax.all_to_all(vectors, "col", 0, 0, tiled=True), axis=0)
    inner_in = vectors[:tok_count, None] / D
    vectors = jnp.concatenate([vectors[tok_count:], grad_norm2])
    vectors = sum(trade(vectors, step, n_row) for step in steps)
    grad_heads = sum_groups(heads_grad)
    grad_unit_in, vectors, inner_in, grad_heads = lax.optimization_barrier(
        (grad_unit_in, vectors, inner_in, grad_heads)
    )
    grad_unit_in = grad_unit_in.astype(F32)
    scaled_in = grad_unit_in * norm1_gain
    grad_input = (grad_mixed + scale_in * (scaled_in - unit_in * inner_in))[inverse]

    grad_w_query, grad_w_key, grad_w_value = (
        grad_heads[:, i * width_local : (i + 1) * width_local] for i in range(3)
    )
    grad_w_down = to_rows(down_pieces)

    grad_query_gain, grad_key_gain = vectors[:DH], vectors[DH : 2 * DH]
    grad_norm1 = vectors[2 * DH : 2 * DH + feat_local]
    grad_norm2 = vectors[2 * DH + feat_local :]
    return (
        output,
        grad_input,
        grad_norm1,
        grad_query_gain,
        grad_key_gain,
        grad_w_query,
        grad_w_key,
        grad_w_value,
        grad_w_out,
        grad_norm2,
        grad_router,
        grad_w_gate,
        grad_w_up,
        grad_w_down,
    )


def solution(mesh):
    return jax.shard_map(
        body,
        mesh=mesh,
        in_specs=(
            P("row", "col"),
            P("row", None),
            P("row", None),
            P("row"),
            P("row", None),
            P("col"),
            P(),
            P(),
            P("row", "col"),
            P("row", "col"),
            P("row", "col"),
            P("row", "col"),
            P("col"),
            P(None, "row"),
            P("col", "row", None),
            P("col", "row", None),
            P("col", "row", None),
            P("row", "col"),
        ),
        out_specs=(
            P("row", "col"),
            P("row", "col"),
            P("col"),
            P(),
            P(),
            P("row", "col"),
            P("row", "col"),
            P("row", "col"),
            P("row", "col"),
            P("col"),
            P(None, "row"),
            P("col", "row", None),
            P("col", "row", None),
            P("col", "row", None),
        ),
        check_vma=False,
    )
```

```python
import jax
import jax.numpy as jnp
from jax import lax
from jax.experimental import pallas as pl
from jax.experimental.pallas import tpu as pltpu
from jax.sharding import PartitionSpec as P

D = 2048
DH = 128
E = 64
TOP = 8


EPSILON = 1e-06
ROPE_BASE = 10000.0
BF16 = jnp.bfloat16
F32 = jnp.float32


def layout(seq_lengths, tok_count):
    seq_ends = jnp.cumsum(seq_lengths)
    seq_starts = seq_ends - seq_lengths
    places = jnp.arange(tok_count, dtype=jnp.int32)
    segment = jnp.sum((places[:, None] >= seq_ends[None, :]).astype(jnp.int32), axis=1)
    member = segment[:, None] == jnp.arange(seq_lengths.shape[0], dtype=jnp.int32)[None, :]
    offset = jnp.sum(jnp.where(member, seq_starts[None, :], 0), axis=1)
    return (segment, places - offset)


def rope_tables(position):
    half_dim = DH // 2
    frequency = ROPE_BASE ** (-2.0 * jnp.arange(half_dim, dtype=F32) / DH)
    angles = position.astype(F32)[:, None] * frequency[None, :]
    cosine, sine = jnp.cos(angles), jnp.sin(angles)
    return jnp.concatenate([cosine, cosine], 1), jnp.concatenate([-sine, sine], 1)


def gather_features(local_rows):
    return lax.all_gather(local_rows, "col", axis=1, tiled=True)


def scatter_partial(partial_rows):
    return lax.psum_scatter(partial_rows, "col", scatter_dimension=1, tiled=True)


def trade(value, step, n_row):
    if step == 0:
        return value
    return lax.ppermute(value, "row", [(r, r ^ step) for r in range(n_row)])


def trade_all(pieces):
    return [trade(piece, step, len(pieces)) for step, piece in enumerate(pieces)]


def contract_last(left_op, right_op, kind=F32):
    return lax.dot_general(
        left_op, right_op, (((1,), (1,)), ((), ())), preferred_element_type=F32
    ).astype(kind)


def contract_first(left_op, right_op, kind=F32):
    return lax.dot_general(
        left_op, right_op, (((0,), (0,)), ((), ())), preferred_element_type=F32
    ).astype(kind)


def plain_dot(left_op, right_op, kind=F32):
    return jnp.dot(left_op, right_op, preferred_element_type=F32).astype(kind)


def after(value, *earlier):
    return lax.optimization_barrier((value, *earlier))[0]


def thirds(values):
    high = lax.reduce_precision(values, 8, 7)
    middle = lax.reduce_precision(values - high, 8, 7)
    return jnp.stack([high, middle, values - high - middle]).astype(BF16)


def cost(flops, moved):
    return pl.CostEstimate(flops=flops, bytes_accessed=moved, transcendentals=0)


def rope(values, cosine, sine):
    return values * cosine + pltpu.roll(values, DH // 2, 1) * sine


def rope_back(grad, cosine, sine):
    return grad * cosine + pltpu.roll(grad * sine, DH // 2, 1)


def project_kernel(x_ref, gain_ref, w_ref, qg_ref, kg_ref, cos_ref, sin_ref, *outs):
    normed_ref, scale_ref, raw_ref, q_ref, k_ref, v_ref = outs
    x = x_ref[...].astype(F32)
    scale = lax.rsqrt(jnp.mean(x * x, axis=1, keepdims=True) + EPSILON)
    normed = (x * scale * gain_ref[...]).astype(BF16)
    normed_ref[...] = normed
    scale_ref[...] = scale
    width = q_ref.shape[1]
    qkv = jnp.dot(normed, w_ref[:, : 3 * width], preferred_element_type=F32)
    raw_ref[...] = qkv[:, : 2 * width]
    v_ref[...] = qkv[:, 2 * width :].astype(BF16)
    cosine, sine = cos_ref[...], sin_ref[...]
    for part, gain, out in ((0, qg_ref, q_ref), (1, kg_ref, k_ref)):
        for h in range(width // DH):
            head = qkv[:, part * width + h * DH : part * width + (h + 1) * DH]
            size = lax.rsqrt(jnp.mean(head * head, axis=1, keepdims=True) + EPSILON)
            out[:, h * DH : (h + 1) * DH] = rope(head * size * gain[...], cosine, sine).astype(BF16)


def project(x, gain, w, q_gain, k_gain, cosine, sine, width, block=256):
    rows = cosine.shape[0]
    by_rows = lambda n: pl.BlockSpec((block, n), lambda i: (i, 0))
    whole = lambda a: pl.BlockSpec(a.shape, lambda i: (0, 0))
    return pl.pallas_call(
        project_kernel,
        name="project",
        grid=(rows // block,),
        in_specs=[
            by_rows(D),
            whole(gain),
            whole(w),
            whole(q_gain),
            whole(k_gain),
            by_rows(DH),
            by_rows(DH),
        ],
        out_specs=[by_rows(n) for n in (D, 1, 2 * width, width, width, width)],
        out_shape=[
            jax.ShapeDtypeStruct((rows, D), BF16),
            jax.ShapeDtypeStruct((rows, 1), F32),
            jax.ShapeDtypeStruct((rows, 2 * width), F32),
            jax.ShapeDtypeStruct((rows, width), BF16),
            jax.ShapeDtypeStruct((rows, width), BF16),
            jax.ShapeDtypeStruct((rows, width), BF16),
        ],
        cost_estimate=cost(1000, 1000),
    )(x, gain, w, q_gain, k_gain, cosine, sine)


def masked_scores(q, k, seg_q, seg_k, first):
    scores = lax.dot_general(q, k, (((1,), (1,)), ((), ())), preferred_element_type=F32)
    rows = first + lax.broadcasted_iota(jnp.int32, scores.shape, 0)
    columns = lax.broadcasted_iota(jnp.int32, scores.shape, 1)
    allowed = (seg_q == seg_k) | (rows == columns)
    return jnp.where(allowed, scores * DH ** (-0.5), -1e30)


def attend_kernel(q_ref, k_ref, v_ref, seg_q_ref, seg_k_ref, out_ref, log_ref):
    first = pl.program_id(1) * q_ref.shape[0]
    scores = masked_scores(q_ref[...], k_ref[...], seg_q_ref[...], seg_k_ref[...], first)
    top = jnp.max(scores, axis=1, keepdims=True)
    terms = jnp.exp(scores - top)
    total = jnp.sum(terms, axis=1, keepdims=True)
    weights = (terms * (1.0 / total)).astype(BF16)
    out_ref[...] = jnp.dot(weights, v_ref[...], preferred_element_type=F32).astype(BF16)
    log_ref[0] = top + jnp.log(total)


def attend(q, k, v, seg_q, seg_k, block=256):
    rows, width = q.shape
    heads = width // DH
    by_rows = pl.BlockSpec((block, DH), lambda h, i: (i, h))
    whole = pl.BlockSpec((rows, DH), lambda h, i: (0, h))
    return pl.pallas_call(
        attend_kernel,
        name="attend",
        grid=(heads, rows // block),
        in_specs=[
            by_rows,
            whole,
            whole,
            pl.BlockSpec((block, 1), lambda h, i: (i, 0)),
            pl.BlockSpec((1, rows), lambda h, i: (0, 0)),
        ],
        out_specs=[by_rows, pl.BlockSpec((1, block, 1), lambda h, i: (h, i, 0))],
        out_shape=[
            jax.ShapeDtypeStruct((rows, width), BF16),
            jax.ShapeDtypeStruct((heads, rows, 1), F32),
        ],
        cost_estimate=cost(1000, 1000),
    )(q, k, v, seg_q, seg_k)


def head_back(grad, raw, gain, cosine, sine):
    grad = rope_back(grad, cosine, sine)
    size = lax.rsqrt(jnp.mean(raw * raw, axis=1, keepdims=True) + EPSILON)
    unit = raw * size
    grad_gain = jnp.sum(grad * unit, axis=0, keepdims=True)
    grad = grad * gain
    return size * (grad - unit * jnp.mean(grad * unit, axis=1, keepdims=True)), grad_gain


def attend_back_kernel(
    q_ref, k_ref, v_ref, grad_ref, log_ref, seg_q_ref, seg_k_ref, raw_q_ref, raw_k_ref,
    qg_ref, kg_ref, cos_q_ref, sin_q_ref, cos_ref, sin_ref,
    dq_ref, dk_ref, dv_ref, dqg_ref, dkg_ref, sum_k, sum_v,
):
    head, i = pl.program_id(0), pl.program_id(1)

    @pl.when((head == 0) & (i == 0))
    def _():
        dqg_ref[...] = jnp.zeros_like(dqg_ref)
        dkg_ref[...] = jnp.zeros_like(dkg_ref)

    @pl.when(i == 0)
    def _():
        sum_k[...] = jnp.zeros_like(sum_k)
        sum_v[...] = jnp.zeros_like(sum_v)

    q, k, grad = q_ref[...], k_ref[...], grad_ref[...]
    scores = masked_scores(q, k, seg_q_ref[...], seg_k_ref[...], i * q.shape[0])
    probs = jnp.exp(scores - log_ref[0])
    sum_v[...] += lax.dot_general(
        probs.astype(BF16), grad, (((0,), (0,)), ((), ())), preferred_element_type=F32
    )
    grad_probs = lax.dot_general(
        grad, v_ref[...], (((1,), (1,)), ((), ())), preferred_element_type=F32
    )
    inner = jnp.sum(probs * grad_probs, axis=1, keepdims=True)
    grad_scores = (probs * (grad_probs - inner)).astype(BF16)
    sum_k[...] += lax.dot_general(
        grad_scores, q, (((0,), (0,)), ((), ())), preferred_element_type=F32
    )
    grad_q = jnp.dot(grad_scores, k, preferred_element_type=F32) * DH ** (-0.5)
    grad_q, grad_gain = head_back(
        grad_q, raw_q_ref[...], qg_ref[...], cos_q_ref[...], sin_q_ref[...]
    )
    dq_ref[...] = grad_q.astype(BF16)
    dqg_ref[...] += grad_gain

    @pl.when(i == pl.num_programs(1) - 1)
    def _():
        grad_k, gain_k = head_back(
            sum_k[...] * DH ** (-0.5), raw_k_ref[...], kg_ref[...], cos_ref[...], sin_ref[...]
        )
        dk_ref[...] = grad_k.astype(BF16)
        dkg_ref[...] += gain_k
        dv_ref[...] = sum_v[...].astype(BF16)


def attend_back(q, k, v, grad, logs, seg_q, seg_k, raw, q_gain, k_gain, cosine, sine, block=256):
    rows, width = q.shape
    heads = width // DH
    by_rows = pl.BlockSpec((block, DH), lambda h, i: (i, h))
    whole = pl.BlockSpec((rows, DH), lambda h, i: (0, h))
    gain = pl.BlockSpec((1, DH), lambda h, i: (0, 0))
    return pl.pallas_call(
        attend_back_kernel,
        name="attend_back",
        grid=(heads, rows // block),
        in_specs=[
            by_rows,
            whole,
            whole,
            by_rows,
            pl.BlockSpec((1, block, 1), lambda h, i: (h, i, 0)),
            pl.BlockSpec((block, 1), lambda h, i: (i, 0)),
            pl.BlockSpec((1, rows), lambda h, i: (0, 0)),
            by_rows,
            pl.BlockSpec((rows, DH), lambda h, i: (0, heads + h)),
            gain,
            gain,
            pl.BlockSpec((block, DH), lambda h, i: (i, 0)),
            pl.BlockSpec((block, DH), lambda h, i: (i, 0)),
            pl.BlockSpec((rows, DH), lambda h, i: (0, 0)),
            pl.BlockSpec((rows, DH), lambda h, i: (0, 0)),
        ],
        out_specs=[by_rows, whole, whole, gain, gain],
        out_shape=[
            jax.ShapeDtypeStruct((rows, width), BF16),
            jax.ShapeDtypeStruct((rows, width), BF16),
            jax.ShapeDtypeStruct((rows, width), BF16),
            jax.ShapeDtypeStruct((1, DH), F32),
            jax.ShapeDtypeStruct((1, DH), F32),
        ],
        scratch_shapes=[pltpu.VMEM((rows, DH), F32), pltpu.VMEM((rows, DH), F32)],
        cost_estimate=cost(1000, 1000),
    )(q, k, v, grad, logs, seg_q, seg_k, raw, raw, q_gain, k_gain, cosine, sine, cosine, sine)


def branch_kernel(
    at_ref, x_ref, att_ref, own_ref, other_ref, gain_ref, normed_ref, scale_ref, mixed_ref, total
):
    half = own_ref.shape[0]
    own = contract_last(att_ref[...], own_ref[...])
    other = contract_last(att_ref[...], other_ref[...])
    second = at_ref[0] == 1
    total[:, :half] = x_ref[:, :half].astype(F32) + jnp.where(second, other, own)
    total[:, half:] = x_ref[:, half:].astype(F32) + jnp.where(second, own, other)
    mixed = total[...]
    scale = lax.rsqrt(jnp.mean(mixed * mixed, axis=1, keepdims=True) + EPSILON)
    normed_ref[...] = (mixed * scale * gain_ref[...]).astype(BF16)
    scale_ref[...] = scale
    width = mixed_ref.shape[1]
    mixed_ref[...] = total[:, pl.ds(pl.multiple_of(at_ref[1] * width, 128), width)]


def run_branch(core, col, x, attended, own, other, gain, width, block=256):
    rows = attended.shape[0]
    by_rows = lambda n: pl.BlockSpec((block, n), lambda i, at: (i, 0))
    whole = lambda a: pl.BlockSpec(a.shape, lambda i, at: (0, 0))
    return pl.pallas_call(
        branch_kernel,
        name="branch",
        grid_spec=pltpu.PrefetchScalarGridSpec(
            num_scalar_prefetch=1,
            grid=(rows // block,),
            in_specs=[by_rows(D), by_rows(D), whole(own), whole(other), whole(gain)],
            out_specs=[by_rows(D), by_rows(1), by_rows(width)],
            scratch_shapes=[pltpu.VMEM((block, D), F32)],
        ),
        out_shape=[
            jax.ShapeDtypeStruct((rows, D), BF16),
            jax.ShapeDtypeStruct((rows, 1), F32),
            jax.ShapeDtypeStruct((rows, width), F32),
        ],
        cost_estimate=cost(1000, 1000),
    )(jnp.stack([core, col]), x, attended, own, other, gain)


def expert_kernel(x_ref, c_ref, gate_ref, w_ref, wd_ref, act_ref, grad_ref, sums_ref, dx_ref):
    width = act_ref.shape[1]
    slot_gate = gate_ref[...]
    pre = x_ref[...]
    if pre.dtype == BF16:
        pre = jnp.dot(pre, w_ref[...], preferred_element_type=F32)
    gate, up = pre[:, :width], pre[:, width:]
    grad = jnp.dot(c_ref[...], wd_ref[...], preferred_element_type=F32)
    opened = 1.0 / (1.0 + jnp.exp(-gate))
    silu = gate * opened
    act = silu * up
    act_ref[...] = (slot_gate * act).astype(BF16)
    grad_gate = jnp.sum(act * grad, axis=1, keepdims=True)
    grad = slot_gate * grad
    dgate = (grad * up * opened * (1.0 + gate * (1.0 - opened))).astype(BF16)
    dup = (grad * silu).astype(BF16)
    grad_ref[:, :width] = dgate
    grad_ref[:, width:] = dup
    inner = jnp.sum(dgate.astype(F32) * gate + dup.astype(F32) * up, axis=1, keepdims=True)
    sums_ref[:, 0:1] = grad_gate
    sums_ref[:, 1:2] = inner
    dx_ref[...] = contract_last(grad_ref[...], w_ref[...], BF16)


def run_expert(x, c, slot_gate, w, wd, block):
    rows, width = x.shape[0], wd.shape[1]
    by_rows = lambda n: pl.BlockSpec((block, n), lambda i: (i, 0))
    whole = lambda a: pl.BlockSpec(a.shape, lambda i: (0, 0), pipeline_mode=pl.Buffered(1))
    return pl.pallas_call(
        expert_kernel,
        name="expert",
        grid=(rows // block,),
        in_specs=[by_rows(x.shape[1]), by_rows(D), by_rows(1), whole(w), whole(wd)],
        out_specs=[by_rows(width), by_rows(2 * width), by_rows(2), by_rows(D)],
        out_shape=[
            jax.ShapeDtypeStruct((rows, width), BF16),
            jax.ShapeDtypeStruct((rows, 2 * width), BF16),
            jax.ShapeDtypeStruct((rows, 2), F32),
            jax.ShapeDtypeStruct((rows, D), BF16),
        ],
        cost_estimate=cost(1000, 1000),
    )(x, c, slot_gate, w, wd)


def through_heads_kernel(grad_ref, w_ref, out_ref):
    width = grad_ref.shape[1]
    out_ref[...] = contract_last(grad_ref[...], w_ref[:, :width], BF16)


def through_heads(grad, w, block=256):
    rows, width = grad.shape
    return pl.pallas_call(
        through_heads_kernel,
        name="through_heads",
        grid=(rows // block,),
        in_specs=[
            pl.BlockSpec((block, width), lambda i: (i, 0)),
            pl.BlockSpec(w.shape, lambda i: (0, 0)),
        ],
        out_specs=pl.BlockSpec((block, D), lambda i: (i, 0)),
        out_shape=jax.ShapeDtypeStruct((rows, D), BF16),
        cost_estimate=cost(1000, 1000),
    )(grad, w)


def combine_kernel(*refs):
    rank_ref, out_ref = refs[0], refs[-1]
    pieces = refs[1:-1]
    total = 0.0
    for i, piece in enumerate(pieces):
        shape = (piece.shape[0], out_ref.shape[0])
        slots = lax.broadcasted_iota(jnp.int32, shape, 0)
        hits = (slots == rank_ref[i : i + 1, :]).astype(BF16)
        total = total + contract_first(hits, piece[...])
    out_ref[...] = total.astype(BF16)


def combine(ranks, pieces, block=256):
    rows = ranks.shape[1]
    width = 1024
    whole = lambda a: pl.BlockSpec((a.shape[0], width), lambda j, i: (0, j))
    return pl.pallas_call(
        combine_kernel,
        name="combine",
        grid=(D // width, rows // block),
        in_specs=[pl.BlockSpec((len(pieces), block), lambda j, i: (0, i))]
        + [whole(piece) for piece in pieces],
        out_specs=pl.BlockSpec((block, width), lambda j, i: (i, j)),
        out_shape=jax.ShapeDtypeStruct((rows, D), BF16),
        cost_estimate=cost(1000, 1000),
    )(ranks, *pieces)


def place_kernel(at_ref, *refs):
    out_ref = refs[-1]
    for i, piece in enumerate(refs[:-1]):
        experts, _, units = piece.shape
        first, unit = at_ref[2 * i], pl.multiple_of(at_ref[2 * i + 1], 128)
        for e in range(experts):
            out_ref[first + e, :, pl.ds(unit, units)] = piece[e].astype(F32)


def place(places, pieces, experts, units, block=64):
    rows = pieces[0].shape[1]
    spec = lambda a: pl.BlockSpec((a.shape[0], block, a.shape[2]), lambda i, at: (0, i, 0))
    return pl.pallas_call(
        place_kernel,
        name="place",
        grid_spec=pltpu.PrefetchScalarGridSpec(
            num_scalar_prefetch=1,
            grid=(rows // block,),
            in_specs=[spec(piece) for piece in pieces],
            out_specs=pl.BlockSpec((experts, block, units), lambda i, at: (0, i, 0)),
        ),
        out_shape=jax.ShapeDtypeStruct((experts, rows, units), F32),
        cost_estimate=cost(1000, 1000),
    )(places, *pieces)


def body(
    hidden_in,
    token_order,
    lengths,
    key_mask,
    routes,
    norm1_gain,
    query_gain,
    key_gain,
    w_query,
    w_key,
    w_value,
    w_out,
    norm2_gain,
    router,
    w_gate,
    w_up,
    w_down,
    cotangent,
):
    tok_count, feat_local = hidden_in.shape
    n_row = D // w_query.shape[0]
    n_col = D // feat_local
    local_experts, _, hidden_units = w_gate.shape
    per_device = max(1, local_experts // n_row)
    unit_split = max(1, n_row // local_experts)
    capacity = 5 * tok_count * TOP // (4 * E)
    col = lax.axis_index("col")
    row = lax.axis_index("row")
    core = row % 2
    steps = range(n_row)
    peers = [row ^ step for step in steps]
    near, far = list(steps)[:2], list(steps)[2:]
    rows_local = D // n_row
    unit_count = hidden_units // unit_split
    places = jnp.arange(tok_count, dtype=jnp.int32)
    order_row = token_order[0]
    inverse = jnp.zeros((tok_count,), jnp.int32).at[order_row].set(places)
    segment, position = layout(lengths[0], tok_count)

    packed_b = hidden_in[order_row]
    gains_b = jnp.concatenate([thirds(norm1_gain), thirds(norm2_gain)])
    gathered = gather_features(jnp.concatenate([packed_b, jnp.pad(gains_b, ((0, 10), (0, 0)))]))
    cot_b = cotangent[order_row]

    width_local = w_query.shape[1]
    head_count = width_local // DH
    weight_rows = jnp.concatenate([w_query, w_key, w_value, w_out, router.T], axis=1)
    weight_pieces = {step: trade(weight_rows, step, n_row) for step in steps if step % 2 == 0}
    for step in steps:
        if step % 2 == 1:
            weight_pieces[step] = trade(weight_pieces[step ^ 1], 1, n_row)
    weight_heads = jnp.zeros((D, weight_rows.shape[1]), BF16)
    for step in steps:
        weight_heads = lax.dynamic_update_slice(
            weight_heads, weight_pieces[step], (peers[step] * rows_local, 0)
        )
    w_qkv = weight_heads[:, : 3 * width_local]
    w_out_own = weight_heads[:, 3 * width_local : 4 * width_local]
    router_all = weight_heads[:, 4 * width_local :]

    def owned_at(peer):
        return (peer * per_device // unit_split, 0, (peer % unit_split) * unit_count)

    all_weights = (w_gate, w_up, w_down)
    all_parts = [(which, e) for which in range(3) for e in range(per_device)]
    owned = {}
    w_in = [jnp.zeros((D, 2 * unit_count), BF16) for e in range(per_device)]
    w_back = [jnp.zeros((D, unit_count), BF16) for e in range(per_device)]

    def slices(parts):
        pieces = []
        for step in steps if parts else ():
            first, _, unit = owned_at(peers[step])
            held = [
                lax.dynamic_slice(
                    all_weights[which], (first + e, 0, unit), (1, rows_local, unit_count)
                )
                for which, e in parts
            ]
            pieces.append(jnp.concatenate(held))
        return pieces

    def to_owner(parts, pieces, *earlier):
        pieces = after(pieces, *earlier)
        pieces = [
            None if step == 1 else trade(pieces[step], step, n_row) for step in steps
        ]
        pieces[1] = jnp.stack([near_pieces[all_parts.index(part)] for part in parts])
        for i, (which, e) in enumerate(parts):
            for step in steps:
                at = (peers[step] * rows_local, unit_count if which == 1 else 0)
                if which < 2:
                    w_in[e] = lax.dynamic_update_slice(w_in[e], pieces[step][i], at)
                else:
                    w_back[e] = lax.dynamic_update_slice(w_back[e], pieces[step][i], at)
        return pieces

    def tied(value):
        value, w_in[:], w_back[:] = lax.optimization_barrier((value, w_in[:], w_back[:]))
        return value

    first_parts, second_parts = all_parts[:per_device], all_parts[per_device : per_device + 1]
    third_parts = all_parts[per_device + 1 : 2 * per_device + 1]
    last_parts = all_parts[2 * per_device + 1 :]
    near_pieces = trade(slices(all_parts)[1], 1, n_row)
    first_pieces = to_owner(first_parts, slices(first_parts))
    second_pieces = after(slices(second_parts), *w_in)
    later = [slices(parts) for parts in (third_parts, last_parts)]
    far_bases = far[::2]
    gathered, second_pieces, later, cot_b, inverse, near_pieces = tied(
        (gathered, second_pieces, later, cot_b, inverse, near_pieces)
    )
    gains = gathered[tok_count : tok_count + 6].astype(F32).reshape(2, 3, D).sum(axis=1)

    expert_ids = jnp.arange(E, dtype=jnp.int32)
    routes_t = routes.T
    chosen = jnp.any(routes_t[None] == expert_ids[:, None, None], axis=1)
    own_ids = col * local_experts + jnp.arange(local_experts, dtype=jnp.int32)
    own_chosen = jnp.any(routes_t[None] == own_ids[:, None, None], axis=1)
    earlier = (places[:, None] < places[None, :]).astype(BF16)
    rank = plain_dot(own_chosen.astype(BF16), earlier).astype(jnp.int32)
    slot_rank = jnp.where(own_chosen, rank, -1)
    slots = jnp.arange(capacity, dtype=jnp.int32)

    def of_peer(table, step, e):
        return lax.dynamic_slice_in_dim(table, owned_at(peers[step])[0] + e, 1, 0)

    hits = [
        [of_peer(slot_rank, step, e) == slots[:, None] for step in steps]
        for e in range(per_device)
    ]
    picks = [[hit.astype(BF16) for hit in hits[e]] for e in range(per_device)]

    far_ranks = {base: trade(slot_rank.astype(F32), base, n_row) for base in far_bases}

    def swap_small(pieces):
        table = jnp.zeros((n_row,) + pieces[0].shape, pieces[0].dtype)
        for step in steps:
            table = jnp.where(
                jnp.arange(n_row).reshape((-1,) + (1,) * pieces[0].ndim) == peers[step],
                pieces[step][None],
                table,
            )
        table = lax.all_to_all(table, "row", 0, 0, tiled=True)
        return [lax.dynamic_index_in_dim(table, peers[step], 0, False) for step in steps]

    cosine, sine = rope_tables(position)
    q_gain, k_gain = query_gain[None], key_gain[None]
    normed1, scale_in, raw_qk, query_rot, key_rot, values_b = project(
        gathered, gains[:1], weight_heads, q_gain, k_gain, cosine, sine, width_local
    )
    seg_q, seg_k = segment[:, None], jnp.where(key_mask == 1, segment, -1)[None]
    attended_b, log_totals = attend(query_rot, key_rot, values_b, seg_q, seg_k)

    half = D // 2
    out_half = lax.dynamic_slice_in_dim(w_out_own, core * half, half, 0)
    out_half_all = gather_features(after(out_half, *first_pieces[:-1]))

    to_owner(second_parts, second_pieces)
    far_cots = [trade(cot_b, base, n_row) for base in far_bases]
    attended_b = tied(attended_b)
    attended_all = gather_features(after(attended_b, out_half_all))
    third_pieces = to_owner(third_parts, later[0], attended_b, far_cots)
    other_half = trade(after(out_half_all, *w_back), 1, n_row)
    cot_alls = {
        base: gather_features(after(cot, third_pieces[2])) for base, cot in zip(far_bases, far_cots)
    }
    attended_all = tied(attended_all)
    if last_parts:
        to_owner(last_parts, later[1], w_back[0])
    normed2, scale_mid, mixed = run_branch(
        core, col, gathered, attended_all, out_half_all, other_half, gains[1:], feat_local
    )
    cot_alls[0] = gather_features(after(cot_b, normed2))
    normed2 = tied(normed2)
    column_start = col * feat_local

    def chosen_rows(e, values):
        return [plain_dot(picks[e][step], values, BF16) for step in steps]

    sent_rows = []
    for e in range(per_device):
        sent_rows.append(chosen_rows(e, after(normed2, sent_rows)))
    all_rows = [trade_all(pieces) for pieces in sent_rows]

    def grad_rows_of(base, cots):
        table = far_ranks[base] if base else slot_rank.astype(F32)
        halves = []
        for step in near:
            held = []
            for e in range(per_device):
                pick = (of_peer(table, step, e) == slots[:, None].astype(F32)).astype(BF16)
                held.append(plain_dot(pick, cots, BF16))
            halves.append(jnp.stack(held))
        return halves

    grad_rows_at = {}

    def hand_on(base, halves):
        grad_rows_at[base], grad_rows_at[base + 1] = halves[0], trade(halves[1], 1, n_row)

    for base in far_bases:
        hand_on(base, grad_rows_of(base, after(cot_alls[base], sent_rows, all_rows[0])))

    logits = lax.dot_general(
        router_all, after(normed2, sent_rows), (((0,), (1,)), ((), ())), preferred_element_type=F32
    )
    top_logit = jnp.max(jnp.where(chosen, logits, -jnp.inf), axis=0, keepdims=True)
    raised = jnp.where(chosen, jnp.exp(logits - top_logit), 0.0)
    gate_probs = raised / jnp.sum(raised, axis=0, keepdims=True)
    own_probs = lax.dynamic_slice_in_dim(gate_probs, col * local_experts, local_experts, 0)

    slot_gates = []
    for step in steps:
        held = [
            jnp.sum(jnp.where(hits[e][step], of_peer(own_probs, step, e), 0.0), axis=1)
            for e in range(per_device)
        ]
        slot_gates.append(jnp.stack(held))
    slot_gates = swap_small(slot_gates)

    both = range(per_device)
    calls, grads_back = {}, [[None] * n_row for e in range(per_device)]

    def rows_and_gates(e, held):
        rows = jnp.concatenate([all_rows[e][step] for step in held])
        return rows, jnp.concatenate([slot_gates[step][e] for step in held])[:, None]

    def expert_call(e, held, rows, slot_gate, pre=None):
        grad_rows = jnp.concatenate([grad_rows_at[step][e] for step in held])
        first = rows if pre is None else pre
        results = run_expert(first, grad_rows, slot_gate, w_in[e], w_back[e], 2 * capacity)
        calls[e, held[0]] = [rows, grad_rows, *results]

    def send_back(e, held):
        grads = calls[e, held[0]][-1]
        for i, step in enumerate(held):
            piece = grads[i * capacity : (i + 1) * capacity]
            grads_back[e][step] = trade(piece, step, n_row)

    expert_call(0, far, *rows_and_gates(0, far))
    send_back(0, far)
    for e in range(1, per_device):
        all_rows[e] = after(all_rows[e], calls[0, 2])
        expert_call(e, far, *rows_and_gates(e, far))
    near_inputs = [rows_and_gates(e, near) for e in both]
    near_inputs = [(*held, plain_dot(held[0], w_in[e])) for e, held in enumerate(near_inputs)]
    near_cots, near_inputs, _ = lax.optimization_barrier(
        (cot_alls[0], near_inputs, [calls[e, 2] for e in both])
    )
    near_halves = grad_rows_of(0, near_cots)
    for e in range(1, per_device):
        calls[e, 2], grads_back[e - 1], near_halves = lax.optimization_barrier(
            (calls[e, 2], grads_back[e - 1], near_halves)
        )
        send_back(e, far)
    hand_on(0, near_halves)
    for e in range(per_device):
        expert_call(e, near, *near_inputs[e])
        send_back(e, near)
    last_near = (per_device - 1, 0)
    calls[last_near], grads_back[-1] = lax.optimization_barrier((calls[last_near], grads_back[-1]))
    scalars = [jnp.concatenate([calls[e, 0][4], calls[e, 2][4]]) for e in range(per_device)]
    scalars = jnp.stack(scalars)
    scalars_back = swap_small(
        [scalars[:, step * capacity : (step + 1) * capacity] for step in steps]
    )
    every = [(e, step) for e in range(per_device) for step in steps]
    ranks = jnp.concatenate([of_peer(slot_rank, step, e) for e, step in every])
    grad_normed2_part = combine(ranks, [grads_back[e][step] for e, step in every])

    calls = after(calls, grad_normed2_part)
    branch_back, weight_grads = [], []
    for e in range(per_device):
        rows, grad_rows, act, grad_pre = (
            jnp.concatenate([calls[e, 0][i], calls[e, 2][i]]) for i in range(4)
        )
        out = contract_last(act, w_back[e], BF16)
        branch_back.append(
            trade_all([out[step * capacity : (step + 1) * capacity] for step in steps])
        )
        grad_in = contract_first(rows, grad_pre, BF16)
        weight_grads.append(
            (
                grad_in[:, :unit_count],
                grad_in[:, unit_count:],
                contract_first(grad_rows, act, BF16),
            )
        )
    grad_normed2 = scatter_partial(grad_normed2_part).astype(F32)

    grad_own = jnp.zeros((local_experts, tok_count), F32)
    inner_own = jnp.zeros((1, tok_count), F32)
    own_rows = jnp.arange(local_experts, dtype=jnp.int32)[:, None]
    for e in range(per_device):
        for step in steps:
            expert = owned_at(peers[step])[0] + e
            back = scalars_back[step][e]
            spread = jnp.sum(jnp.where(hits[e][step], back[:, :1], 0.0), axis=0, keepdims=True)
            grad_own = grad_own + jnp.where(own_rows == expert, spread, 0.0)
            inner_own = inner_own + jnp.sum(
                jnp.where(hits[e][step], back[:, 1:], 0.0), axis=0, keepdims=True
            )
    small = jnp.concatenate([grad_own, inner_own], axis=0)
    small, branch_back[0] = lax.optimization_barrier((small, branch_back[0]))
    small = lax.all_to_all(
        jnp.broadcast_to(small.astype(BF16)[None], (n_col,) + small.shape), "col", 0, 0, tiled=True
    )
    small, branch_back = lax.optimization_barrier((small, branch_back))
    small = small.astype(F32)
    grad_gates = small[:, :local_experts].reshape(E, tok_count)
    grad_logits = gate_probs * (
        grad_gates - jnp.sum(gate_probs * grad_gates, axis=0, keepdims=True)
    )
    grad_logits = grad_logits.astype(BF16)
    inner_mid = jnp.sum(small[:, local_experts], axis=0) + jnp.sum(
        grad_logits.astype(F32) * logits, axis=0
    )
    inner_mid = (inner_mid / D)[:, None]
    grad_router = lax.dot_general(
        normed2, grad_logits, (((0,), (1,)), ((), ())), preferred_element_type=F32
    )
    router_local = lax.dynamic_slice_in_dim(router_all, column_start, feat_local, 0)
    grad_unit_mid = grad_normed2 + lax.dot_general(
        grad_logits, router_local, (((0,), (1,)), ((), ())), preferred_element_type=F32
    )
    unit_mid = mixed * scale_mid
    grad_norm2 = jnp.sum(grad_unit_mid * unit_mid, axis=0)
    scaled_mid = grad_unit_mid * norm2_gain
    grad_mixed = cot_b.astype(F32) + scale_mid * (scaled_mid - unit_mid * inner_mid)
    def held_slices(which, experts):
        return [
            jnp.stack(
                [
                    lax.dynamic_slice_in_dim(
                        weight_grads[e][which], peers[step] * rows_local, rows_local, 0
                    )
                    for e in experts
                ]
            )
            for step in steps
        ]

    def to_holders(pieces, *earlier):
        return trade_all(after(pieces, *earlier))

    gate_slices, up_slices = held_slices(0, both), held_slices(1, both)
    grad_mixed_b, gate_slices, up_slices = lax.optimization_barrier(
        (grad_mixed.astype(BF16), gate_slices, up_slices)
    )
    grad_branch = gather_features(grad_mixed_b)
    gate_pieces = to_holders(gate_slices)

    def to_rows(pieces):
        flat, places = [], []
        for e, held in enumerate(pieces):
            for step in steps:
                first, _, unit = owned_at(peers[step])
                flat.append(held[step])
                places += [first + e, unit]
        return place(jnp.stack(places), flat, local_experts, hidden_units)

    def sum_cores(grad):
        parts = [
            lax.dynamic_slice_in_dim(grad, peers[step] * rows_local, rows_local, 0)
            for step in steps
        ]
        other = trade(jnp.stack(parts[1::2]), 1, n_row).astype(F32)
        sums = [part.astype(F32) + other[i] for i, part in enumerate(parts[::2])]
        return [sums[0]] + [part.astype(grad.dtype) for part in sums[1:]]

    def sum_chips(sums):
        total = sums[0]
        for part, base in zip(sums[1:], far_bases):
            total = total + trade(part, base, n_row).astype(F32)
        return total

    def sum_groups(grad, *earlier):
        return sum_chips(sum_cores(after(grad, *earlier)))

    combined_part = combine(ranks, [branch_back[e][step] for e, step in every])
    grad_branch, gate_pieces, combined_part = lax.optimization_barrier(
        (grad_branch, gate_pieces, combined_part)
    )
    up_pieces = to_holders(up_slices, gate_pieces)

    combined = scatter_partial(combined_part)

    grad_w_out = contract_first(grad_branch, attended_b, BF16)
    grad_w_gate = to_rows([gate_pieces])
    grad_attended = plain_dot(after(grad_branch, grad_w_gate), w_out_own, BF16)
    grad_q, grad_k, grad_v, grad_query_gain, grad_key_gain = attend_back(
        query_rot, key_rot, values_b, grad_attended, log_totals, seg_q, seg_k, raw_qk,
        q_gain, k_gain, cosine, sine,
    )
    grad_qkv = jnp.concatenate([grad_q, grad_k, grad_v], axis=1)
    grad_w_out = sum_groups(grad_w_out)
    grad_router = sum_groups(grad_router, grad_branch).T
    down_slices = [held_slices(2, [e]) for e in range(per_device)]
    grad_qkv, up_pieces, combined, down_slices, grad_w_out, grad_router = (
        lax.optimization_barrier(
            (grad_qkv, up_pieces, combined, down_slices, grad_w_out, grad_router)
        )
    )
    down_pieces = [to_holders(down_slices[0])]
    grad_normed1_part = through_heads(grad_qkv, weight_heads)
    grad_unit_in = scatter_partial(grad_normed1_part)
    output = (mixed + combined.astype(F32)).astype(BF16)[inverse]
    grad_w_up = to_rows([up_pieces])
    grad_normed1_part, down_pieces, output, grad_w_up = lax.optimization_barrier(
        (grad_normed1_part, down_pieces, output, grad_w_up)
    )
    down_pieces += [to_holders(held, down_pieces) for held in down_slices[1:]]
    inner_in = jnp.sum(
        grad_qkv.astype(F32) * jnp.concatenate([raw_qk, values_b.astype(F32)], axis=1), axis=1
    )
    packed = packed_b.astype(F32)
    unit_in = packed * scale_in
    unit_all = gathered[:tok_count].astype(F32) * scale_in
    grad_norm1 = jnp.sum(grad_normed1_part.astype(F32) * unit_all, axis=0)
    def for_all(vector):
        return jnp.broadcast_to(vector[None], (n_col,) + vector.shape)

    vectors = jnp.concatenate(
        [
            for_all(inner_in),
            for_all(grad_query_gain[0]),
            for_all(grad_key_gain[0]),
            grad_norm1.reshape(n_col, feat_local),
        ],
        axis=1,
    )
    heads_sums = sum_cores(contract_first(normed1, grad_qkv, BF16))
    vectors, heads_sums = lax.optimization_barrier((vectors, heads_sums))
    vectors = jnp.sum(lax.all_to_all(vectors, "col", 0, 0, tiled=True), axis=0)
    vectors, down_pieces, heads_sums = lax.optimization_barrier(
        (vectors, down_pieces, heads_sums)
    )
    inner_in = vectors[:tok_count, None] / D
    vectors = jnp.concatenate([vectors[tok_count:], grad_norm2])
    vectors = sum(trade(vectors, step, n_row) for step in steps)
    grad_heads = sum_chips(heads_sums)
    grad_unit_in, vectors, inner_in, grad_heads = lax.optimization_barrier(
        (grad_unit_in, vectors, inner_in, grad_heads)
    )
    grad_unit_in = grad_unit_in.astype(F32)
    scaled_in = grad_unit_in * norm1_gain
    grad_input = (grad_mixed + scale_in * (scaled_in - unit_in * inner_in))[inverse]

    grad_w_query, grad_w_key, grad_w_value = (
        grad_heads[:, i * width_local : (i + 1) * width_local] for i in range(3)
    )
    grad_w_down = to_rows(down_pieces)

    grad_query_gain, grad_key_gain = vectors[:DH], vectors[DH : 2 * DH]
    grad_norm1 = vectors[2 * DH : 2 * DH + feat_local]
    grad_norm2 = vectors[2 * DH + feat_local :]
    return (
        output,
        grad_input,
        grad_norm1,
        grad_query_gain,
        grad_key_gain,
        grad_w_query,
        grad_w_key,
        grad_w_value,
        grad_w_out,
        grad_norm2,
        grad_router,
        grad_w_gate,
        grad_w_up,
        grad_w_down,
    )


def solution(mesh):
    return jax.shard_map(
        body,
        mesh=mesh,
        in_specs=(
            P("row", "col"),
            P("row", None),
            P("row", None),
            P("row"),
            P("row", None),
            P("col"),
            P(),
            P(),
            P("row", "col"),
            P("row", "col"),
            P("row", "col"),
            P("row", "col"),
            P("col"),
            P(None, "row"),
            P("col", "row", None),
            P("col", "row", None),
            P("col", "row", None),
            P("row", "col"),
        ),
        out_specs=(
            P("row", "col"),
            P("row", "col"),
            P("col"),
            P(),
            P(),
            P("row", "col"),
            P("row", "col"),
            P("row", "col"),
            P("row", "col"),
            P("col"),
            P(None, "row"),
            P("col", "row", None),
            P("col", "row", None),
            P("col", "row", None),
        ),
        check_vma=False,
    )
```

```python
import jax
import jax.numpy as jnp
from jax import lax
from jax.experimental import pallas as pl
from jax.experimental.pallas import tpu as pltpu
from jax.sharding import PartitionSpec as P

D = 2048
DH = 128
E = 64
TOP = 8


EPSILON = 1e-06
ROPE_BASE = 10000.0
BF16 = jnp.bfloat16
F32 = jnp.float32


def layout(seq_lengths, tok_count):
    seq_ends = jnp.cumsum(seq_lengths)
    seq_starts = seq_ends - seq_lengths
    places = jnp.arange(tok_count, dtype=jnp.int32)
    segment = jnp.sum((places[:, None] >= seq_ends[None, :]).astype(jnp.int32), axis=1)
    member = segment[:, None] == jnp.arange(seq_lengths.shape[0], dtype=jnp.int32)[None, :]
    offset = jnp.sum(jnp.where(member, seq_starts[None, :], 0), axis=1)
    return (segment, places - offset)


def rope_tables(position):
    half_dim = DH // 2
    frequency = ROPE_BASE ** (-2.0 * jnp.arange(half_dim, dtype=F32) / DH)
    angles = position.astype(F32)[:, None] * frequency[None, :]
    cosine, sine = jnp.cos(angles), jnp.sin(angles)
    return jnp.concatenate([cosine, cosine], 1), jnp.concatenate([-sine, sine], 1)


def gather_features(local_rows):
    return lax.all_gather(local_rows, "col", axis=1, tiled=True)


def scatter_partial(partial_rows):
    return lax.psum_scatter(partial_rows, "col", scatter_dimension=1, tiled=True)


def trade(value, step, n_row):
    if step == 0:
        return value
    return lax.ppermute(value, "row", [(r, r ^ step) for r in range(n_row)])


def trade_all(pieces):
    return [trade(piece, step, len(pieces)) for step, piece in enumerate(pieces)]


def contract_last(left_op, right_op, kind=F32):
    return lax.dot_general(
        left_op, right_op, (((1,), (1,)), ((), ())), preferred_element_type=F32
    ).astype(kind)


def contract_first(left_op, right_op, kind=F32):
    return lax.dot_general(
        left_op, right_op, (((0,), (0,)), ((), ())), preferred_element_type=F32
    ).astype(kind)


def plain_dot(left_op, right_op, kind=F32):
    return jnp.dot(left_op, right_op, preferred_element_type=F32).astype(kind)


def after(value, *earlier):
    return lax.optimization_barrier((value, *earlier))[0]


def thirds(values):
    high = lax.reduce_precision(values, 8, 7)
    middle = lax.reduce_precision(values - high, 8, 7)
    return jnp.stack([high, middle, values - high - middle]).astype(BF16)


def cost(flops, moved):
    return pl.CostEstimate(flops=flops, bytes_accessed=moved, transcendentals=0)


def rope(values, cosine, sine):
    return values * cosine + pltpu.roll(values, DH // 2, 1) * sine


def rope_back(grad, cosine, sine):
    return grad * cosine + pltpu.roll(grad * sine, DH // 2, 1)


def project_kernel(x_ref, gain_ref, w_ref, qg_ref, kg_ref, cos_ref, sin_ref, *outs):
    normed_ref, scale_ref, raw_ref, q_ref, k_ref, v_ref = outs
    x = x_ref[...].astype(F32)
    scale = lax.rsqrt(jnp.mean(x * x, axis=1, keepdims=True) + EPSILON)
    normed = (x * scale * gain_ref[...]).astype(BF16)
    normed_ref[...] = normed
    scale_ref[...] = scale
    width = q_ref.shape[1]
    qkv = jnp.dot(normed, w_ref[:, : 3 * width], preferred_element_type=F32)
    raw_ref[...] = qkv[:, : 2 * width]
    v_ref[...] = qkv[:, 2 * width :].astype(BF16)
    cosine, sine = cos_ref[...], sin_ref[...]
    for part, gain, out in ((0, qg_ref, q_ref), (1, kg_ref, k_ref)):
        for h in range(width // DH):
            head = qkv[:, part * width + h * DH : part * width + (h + 1) * DH]
            size = lax.rsqrt(jnp.mean(head * head, axis=1, keepdims=True) + EPSILON)
            out[:, h * DH : (h + 1) * DH] = rope(head * size * gain[...], cosine, sine).astype(BF16)


def project(x, gain, w, q_gain, k_gain, cosine, sine, width, block=256):
    rows = cosine.shape[0]
    by_rows = lambda n: pl.BlockSpec((block, n), lambda i: (i, 0))
    whole = lambda a: pl.BlockSpec(a.shape, lambda i: (0, 0))
    return pl.pallas_call(
        project_kernel,
        name="project",
        grid=(rows // block,),
        in_specs=[
            by_rows(D),
            whole(gain),
            whole(w),
            whole(q_gain),
            whole(k_gain),
            by_rows(DH),
            by_rows(DH),
        ],
        out_specs=[by_rows(n) for n in (D, 1, 2 * width, width, width, width)],
        out_shape=[
            jax.ShapeDtypeStruct((rows, D), BF16),
            jax.ShapeDtypeStruct((rows, 1), F32),
            jax.ShapeDtypeStruct((rows, 2 * width), F32),
            jax.ShapeDtypeStruct((rows, width), BF16),
            jax.ShapeDtypeStruct((rows, width), BF16),
            jax.ShapeDtypeStruct((rows, width), BF16),
        ],
        cost_estimate=cost(1000, 1000),
    )(x, gain, w, q_gain, k_gain, cosine, sine)


def masked_scores(q, k, seg_q, seg_k, first):
    scores = lax.dot_general(q, k, (((1,), (1,)), ((), ())), preferred_element_type=F32)
    rows = first + lax.broadcasted_iota(jnp.int32, scores.shape, 0)
    columns = lax.broadcasted_iota(jnp.int32, scores.shape, 1)
    allowed = (seg_q == seg_k) | (rows == columns)
    return jnp.where(allowed, scores * DH ** (-0.5), -1e30)


def attend_kernel(q_ref, k_ref, v_ref, seg_q_ref, seg_k_ref, out_ref, log_ref):
    first = pl.program_id(1) * q_ref.shape[0]
    scores = masked_scores(q_ref[...], k_ref[...], seg_q_ref[...], seg_k_ref[...], first)
    top = jnp.max(scores, axis=1, keepdims=True)
    terms = jnp.exp(scores - top)
    total = jnp.sum(terms, axis=1, keepdims=True)
    weights = (terms * (1.0 / total)).astype(BF16)
    out_ref[...] = jnp.dot(weights, v_ref[...], preferred_element_type=F32).astype(BF16)
    log_ref[0] = top + jnp.log(total)


def attend(q, k, v, seg_q, seg_k, block=256):
    rows, width = q.shape
    heads = width // DH
    by_rows = pl.BlockSpec((block, DH), lambda h, i: (i, h))
    whole = pl.BlockSpec((rows, DH), lambda h, i: (0, h))
    return pl.pallas_call(
        attend_kernel,
        name="attend",
        grid=(heads, rows // block),
        in_specs=[
            by_rows,
            whole,
            whole,
            pl.BlockSpec((block, 1), lambda h, i: (i, 0)),
            pl.BlockSpec((1, rows), lambda h, i: (0, 0)),
        ],
        out_specs=[by_rows, pl.BlockSpec((1, block, 1), lambda h, i: (h, i, 0))],
        out_shape=[
            jax.ShapeDtypeStruct((rows, width), BF16),
            jax.ShapeDtypeStruct((heads, rows, 1), F32),
        ],
        cost_estimate=cost(1000, 1000),
    )(q, k, v, seg_q, seg_k)


def head_back(grad, raw, gain, cosine, sine):
    grad = rope_back(grad, cosine, sine)
    size = lax.rsqrt(jnp.mean(raw * raw, axis=1, keepdims=True) + EPSILON)
    unit = raw * size
    grad_gain = jnp.sum(grad * unit, axis=0, keepdims=True)
    grad = grad * gain
    return size * (grad - unit * jnp.mean(grad * unit, axis=1, keepdims=True)), grad_gain


def attend_back_kernel(
    q_ref, k_ref, v_ref, grad_ref, log_ref, seg_q_ref, seg_k_ref, raw_q_ref, raw_k_ref,
    qg_ref, kg_ref, cos_q_ref, sin_q_ref, cos_ref, sin_ref,
    dq_ref, dk_ref, dv_ref, dqg_ref, dkg_ref, sum_k, sum_v,
):
    head, i = pl.program_id(0), pl.program_id(1)

    @pl.when((head == 0) & (i == 0))
    def _():
        dqg_ref[...] = jnp.zeros_like(dqg_ref)
        dkg_ref[...] = jnp.zeros_like(dkg_ref)

    @pl.when(i == 0)
    def _():
        sum_k[...] = jnp.zeros_like(sum_k)
        sum_v[...] = jnp.zeros_like(sum_v)

    q, k, grad = q_ref[...], k_ref[...], grad_ref[...]
    scores = masked_scores(q, k, seg_q_ref[...], seg_k_ref[...], i * q.shape[0])
    probs = jnp.exp(scores - log_ref[0])
    sum_v[...] += lax.dot_general(
        probs.astype(BF16), grad, (((0,), (0,)), ((), ())), preferred_element_type=F32
    )
    grad_probs = lax.dot_general(
        grad, v_ref[...], (((1,), (1,)), ((), ())), preferred_element_type=F32
    )
    inner = jnp.sum(probs * grad_probs, axis=1, keepdims=True)
    grad_scores = (probs * (grad_probs - inner)).astype(BF16)
    sum_k[...] += lax.dot_general(
        grad_scores, q, (((0,), (0,)), ((), ())), preferred_element_type=F32
    )
    grad_q = jnp.dot(grad_scores, k, preferred_element_type=F32) * DH ** (-0.5)
    grad_q, grad_gain = head_back(
        grad_q, raw_q_ref[...], qg_ref[...], cos_q_ref[...], sin_q_ref[...]
    )
    dq_ref[...] = grad_q.astype(BF16)
    dqg_ref[...] += grad_gain

    @pl.when(i == pl.num_programs(1) - 1)
    def _():
        grad_k, gain_k = head_back(
            sum_k[...] * DH ** (-0.5), raw_k_ref[...], kg_ref[...], cos_ref[...], sin_ref[...]
        )
        dk_ref[...] = grad_k.astype(BF16)
        dkg_ref[...] += gain_k
        dv_ref[...] = sum_v[...].astype(BF16)


def attend_back(q, k, v, grad, logs, seg_q, seg_k, raw, q_gain, k_gain, cosine, sine, block=256):
    rows, width = q.shape
    heads = width // DH
    by_rows = pl.BlockSpec((block, DH), lambda h, i: (i, h))
    whole = pl.BlockSpec((rows, DH), lambda h, i: (0, h))
    gain = pl.BlockSpec((1, DH), lambda h, i: (0, 0))
    return pl.pallas_call(
        attend_back_kernel,
        name="attend_back",
        grid=(heads, rows // block),
        in_specs=[
            by_rows,
            whole,
            whole,
            by_rows,
            pl.BlockSpec((1, block, 1), lambda h, i: (h, i, 0)),
            pl.BlockSpec((block, 1), lambda h, i: (i, 0)),
            pl.BlockSpec((1, rows), lambda h, i: (0, 0)),
            by_rows,
            pl.BlockSpec((rows, DH), lambda h, i: (0, heads + h)),
            gain,
            gain,
            pl.BlockSpec((block, DH), lambda h, i: (i, 0)),
            pl.BlockSpec((block, DH), lambda h, i: (i, 0)),
            pl.BlockSpec((rows, DH), lambda h, i: (0, 0)),
            pl.BlockSpec((rows, DH), lambda h, i: (0, 0)),
        ],
        out_specs=[by_rows, whole, whole, gain, gain],
        out_shape=[
            jax.ShapeDtypeStruct((rows, width), BF16),
            jax.ShapeDtypeStruct((rows, width), BF16),
            jax.ShapeDtypeStruct((rows, width), BF16),
            jax.ShapeDtypeStruct((1, DH), F32),
            jax.ShapeDtypeStruct((1, DH), F32),
        ],
        scratch_shapes=[pltpu.VMEM((rows, DH), F32), pltpu.VMEM((rows, DH), F32)],
        cost_estimate=cost(1000, 1000),
    )(q, k, v, grad, logs, seg_q, seg_k, raw, raw, q_gain, k_gain, cosine, sine, cosine, sine)


def branch_kernel(
    at_ref, x_ref, att_ref, own_ref, other_ref, gain_ref, normed_ref, scale_ref, mixed_ref, total
):
    half = own_ref.shape[0]
    own = contract_last(att_ref[...], own_ref[...])
    other = contract_last(att_ref[...], other_ref[...])
    second = at_ref[0] == 1
    total[:, :half] = x_ref[:, :half].astype(F32) + jnp.where(second, other, own)
    total[:, half:] = x_ref[:, half:].astype(F32) + jnp.where(second, own, other)
    mixed = total[...]
    scale = lax.rsqrt(jnp.mean(mixed * mixed, axis=1, keepdims=True) + EPSILON)
    normed_ref[...] = (mixed * scale * gain_ref[...]).astype(BF16)
    scale_ref[...] = scale
    width = mixed_ref.shape[1]
    mixed_ref[...] = total[:, pl.ds(pl.multiple_of(at_ref[1] * width, 128), width)]


def run_branch(core, col, x, attended, own, other, gain, width, block=256):
    rows = attended.shape[0]
    by_rows = lambda n: pl.BlockSpec((block, n), lambda i, at: (i, 0))
    whole = lambda a: pl.BlockSpec(a.shape, lambda i, at: (0, 0))
    return pl.pallas_call(
        branch_kernel,
        name="branch",
        grid_spec=pltpu.PrefetchScalarGridSpec(
            num_scalar_prefetch=1,
            grid=(rows // block,),
            in_specs=[by_rows(D), by_rows(D), whole(own), whole(other), whole(gain)],
            out_specs=[by_rows(D), by_rows(1), by_rows(width)],
            scratch_shapes=[pltpu.VMEM((block, D), F32)],
        ),
        out_shape=[
            jax.ShapeDtypeStruct((rows, D), BF16),
            jax.ShapeDtypeStruct((rows, 1), F32),
            jax.ShapeDtypeStruct((rows, width), F32),
        ],
        cost_estimate=cost(1000, 1000),
    )(jnp.stack([core, col]), x, attended, own, other, gain)


def expert_kernel(
    x0_ref, x1_ref, c0_ref, c1_ref, gate_ref, w_ref, wd_ref,
    act_ref, grad_ref, sums_ref, dx0_ref, dx1_ref,
):
    width = act_ref.shape[1]
    slot_gate = gate_ref[...]
    rows = jnp.concatenate([x0_ref[...], x1_ref[...]], axis=0)
    pre = jnp.dot(rows, w_ref[...], preferred_element_type=F32)
    gate, up = pre[:, :width], pre[:, width:]
    cots = jnp.concatenate([c0_ref[...], c1_ref[...]], axis=0)
    grad = jnp.dot(cots, wd_ref[...], preferred_element_type=F32)
    opened = 1.0 / (1.0 + jnp.exp(-gate))
    silu = gate * opened
    act = silu * up
    act_ref[...] = (slot_gate * act).astype(BF16)
    grad_gate = jnp.sum(act * grad, axis=1, keepdims=True)
    grad = slot_gate * grad
    dgate = (grad * up * opened * (1.0 + gate * (1.0 - opened))).astype(BF16)
    dup = (grad * silu).astype(BF16)
    grad_ref[:, :width] = dgate
    grad_ref[:, width:] = dup
    inner = jnp.sum(dgate.astype(F32) * gate + dup.astype(F32) * up, axis=1, keepdims=True)
    sums_ref[:, 0:1] = grad_gate
    sums_ref[:, 1:2] = inner
    back = contract_last(grad_ref[...], w_ref[...], BF16)
    dx0_ref[...] = back[: dx0_ref.shape[0]]
    dx1_ref[...] = back[dx0_ref.shape[0] :]


def run_expert(xs, cs, slot_gate, w, wd):
    capacity, width = xs[0].shape[0], wd.shape[1]
    slots = 2 * capacity
    operands = [*xs, *cs, slot_gate, w, wd]
    outs = [(slots, width, BF16), (slots, 2 * width, BF16), (slots, 2, F32)]
    outs += [(capacity, D, BF16)] * 2
    whole = lambda shape: pl.BlockSpec(shape, lambda i: (0, 0), pipeline_mode=pl.Buffered(1))
    return pl.pallas_call(
        expert_kernel,
        name="expert",
        grid=(1,),
        in_specs=[whole(a.shape) for a in operands],
        out_specs=[pl.BlockSpec(out[:2], lambda i: (0, 0)) for out in outs],
        out_shape=[jax.ShapeDtypeStruct(out[:2], out[2]) for out in outs],
        cost_estimate=cost(1000, 1000),
    )(*operands)


def through_heads_kernel(grad_ref, w_ref, out_ref):
    width = grad_ref.shape[1]
    out_ref[...] = contract_last(grad_ref[...], w_ref[:, :width], BF16)


def through_heads(grad, w, block=256):
    rows, width = grad.shape
    return pl.pallas_call(
        through_heads_kernel,
        name="through_heads",
        grid=(rows // block,),
        in_specs=[
            pl.BlockSpec((block, width), lambda i: (i, 0)),
            pl.BlockSpec(w.shape, lambda i: (0, 0)),
        ],
        out_specs=pl.BlockSpec((block, D), lambda i: (i, 0)),
        out_shape=jax.ShapeDtypeStruct((rows, D), BF16),
        cost_estimate=cost(1000, 1000),
    )(grad, w)


def combine_kernel(*refs):
    rank_ref, out_ref = refs[0], refs[-1]
    pieces = refs[1:-1]
    total = 0.0
    for i, piece in enumerate(pieces):
        shape = (piece.shape[0], out_ref.shape[0])
        slots = lax.broadcasted_iota(jnp.int32, shape, 0)
        hits = (slots == rank_ref[i : i + 1, :]).astype(BF16)
        total = total + contract_first(hits, piece[...])
    out_ref[...] = total.astype(BF16)


def combine(ranks, pieces, block=256):
    rows = ranks.shape[1]
    width = 1024
    whole = lambda a: pl.BlockSpec((a.shape[0], width), lambda j, i: (0, j))
    return pl.pallas_call(
        combine_kernel,
        name="combine",
        grid=(D // width, rows // block),
        in_specs=[pl.BlockSpec((len(pieces), block), lambda j, i: (0, i))]
        + [whole(piece) for piece in pieces],
        out_specs=pl.BlockSpec((block, width), lambda j, i: (i, j)),
        out_shape=jax.ShapeDtypeStruct((rows, D), BF16),
        cost_estimate=cost(1000, 1000),
    )(ranks, *pieces)


def place_kernel(at_ref, *refs):
    out_ref = refs[-1]
    for i, piece in enumerate(refs[:-1]):
        experts, _, units = piece.shape
        first, unit = at_ref[2 * i], pl.multiple_of(at_ref[2 * i + 1], 128)
        for e in range(experts):
            out_ref[first + e, :, pl.ds(unit, units)] = piece[e].astype(F32)


def place(places, pieces, experts, units, block=64):
    rows = pieces[0].shape[1]
    spec = lambda a: pl.BlockSpec((a.shape[0], block, a.shape[2]), lambda i, at: (0, i, 0))
    return pl.pallas_call(
        place_kernel,
        name="place",
        grid_spec=pltpu.PrefetchScalarGridSpec(
            num_scalar_prefetch=1,
            grid=(rows // block,),
            in_specs=[spec(piece) for piece in pieces],
            out_specs=pl.BlockSpec((experts, block, units), lambda i, at: (0, i, 0)),
        ),
        out_shape=jax.ShapeDtypeStruct((experts, rows, units), F32),
        cost_estimate=cost(1000, 1000),
    )(places, *pieces)


def body(
    hidden_in,
    token_order,
    lengths,
    key_mask,
    routes,
    norm1_gain,
    query_gain,
    key_gain,
    w_query,
    w_key,
    w_value,
    w_out,
    norm2_gain,
    router,
    w_gate,
    w_up,
    w_down,
    cotangent,
):
    tok_count, feat_local = hidden_in.shape
    n_row = D // w_query.shape[0]
    n_col = D // feat_local
    local_experts, _, hidden_units = w_gate.shape
    per_device = max(1, local_experts // n_row)
    unit_split = max(1, n_row // local_experts)
    capacity = 5 * tok_count * TOP // (4 * E)
    col = lax.axis_index("col")
    row = lax.axis_index("row")
    core = row % 2
    steps = range(n_row)
    peers = [row ^ step for step in steps]
    near, far = list(steps)[:2], list(steps)[2:]
    rows_local = D // n_row
    unit_count = hidden_units // unit_split
    places = jnp.arange(tok_count, dtype=jnp.int32)
    order_row = token_order[0]
    inverse = jnp.zeros((tok_count,), jnp.int32).at[order_row].set(places)
    segment, position = layout(lengths[0], tok_count)

    packed_b = hidden_in[order_row]
    gains_b = jnp.concatenate([thirds(norm1_gain), thirds(norm2_gain)])
    gathered = gather_features(jnp.concatenate([packed_b, jnp.pad(gains_b, ((0, 10), (0, 0)))]))
    cot_b = cotangent[order_row]

    width_local = w_query.shape[1]
    head_count = width_local // DH
    weight_rows = jnp.concatenate([w_query, w_key, w_value, w_out, router.T], axis=1)
    weight_pieces = {step: trade(weight_rows, step, n_row) for step in steps if step % 2 == 0}
    for step in steps:
        if step % 2 == 1:
            weight_pieces[step] = trade(weight_pieces[step ^ 1], 1, n_row)
    weight_heads = jnp.zeros((D, weight_rows.shape[1]), BF16)
    for step in steps:
        weight_heads = lax.dynamic_update_slice(
            weight_heads, weight_pieces[step], (peers[step] * rows_local, 0)
        )
    w_qkv = weight_heads[:, : 3 * width_local]
    w_out_own = weight_heads[:, 3 * width_local : 4 * width_local]
    router_all = weight_heads[:, 4 * width_local :]

    def owned_at(peer):
        return (peer * per_device // unit_split, 0, (peer % unit_split) * unit_count)

    all_weights = (w_gate, w_up, w_down)
    all_parts = [(which, e) for which in range(3) for e in range(per_device)]
    owned = {}
    w_in = [jnp.zeros((D, 2 * unit_count), BF16) for e in range(per_device)]
    w_back = [jnp.zeros((D, unit_count), BF16) for e in range(per_device)]

    def slices(parts):
        pieces = []
        for step in steps if parts else ():
            first, _, unit = owned_at(peers[step])
            held = [
                lax.dynamic_slice(
                    all_weights[which], (first + e, 0, unit), (1, rows_local, unit_count)
                )
                for which, e in parts
            ]
            pieces.append(jnp.concatenate(held))
        return pieces

    def to_owner(parts, pieces, *earlier):
        pieces = after(pieces, *earlier)
        pieces = [
            None if step == 1 else trade(pieces[step], step, n_row) for step in steps
        ]
        pieces[1] = jnp.stack([near_pieces[all_parts.index(part)] for part in parts])
        for i, (which, e) in enumerate(parts):
            for step in steps:
                at = (peers[step] * rows_local, unit_count if which == 1 else 0)
                if which < 2:
                    w_in[e] = lax.dynamic_update_slice(w_in[e], pieces[step][i], at)
                else:
                    w_back[e] = lax.dynamic_update_slice(w_back[e], pieces[step][i], at)
        return pieces

    def tied(value):
        value, w_in[:], w_back[:] = lax.optimization_barrier((value, w_in[:], w_back[:]))
        return value

    first_parts, second_parts = all_parts[:per_device], all_parts[per_device : per_device + 1]
    third_parts = all_parts[per_device + 1 : 2 * per_device + 1]
    last_parts = all_parts[2 * per_device + 1 :]
    near_pieces = trade(slices(all_parts)[1], 1, n_row)
    first_pieces = to_owner(first_parts, slices(first_parts))
    second_pieces = after(slices(second_parts), *w_in)
    later = [slices(parts) for parts in (third_parts, last_parts)]
    far_bases = far[::2]
    gathered, second_pieces, later, cot_b, inverse, near_pieces = tied(
        (gathered, second_pieces, later, cot_b, inverse, near_pieces)
    )
    gains = gathered[tok_count : tok_count + 6].astype(F32).reshape(2, 3, D).sum(axis=1)

    expert_ids = jnp.arange(E, dtype=jnp.int32)
    routes_t = routes.T
    chosen = jnp.any(routes_t[None] == expert_ids[:, None, None], axis=1)
    own_ids = col * local_experts + jnp.arange(local_experts, dtype=jnp.int32)
    own_chosen = jnp.any(routes_t[None] == own_ids[:, None, None], axis=1)
    earlier = (places[:, None] < places[None, :]).astype(BF16)
    rank = plain_dot(own_chosen.astype(BF16), earlier).astype(jnp.int32)
    slot_rank = jnp.where(own_chosen, rank, -1)
    slots = jnp.arange(capacity, dtype=jnp.int32)

    def of_peer(table, step, e):
        return lax.dynamic_slice_in_dim(table, owned_at(peers[step])[0] + e, 1, 0)

    hits = [
        [of_peer(slot_rank, step, e) == slots[:, None] for step in steps]
        for e in range(per_device)
    ]
    picks = [[hit.astype(BF16) for hit in hits[e]] for e in range(per_device)]

    far_ranks = {base: trade(slot_rank.astype(F32), base, n_row) for base in far_bases}

    def swap_small(pieces):
        table = jnp.zeros((n_row,) + pieces[0].shape, pieces[0].dtype)
        for step in steps:
            table = jnp.where(
                jnp.arange(n_row).reshape((-1,) + (1,) * pieces[0].ndim) == peers[step],
                pieces[step][None],
                table,
            )
        table = lax.all_to_all(table, "row", 0, 0, tiled=True)
        return [lax.dynamic_index_in_dim(table, peers[step], 0, False) for step in steps]

    cosine, sine = rope_tables(position)
    q_gain, k_gain = query_gain[None], key_gain[None]
    normed1, scale_in, raw_qk, query_rot, key_rot, values_b = project(
        gathered, gains[:1], weight_heads, q_gain, k_gain, cosine, sine, width_local
    )
    seg_q, seg_k = segment[:, None], jnp.where(key_mask == 1, segment, -1)[None]
    attended_b, log_totals = attend(query_rot, key_rot, values_b, seg_q, seg_k)

    half = D // 2
    out_half = lax.dynamic_slice_in_dim(w_out_own, core * half, half, 0)
    out_half_all = gather_features(after(out_half, *first_pieces[:-1]))

    to_owner(second_parts, second_pieces)
    far_cots = [trade(cot_b, base, n_row) for base in far_bases]
    attended_b = tied(attended_b)
    attended_all = gather_features(after(attended_b, out_half_all))
    third_pieces = to_owner(third_parts, later[0], attended_b, far_cots)
    other_half = trade(after(out_half_all, *w_back), 1, n_row)
    cot_alls = {
        base: gather_features(after(cot, third_pieces[2])) for base, cot in zip(far_bases, far_cots)
    }
    attended_all = tied(attended_all)
    if last_parts:
        to_owner(last_parts, later[1], w_back[0])
    normed2, scale_mid, mixed = run_branch(
        core, col, gathered, attended_all, out_half_all, other_half, gains[1:], feat_local
    )
    cot_alls[0] = gather_features(after(cot_b, normed2))
    normed2 = tied(normed2)
    column_start = col * feat_local

    all_rows = [[None] * n_row for e in range(per_device)]

    def send_rows(e, held, values):
        rows = [plain_dot(picks[e][step], values, BF16) for step in held]
        for step, row_piece in zip(held, rows):
            all_rows[e][step] = trade(row_piece, step, n_row)
        return rows

    sent = [send_rows(0, far, normed2)]
    near_values = after(normed2, sent)
    sent += [send_rows(e, near, near_values) for e in range(per_device)]

    def grad_rows_of(base, cots):
        table = far_ranks[base] if base else slot_rank.astype(F32)
        halves = []
        for step in near:
            held = []
            for e in range(per_device):
                pick = (of_peer(table, step, e) == slots[:, None].astype(F32)).astype(BF16)
                held.append(plain_dot(pick, cots, BF16))
            halves.append(held)
        return halves

    grad_rows_at = {}

    def hand_on(base, halves):
        grad_rows_at[base] = halves[0]
        grad_rows_at[base + 1] = [trade(piece, 1, n_row) for piece in halves[1]]

    logits = lax.dot_general(
        router_all, after(normed2, sent), (((0,), (1,)), ((), ())), preferred_element_type=F32
    )
    top_logit = jnp.max(jnp.where(chosen, logits, -jnp.inf), axis=0, keepdims=True)
    raised = jnp.where(chosen, jnp.exp(logits - top_logit), 0.0)
    gate_probs = raised / jnp.sum(raised, axis=0, keepdims=True)
    own_probs = lax.dynamic_slice_in_dim(gate_probs, col * local_experts, local_experts, 0)

    slot_gates = []
    for step in steps:
        held = [
            jnp.sum(jnp.where(hits[e][step], of_peer(own_probs, step, e), 0.0), axis=1)
            for e in range(per_device)
        ]
        slot_gates.append(jnp.stack(held))
    slot_gates = swap_small(slot_gates)

    all_rows[0], slot_gates, later_rows = lax.optimization_barrier(
        (all_rows[0], slot_gates, normed2)
    )
    for e in range(1, per_device):
        sent.append(send_rows(e, far, later_rows))
    far_cots = after([cot_alls[base] for base in far_bases], sent, later_rows)
    for base, cots in zip(far_bases, far_cots):
        hand_on(base, grad_rows_of(base, cots))

    both = range(per_device)
    calls, grads_back = {}, [[None] * n_row for e in range(per_device)]

    def gates_of(e, step):
        return jnp.concatenate([slot_gates[step][e], slot_gates[step + 1][e]])[:, None]

    def expert_call(e, step, gates):
        xs = [all_rows[e][step], all_rows[e][step + 1]]
        cs = [grad_rows_at[step][e], grad_rows_at[step + 1][e]]
        act, grad_pre, sums, *back = run_expert(xs, cs, gates, w_in[e], w_back[e])
        calls[e, step] = [xs, cs, [act], [grad_pre], [sums], back]

    def send_back(e, step):
        for i, piece in enumerate(calls[e, step][-1]):
            grads_back[e][step + i] = trade(piece, step + i, n_row)

    def far_calls(e):
        return [calls[e, step] for step in far_bases]

    for step in far_bases:
        expert_call(0, step, gates_of(0, step))
        send_back(0, step)
    for e in range(1, per_device):
        all_rows[e] = after(all_rows[e], far_calls(0))
        for step in far_bases:
            expert_call(e, step, gates_of(e, step))
    every = [(e, step) for e in range(per_device) for step in steps]
    ranks = jnp.concatenate([of_peer(slot_rank, step, e) for e, step in every])
    near_gates = [gates_of(e, 0) for e in both]
    near_cots, near_gates, ranks, _ = lax.optimization_barrier(
        (cot_alls[0], near_gates, ranks, [far_calls(e) for e in both])
    )
    near_halves = grad_rows_of(0, near_cots)
    for e in range(1, per_device):
        held, grads_back[e - 1], near_halves = lax.optimization_barrier(
            (far_calls(e), grads_back[e - 1], near_halves)
        )
        for step, call in zip(far_bases, held):
            calls[e, step] = call
            send_back(e, step)
    hand_on(0, near_halves)
    for e in range(per_device):
        expert_call(e, 0, near_gates[e])
        send_back(e, 0)
    last_near = (per_device - 1, 0)
    calls[last_near], grads_back[-1] = lax.optimization_barrier((calls[last_near], grads_back[-1]))

    def joined(e, which):
        return jnp.concatenate([piece for step in steps[::2] for piece in calls[e, step][which]])

    scalars = [joined(e, 4) for e in range(per_device)]
    scalars = jnp.stack(scalars)
    scalars_back = swap_small(
        [scalars[:, step * capacity : (step + 1) * capacity] for step in steps]
    )
    grad_normed2_part = combine(ranks, [grads_back[e][step] for e, step in every])

    calls = after(calls, grad_normed2_part)
    branch_back, weight_grads = [], []
    for e in range(per_device):
        rows, grad_rows, act, grad_pre = (joined(e, which) for which in range(4))
        out = contract_last(act, w_back[e], BF16)
        branch_back.append(
            trade_all([out[step * capacity : (step + 1) * capacity] for step in steps])
        )
        grad_in = contract_first(rows, grad_pre, BF16)
        weight_grads.append(
            (
                grad_in[:, :unit_count],
                grad_in[:, unit_count:],
                contract_first(grad_rows, act, BF16),
            )
        )
    grad_normed2 = scatter_partial(grad_normed2_part).astype(F32)

    grad_own = jnp.zeros((local_experts, tok_count), F32)
    inner_own = jnp.zeros((1, tok_count), F32)
    own_rows = jnp.arange(local_experts, dtype=jnp.int32)[:, None]
    for e in range(per_device):
        for step in steps:
            expert = owned_at(peers[step])[0] + e
            back = scalars_back[step][e]
            spread = jnp.sum(jnp.where(hits[e][step], back[:, :1], 0.0), axis=0, keepdims=True)
            grad_own = grad_own + jnp.where(own_rows == expert, spread, 0.0)
            inner_own = inner_own + jnp.sum(
                jnp.where(hits[e][step], back[:, 1:], 0.0), axis=0, keepdims=True
            )
    small = jnp.concatenate([grad_own, inner_own], axis=0)
    small, branch_back[0] = lax.optimization_barrier((small, branch_back[0]))
    small = lax.all_to_all(
        jnp.broadcast_to(small.astype(BF16)[None], (n_col,) + small.shape), "col", 0, 0, tiled=True
    )
    small, branch_back = lax.optimization_barrier((small, branch_back))
    small = small.astype(F32)
    grad_gates = small[:, :local_experts].reshape(E, tok_count)
    grad_logits = gate_probs * (
        grad_gates - jnp.sum(gate_probs * grad_gates, axis=0, keepdims=True)
    )
    grad_logits = grad_logits.astype(BF16)
    inner_mid = jnp.sum(small[:, local_experts], axis=0) + jnp.sum(
        grad_logits.astype(F32) * logits, axis=0
    )
    inner_mid = (inner_mid / D)[:, None]
    grad_router = lax.dot_general(
        normed2, grad_logits, (((0,), (1,)), ((), ())), preferred_element_type=F32
    )
    router_local = lax.dynamic_slice_in_dim(router_all, column_start, feat_local, 0)
    grad_unit_mid = grad_normed2 + lax.dot_general(
        grad_logits, router_local, (((0,), (1,)), ((), ())), preferred_element_type=F32
    )
    unit_mid = mixed * scale_mid
    grad_norm2 = jnp.sum(grad_unit_mid * unit_mid, axis=0)
    scaled_mid = grad_unit_mid * norm2_gain
    grad_mixed = cot_b.astype(F32) + scale_mid * (scaled_mid - unit_mid * inner_mid)
    def held_slices(which, experts):
        return [
            jnp.stack(
                [
                    lax.dynamic_slice_in_dim(
                        weight_grads[e][which], peers[step] * rows_local, rows_local, 0
                    )
                    for e in experts
                ]
            )
            for step in steps
        ]

    def to_holders(pieces, *earlier):
        return trade_all(after(pieces, *earlier))

    gate_slices, up_slices = held_slices(0, both), held_slices(1, both)
    grad_mixed_b, gate_slices, up_slices = lax.optimization_barrier(
        (grad_mixed.astype(BF16), gate_slices, up_slices)
    )
    grad_branch = gather_features(grad_mixed_b)
    gate_pieces = to_holders(gate_slices)

    def to_rows(pieces):
        flat, places = [], []
        for e, held in enumerate(pieces):
            for step in steps:
                first, _, unit = owned_at(peers[step])
                flat.append(held[step])
                places += [first + e, unit]
        return place(jnp.stack(places), flat, local_experts, hidden_units)

    def sum_cores(grad):
        parts = [
            lax.dynamic_slice_in_dim(grad, peers[step] * rows_local, rows_local, 0)
            for step in steps
        ]
        other = trade(jnp.stack(parts[1::2]), 1, n_row).astype(F32)
        sums = [part.astype(F32) + other[i] for i, part in enumerate(parts[::2])]
        return [sums[0]] + [part.astype(grad.dtype) for part in sums[1:]]

    def sum_chips(sums):
        total = sums[0]
        for part, base in zip(sums[1:], far_bases):
            total = total + trade(part, base, n_row).astype(F32)
        return total

    def sum_groups(grad, *earlier):
        return sum_chips(sum_cores(after(grad, *earlier)))

    combined_part = combine(ranks, [branch_back[e][step] for e, step in every])
    grad_branch, gate_pieces, combined_part = lax.optimization_barrier(
        (grad_branch, gate_pieces, combined_part)
    )
    up_pieces = to_holders(up_slices, gate_pieces)

    combined = scatter_partial(combined_part)

    grad_w_out = contract_first(grad_branch, attended_b, BF16)
    grad_w_gate = to_rows([gate_pieces])
    grad_attended = plain_dot(after(grad_branch, grad_w_gate), w_out_own, BF16)
    grad_q, grad_k, grad_v, grad_query_gain, grad_key_gain = attend_back(
        query_rot, key_rot, values_b, grad_attended, log_totals, seg_q, seg_k, raw_qk,
        q_gain, k_gain, cosine, sine,
    )
    grad_qkv = jnp.concatenate([grad_q, grad_k, grad_v], axis=1)
    grad_w_out = sum_groups(grad_w_out)
    grad_router = sum_groups(grad_router, grad_branch).T
    down_slices = [held_slices(2, [e]) for e in range(per_device)]
    grad_qkv, up_pieces, combined, down_slices, grad_w_out, grad_router = (
        lax.optimization_barrier(
            (grad_qkv, up_pieces, combined, down_slices, grad_w_out, grad_router)
        )
    )
    down_pieces = [to_holders(down_slices[0])]
    grad_normed1_part = through_heads(grad_qkv, weight_heads)
    grad_unit_in = scatter_partial(grad_normed1_part)
    output = (mixed + combined.astype(F32)).astype(BF16)[inverse]
    grad_w_up = to_rows([up_pieces])
    grad_normed1_part, down_pieces, output, grad_w_up = lax.optimization_barrier(
        (grad_normed1_part, down_pieces, output, grad_w_up)
    )
    down_pieces += [to_holders(held, down_pieces) for held in down_slices[1:]]
    inner_in = jnp.sum(
        grad_qkv.astype(F32) * jnp.concatenate([raw_qk, values_b.astype(F32)], axis=1), axis=1
    )
    packed = packed_b.astype(F32)
    unit_in = packed * scale_in
    unit_all = gathered[:tok_count].astype(F32) * scale_in
    grad_norm1 = jnp.sum(grad_normed1_part.astype(F32) * unit_all, axis=0)
    def for_all(vector):
        return jnp.broadcast_to(vector[None], (n_col,) + vector.shape)

    vectors = jnp.concatenate(
        [
            for_all(inner_in),
            for_all(grad_query_gain[0]),
            for_all(grad_key_gain[0]),
            grad_norm1.reshape(n_col, feat_local),
        ],
        axis=1,
    )
    heads_sums = sum_cores(contract_first(normed1, grad_qkv, BF16))
    vectors, heads_sums = lax.optimization_barrier((vectors, heads_sums))
    vectors = jnp.sum(lax.all_to_all(vectors, "col", 0, 0, tiled=True), axis=0)
    vectors, down_pieces, heads_sums = lax.optimization_barrier(
        (vectors, down_pieces, heads_sums)
    )
    inner_in = vectors[:tok_count, None] / D
    vectors = jnp.concatenate([vectors[tok_count:], grad_norm2])
    vectors = sum(trade(vectors, step, n_row) for step in steps)
    grad_heads = sum_chips(heads_sums)
    grad_unit_in, vectors, inner_in, grad_heads = lax.optimization_barrier(
        (grad_unit_in, vectors, inner_in, grad_heads)
    )
    grad_unit_in = grad_unit_in.astype(F32)
    scaled_in = grad_unit_in * norm1_gain
    grad_input = (grad_mixed + scale_in * (scaled_in - unit_in * inner_in))[inverse]

    grad_w_query, grad_w_key, grad_w_value = (
        grad_heads[:, i * width_local : (i + 1) * width_local] for i in range(3)
    )
    grad_w_down = to_rows(down_pieces)

    grad_query_gain, grad_key_gain = vectors[:DH], vectors[DH : 2 * DH]
    grad_norm1 = vectors[2 * DH : 2 * DH + feat_local]
    grad_norm2 = vectors[2 * DH + feat_local :]
    return (
        output,
        grad_input,
        grad_norm1,
        grad_query_gain,
        grad_key_gain,
        grad_w_query,
        grad_w_key,
        grad_w_value,
        grad_w_out,
        grad_norm2,
        grad_router,
        grad_w_gate,
        grad_w_up,
        grad_w_down,
    )


def solution(mesh):
    return jax.shard_map(
        body,
        mesh=mesh,
        in_specs=(
            P("row", "col"),
            P("row", None),
            P("row", None),
            P("row"),
            P("row", None),
            P("col"),
            P(),
            P(),
            P("row", "col"),
            P("row", "col"),
            P("row", "col"),
            P("row", "col"),
            P("col"),
            P(None, "row"),
            P("col", "row", None),
            P("col", "row", None),
            P("col", "row", None),
            P("row", "col"),
        ),
        out_specs=(
            P("row", "col"),
            P("row", "col"),
            P("col"),
            P(),
            P(),
            P("row", "col"),
            P("row", "col"),
            P("row", "col"),
            P("row", "col"),
            P("col"),
            P(None, "row"),
            P("col", "row", None),
            P("col", "row", None),
            P("col", "row", None),
        ),
        check_vma=False,
    )
```

```python
import jax
import jax.numpy as jnp
from jax import lax
from jax.experimental import pallas as pl
from jax.experimental.pallas import tpu as pltpu
from jax.sharding import PartitionSpec as P

D = 2048
DH = 128
E = 64
TOP = 8


EPSILON = 1e-06
ROPE_BASE = 10000.0
BF16 = jnp.bfloat16
F32 = jnp.float32


def layout(seq_lengths, tok_count):
    seq_ends = jnp.cumsum(seq_lengths)
    seq_starts = seq_ends - seq_lengths
    places = jnp.arange(tok_count, dtype=jnp.int32)
    segment = jnp.sum((places[:, None] >= seq_ends[None, :]).astype(jnp.int32), axis=1)
    member = segment[:, None] == jnp.arange(seq_lengths.shape[0], dtype=jnp.int32)[None, :]
    offset = jnp.sum(jnp.where(member, seq_starts[None, :], 0), axis=1)
    return (segment, places - offset)


def rope_tables(position):
    half_dim = DH // 2
    frequency = ROPE_BASE ** (-2.0 * jnp.arange(half_dim, dtype=F32) / DH)
    angles = position.astype(F32)[:, None] * frequency[None, :]
    cosine, sine = jnp.cos(angles), jnp.sin(angles)
    return jnp.concatenate([cosine, cosine], 1), jnp.concatenate([-sine, sine], 1)


def gather_features(local_rows):
    return lax.all_gather(local_rows, "col", axis=1, tiled=True)


def scatter_partial(partial_rows):
    return lax.psum_scatter(partial_rows, "col", scatter_dimension=1, tiled=True)


def trade(value, step, n_row):
    if step == 0:
        return value
    return lax.ppermute(value, "row", [(r, r ^ step) for r in range(n_row)])


def trade_all(pieces):
    return [trade(piece, step, len(pieces)) for step, piece in enumerate(pieces)]


def contract_last(left_op, right_op, kind=F32):
    return lax.dot_general(
        left_op, right_op, (((1,), (1,)), ((), ())), preferred_element_type=F32
    ).astype(kind)


def contract_first(left_op, right_op, kind=F32):
    return lax.dot_general(
        left_op, right_op, (((0,), (0,)), ((), ())), preferred_element_type=F32
    ).astype(kind)


def plain_dot(left_op, right_op, kind=F32):
    return jnp.dot(left_op, right_op, preferred_element_type=F32).astype(kind)


def after(value, *earlier):
    return lax.optimization_barrier((value, *earlier))[0]


def thirds(values):
    high = lax.reduce_precision(values, 8, 7)
    middle = lax.reduce_precision(values - high, 8, 7)
    return jnp.stack([high, middle, values - high - middle]).astype(BF16)


def cost(flops, moved):
    return pl.CostEstimate(flops=flops, bytes_accessed=moved, transcendentals=0)


def rope(values, cosine, sine):
    return values * cosine + pltpu.roll(values, DH // 2, 1) * sine


def rope_back(grad, cosine, sine):
    return grad * cosine + pltpu.roll(grad * sine, DH // 2, 1)


def project_kernel(x_ref, gain_ref, w_ref, qg_ref, kg_ref, cos_ref, sin_ref, *outs):
    normed_ref, scale_ref, raw_ref, q_ref, k_ref, v_ref = outs
    x = x_ref[...].astype(F32)
    scale = lax.rsqrt(jnp.mean(x * x, axis=1, keepdims=True) + EPSILON)
    normed = (x * scale * gain_ref[...]).astype(BF16)
    normed_ref[...] = normed
    scale_ref[...] = scale
    width = q_ref.shape[1]
    qkv = jnp.dot(normed, w_ref[:, : 3 * width], preferred_element_type=F32)
    raw_ref[...] = qkv[:, : 2 * width]
    v_ref[...] = qkv[:, 2 * width :].astype(BF16)
    cosine, sine = cos_ref[...], sin_ref[...]
    for part, gain, out in ((0, qg_ref, q_ref), (1, kg_ref, k_ref)):
        for h in range(width // DH):
            head = qkv[:, part * width + h * DH : part * width + (h + 1) * DH]
            size = lax.rsqrt(jnp.mean(head * head, axis=1, keepdims=True) + EPSILON)
            out[:, h * DH : (h + 1) * DH] = rope(head * size * gain[...], cosine, sine).astype(BF16)


def project(x, gain, w, q_gain, k_gain, cosine, sine, width, block=256):
    rows = cosine.shape[0]
    by_rows = lambda n: pl.BlockSpec((block, n), lambda i: (i, 0))
    whole = lambda a: pl.BlockSpec(a.shape, lambda i: (0, 0))
    return pl.pallas_call(
        project_kernel,
        name="project",
        grid=(rows // block,),
        in_specs=[
            by_rows(D),
            whole(gain),
            whole(w),
            whole(q_gain),
            whole(k_gain),
            by_rows(DH),
            by_rows(DH),
        ],
        out_specs=[by_rows(n) for n in (D, 1, 2 * width, width, width, width)],
        out_shape=[
            jax.ShapeDtypeStruct((rows, D), BF16),
            jax.ShapeDtypeStruct((rows, 1), F32),
            jax.ShapeDtypeStruct((rows, 2 * width), F32),
            jax.ShapeDtypeStruct((rows, width), BF16),
            jax.ShapeDtypeStruct((rows, width), BF16),
            jax.ShapeDtypeStruct((rows, width), BF16),
        ],
        cost_estimate=cost(1000, 1000),
    )(x, gain, w, q_gain, k_gain, cosine, sine)


def masked_scores(q, k, seg_q, seg_k, first):
    scores = lax.dot_general(q, k, (((1,), (1,)), ((), ())), preferred_element_type=F32)
    rows = first + lax.broadcasted_iota(jnp.int32, scores.shape, 0)
    columns = lax.broadcasted_iota(jnp.int32, scores.shape, 1)
    allowed = (seg_q == seg_k) | (rows == columns)
    return jnp.where(allowed, scores * DH ** (-0.5), -1e30)


def attend_kernel(q_ref, k_ref, v_ref, seg_q_ref, seg_k_ref, out_ref, log_ref):
    first = pl.program_id(1) * q_ref.shape[0]
    scores = masked_scores(q_ref[...], k_ref[...], seg_q_ref[...], seg_k_ref[...], first)
    top = jnp.max(scores, axis=1, keepdims=True)
    terms = jnp.exp(scores - top)
    total = jnp.sum(terms, axis=1, keepdims=True)
    weights = (terms * (1.0 / total)).astype(BF16)
    out_ref[...] = jnp.dot(weights, v_ref[...], preferred_element_type=F32).astype(BF16)
    log_ref[0] = top + jnp.log(total)


def attend(q, k, v, seg_q, seg_k, block=256):
    rows, width = q.shape
    heads = width // DH
    by_rows = pl.BlockSpec((block, DH), lambda h, i: (i, h))
    whole = pl.BlockSpec((rows, DH), lambda h, i: (0, h))
    return pl.pallas_call(
        attend_kernel,
        name="attend",
        grid=(heads, rows // block),
        in_specs=[
            by_rows,
            whole,
            whole,
            pl.BlockSpec((block, 1), lambda h, i: (i, 0)),
            pl.BlockSpec((1, rows), lambda h, i: (0, 0)),
        ],
        out_specs=[by_rows, pl.BlockSpec((1, block, 1), lambda h, i: (h, i, 0))],
        out_shape=[
            jax.ShapeDtypeStruct((rows, width), BF16),
            jax.ShapeDtypeStruct((heads, rows, 1), F32),
        ],
        cost_estimate=cost(1000, 1000),
    )(q, k, v, seg_q, seg_k)


def head_back(grad, raw, gain, cosine, sine):
    grad = rope_back(grad, cosine, sine)
    size = lax.rsqrt(jnp.mean(raw * raw, axis=1, keepdims=True) + EPSILON)
    unit = raw * size
    grad_gain = jnp.sum(grad * unit, axis=0, keepdims=True)
    grad = grad * gain
    return size * (grad - unit * jnp.mean(grad * unit, axis=1, keepdims=True)), grad_gain


def attend_back_kernel(
    q_ref, k_ref, v_ref, grad_ref, log_ref, seg_q_ref, seg_k_ref, raw_q_ref, raw_k_ref,
    qg_ref, kg_ref, cos_q_ref, sin_q_ref, cos_ref, sin_ref,
    dq_ref, dk_ref, dv_ref, dqg_ref, dkg_ref, sum_k, sum_v,
):
    head, i = pl.program_id(0), pl.program_id(1)

    @pl.when((head == 0) & (i == 0))
    def _():
        dqg_ref[...] = jnp.zeros_like(dqg_ref)
        dkg_ref[...] = jnp.zeros_like(dkg_ref)

    @pl.when(i == 0)
    def _():
        sum_k[...] = jnp.zeros_like(sum_k)
        sum_v[...] = jnp.zeros_like(sum_v)

    q, k, grad = q_ref[...], k_ref[...], grad_ref[...]
    scores = masked_scores(q, k, seg_q_ref[...], seg_k_ref[...], i * q.shape[0])
    probs = jnp.exp(scores - log_ref[0])
    sum_v[...] += lax.dot_general(
        probs.astype(BF16), grad, (((0,), (0,)), ((), ())), preferred_element_type=F32
    )
    grad_probs = lax.dot_general(
        grad, v_ref[...], (((1,), (1,)), ((), ())), preferred_element_type=F32
    )
    inner = jnp.sum(probs * grad_probs, axis=1, keepdims=True)
    grad_scores = (probs * (grad_probs - inner)).astype(BF16)
    sum_k[...] += lax.dot_general(
        grad_scores, q, (((0,), (0,)), ((), ())), preferred_element_type=F32
    )
    grad_q = jnp.dot(grad_scores, k, preferred_element_type=F32) * DH ** (-0.5)
    grad_q, grad_gain = head_back(
        grad_q, raw_q_ref[...], qg_ref[...], cos_q_ref[...], sin_q_ref[...]
    )
    dq_ref[...] = grad_q.astype(BF16)
    dqg_ref[...] += grad_gain

    @pl.when(i == pl.num_programs(1) - 1)
    def _():
        grad_k, gain_k = head_back(
            sum_k[...] * DH ** (-0.5), raw_k_ref[...], kg_ref[...], cos_ref[...], sin_ref[...]
        )
        dk_ref[...] = grad_k.astype(BF16)
        dkg_ref[...] += gain_k
        dv_ref[...] = sum_v[...].astype(BF16)


def attend_back(q, k, v, grad, logs, seg_q, seg_k, raw, q_gain, k_gain, cosine, sine, block=256):
    rows, width = q.shape
    heads = width // DH
    by_rows = pl.BlockSpec((block, DH), lambda h, i: (i, h))
    whole = pl.BlockSpec((rows, DH), lambda h, i: (0, h))
    gain = pl.BlockSpec((1, DH), lambda h, i: (0, 0))
    return pl.pallas_call(
        attend_back_kernel,
        name="attend_back",
        grid=(heads, rows // block),
        in_specs=[
            by_rows,
            whole,
            whole,
            by_rows,
            pl.BlockSpec((1, block, 1), lambda h, i: (h, i, 0)),
            pl.BlockSpec((block, 1), lambda h, i: (i, 0)),
            pl.BlockSpec((1, rows), lambda h, i: (0, 0)),
            by_rows,
            pl.BlockSpec((rows, DH), lambda h, i: (0, heads + h)),
            gain,
            gain,
            pl.BlockSpec((block, DH), lambda h, i: (i, 0)),
            pl.BlockSpec((block, DH), lambda h, i: (i, 0)),
            pl.BlockSpec((rows, DH), lambda h, i: (0, 0)),
            pl.BlockSpec((rows, DH), lambda h, i: (0, 0)),
        ],
        out_specs=[by_rows, whole, whole, gain, gain],
        out_shape=[
            jax.ShapeDtypeStruct((rows, width), BF16),
            jax.ShapeDtypeStruct((rows, width), BF16),
            jax.ShapeDtypeStruct((rows, width), BF16),
            jax.ShapeDtypeStruct((1, DH), F32),
            jax.ShapeDtypeStruct((1, DH), F32),
        ],
        scratch_shapes=[pltpu.VMEM((rows, DH), F32), pltpu.VMEM((rows, DH), F32)],
        cost_estimate=cost(1000, 1000),
    )(q, k, v, grad, logs, seg_q, seg_k, raw, raw, q_gain, k_gain, cosine, sine, cosine, sine)


def branch_kernel(
    at_ref, x_ref, att_ref, own_ref, other_ref, gain_ref, normed_ref, scale_ref, mixed_ref, total
):
    half = own_ref.shape[0]
    own = contract_last(att_ref[...], own_ref[...])
    other = contract_last(att_ref[...], other_ref[...])
    second = at_ref[0] == 1
    total[:, :half] = x_ref[:, :half].astype(F32) + jnp.where(second, other, own)
    total[:, half:] = x_ref[:, half:].astype(F32) + jnp.where(second, own, other)
    mixed = total[...]
    scale = lax.rsqrt(jnp.mean(mixed * mixed, axis=1, keepdims=True) + EPSILON)
    normed_ref[...] = (mixed * scale * gain_ref[...]).astype(BF16)
    scale_ref[...] = scale
    width = mixed_ref.shape[1]
    mixed_ref[...] = total[:, pl.ds(pl.multiple_of(at_ref[1] * width, 128), width)]


def run_branch(core, col, x, attended, own, other, gain, width, block=256):
    rows = attended.shape[0]
    by_rows = lambda n: pl.BlockSpec((block, n), lambda i, at: (i, 0))
    whole = lambda a: pl.BlockSpec(a.shape, lambda i, at: (0, 0))
    return pl.pallas_call(
        branch_kernel,
        name="branch",
        grid_spec=pltpu.PrefetchScalarGridSpec(
            num_scalar_prefetch=1,
            grid=(rows // block,),
            in_specs=[by_rows(D), by_rows(D), whole(own), whole(other), whole(gain)],
            out_specs=[by_rows(D), by_rows(1), by_rows(width)],
            scratch_shapes=[pltpu.VMEM((block, D), F32)],
        ),
        out_shape=[
            jax.ShapeDtypeStruct((rows, D), BF16),
            jax.ShapeDtypeStruct((rows, 1), F32),
            jax.ShapeDtypeStruct((rows, width), F32),
        ],
        cost_estimate=cost(1000, 1000),
    )(jnp.stack([core, col]), x, attended, own, other, gain)


def expert_kernel(
    x0_ref, x1_ref, c0_ref, c1_ref, gate_ref, w_ref, wd_ref,
    act_ref, grad_ref, sums_ref, dx0_ref, dx1_ref,
):
    width = act_ref.shape[1]
    slot_gate = gate_ref[...]
    rows = jnp.concatenate([x0_ref[...], x1_ref[...]], axis=0)
    pre = jnp.dot(rows, w_ref[...], preferred_element_type=F32)
    gate, up = pre[:, :width], pre[:, width:]
    cots = jnp.concatenate([c0_ref[...], c1_ref[...]], axis=0)
    grad = jnp.dot(cots, wd_ref[...], preferred_element_type=F32)
    opened = 1.0 / (1.0 + jnp.exp(-gate))
    silu = gate * opened
    act = silu * up
    act_ref[...] = (slot_gate * act).astype(BF16)
    grad_gate = jnp.sum(act * grad, axis=1, keepdims=True)
    grad = slot_gate * grad
    dgate = (grad * up * opened * (1.0 + gate * (1.0 - opened))).astype(BF16)
    dup = (grad * silu).astype(BF16)
    grad_ref[:, :width] = dgate
    grad_ref[:, width:] = dup
    inner = jnp.sum(dgate.astype(F32) * gate + dup.astype(F32) * up, axis=1, keepdims=True)
    sums_ref[:, 0:1] = grad_gate
    sums_ref[:, 1:2] = inner
    back = contract_last(grad_ref[...], w_ref[...], BF16)
    dx0_ref[...] = back[: dx0_ref.shape[0]]
    dx1_ref[...] = back[dx0_ref.shape[0] :]


def run_expert(xs, cs, slot_gate, w, wd):
    capacity, width = xs[0].shape[0], wd.shape[1]
    slots = 2 * capacity
    operands = [*xs, *cs, slot_gate, w, wd]
    outs = [(slots, width, BF16), (slots, 2 * width, BF16), (slots, 2, F32)]
    outs += [(capacity, D, BF16)] * 2
    whole = lambda shape: pl.BlockSpec(shape, lambda i: (0, 0), pipeline_mode=pl.Buffered(1))
    return pl.pallas_call(
        expert_kernel,
        name="expert",
        grid=(1,),
        in_specs=[whole(a.shape) for a in operands],
        out_specs=[pl.BlockSpec(out[:2], lambda i: (0, 0)) for out in outs],
        out_shape=[jax.ShapeDtypeStruct(out[:2], out[2]) for out in outs],
        cost_estimate=cost(1000, 1000),
    )(*operands)


def through_heads_kernel(grad_ref, w_ref, out_ref):
    width = grad_ref.shape[1]
    out_ref[...] = contract_last(grad_ref[...], w_ref[:, :width], BF16)


def through_heads(grad, w, block=768):
    rows, width = grad.shape
    return pl.pallas_call(
        through_heads_kernel,
        name="through_heads",
        grid=(rows // block,),
        in_specs=[
            pl.BlockSpec((block, width), lambda i: (i, 0)),
            pl.BlockSpec(w.shape, lambda i: (0, 0)),
        ],
        out_specs=pl.BlockSpec((block, D), lambda i: (i, 0)),
        out_shape=jax.ShapeDtypeStruct((rows, D), BF16),
        cost_estimate=cost(1000, 1000),
    )(grad, w)


def pick_kernel(rank_ref, value_ref, *refs):
    hits_ref = refs[-1]
    pieces = refs[:-1]
    capacity = pieces[0].shape[0]

    @pl.when(pl.program_id(0) == 0)
    def _():
        slots = lax.broadcasted_iota(jnp.int32, (capacity, hits_ref.shape[1]), 0)
        for i in range(len(pieces)):
            hits = (slots == rank_ref[i : i + 1, :]).astype(BF16)
            hits_ref[i * capacity : (i + 1) * capacity, :] = hits

    rows = jnp.dot(hits_ref[...], value_ref[...], preferred_element_type=F32).astype(BF16)
    for i, piece in enumerate(pieces):
        piece[...] = rows[i * capacity : (i + 1) * capacity]


def pick(ranks, values, capacity, block=512):
    pieces, rows = ranks.shape
    by_width = lambda n: pl.BlockSpec((n, block), lambda j: (0, j))
    return pl.pallas_call(
        pick_kernel,
        name="pick",
        grid=(D // block,),
        in_specs=[pl.BlockSpec(ranks.shape, lambda j: (0, 0)), by_width(rows)],
        out_specs=[by_width(capacity)] * pieces,
        out_shape=[jax.ShapeDtypeStruct((capacity, D), BF16)] * pieces,
        scratch_shapes=[pltpu.VMEM((pieces * capacity, rows), BF16)],
        cost_estimate=cost(1000, 1000),
    )(ranks, values)


def combine_kernel(*refs):
    rank_ref, out_ref = refs[0], refs[-1]
    pieces = refs[1:-1]
    total = 0.0
    for i, piece in enumerate(pieces):
        shape = (piece.shape[0], out_ref.shape[0])
        slots = lax.broadcasted_iota(jnp.int32, shape, 0)
        hits = (slots == rank_ref[i : i + 1, :]).astype(BF16)
        total = total + contract_first(hits, piece[...])
    out_ref[...] = total.astype(BF16)


def combine(ranks, pieces, block=768):
    rows = ranks.shape[1]
    width = 1024
    whole = lambda a: pl.BlockSpec((a.shape[0], width), lambda j, i: (0, j))
    return pl.pallas_call(
        combine_kernel,
        name="combine",
        grid=(D // width, rows // block),
        in_specs=[pl.BlockSpec((len(pieces), block), lambda j, i: (0, i))]
        + [whole(piece) for piece in pieces],
        out_specs=pl.BlockSpec((block, width), lambda j, i: (i, j)),
        out_shape=jax.ShapeDtypeStruct((rows, D), BF16),
        cost_estimate=cost(1000, 1000),
    )(ranks, *pieces)


def place_kernel(at_ref, *refs):
    out_ref = refs[-1]
    for i, piece in enumerate(refs[:-1]):
        experts, _, units = piece.shape
        first, unit = at_ref[2 * i], pl.multiple_of(at_ref[2 * i + 1], 128)
        for e in range(experts):
            out_ref[first + e, :, pl.ds(unit, units)] = piece[e].astype(F32)


def place(places, pieces, experts, units, block=64):
    rows = pieces[0].shape[1]
    spec = lambda a: pl.BlockSpec((a.shape[0], block, a.shape[2]), lambda i, at: (0, i, 0))
    return pl.pallas_call(
        place_kernel,
        name="place",
        grid_spec=pltpu.PrefetchScalarGridSpec(
            num_scalar_prefetch=1,
            grid=(rows // block,),
            in_specs=[spec(piece) for piece in pieces],
            out_specs=pl.BlockSpec((experts, block, units), lambda i, at: (0, i, 0)),
        ),
        out_shape=jax.ShapeDtypeStruct((experts, rows, units), F32),
        cost_estimate=cost(1000, 1000),
    )(places, *pieces)


def body(
    hidden_in,
    token_order,
    lengths,
    key_mask,
    routes,
    norm1_gain,
    query_gain,
    key_gain,
    w_query,
    w_key,
    w_value,
    w_out,
    norm2_gain,
    router,
    w_gate,
    w_up,
    w_down,
    cotangent,
):
    tok_count, feat_local = hidden_in.shape
    n_row = D // w_query.shape[0]
    n_col = D // feat_local
    local_experts, _, hidden_units = w_gate.shape
    per_device = max(1, local_experts // n_row)
    unit_split = max(1, n_row // local_experts)
    capacity = 5 * tok_count * TOP // (4 * E)
    col = lax.axis_index("col")
    row = lax.axis_index("row")
    core = row % 2
    steps = range(n_row)
    peers = [row ^ step for step in steps]
    near, far = list(steps)[:2], list(steps)[2:]
    rows_local = D // n_row
    unit_count = hidden_units // unit_split
    places = jnp.arange(tok_count, dtype=jnp.int32)
    order_row = token_order[0]
    inverse = jnp.zeros((tok_count,), jnp.int32).at[order_row].set(places)
    segment, position = layout(lengths[0], tok_count)

    packed_b = hidden_in[order_row]
    gains_b = jnp.concatenate([thirds(norm1_gain), thirds(norm2_gain)])
    gathered = gather_features(jnp.concatenate([packed_b, jnp.pad(gains_b, ((0, 10), (0, 0)))]))
    cot_b = cotangent[order_row]

    width_local = w_query.shape[1]
    head_count = width_local // DH
    weight_rows = jnp.concatenate([w_query, w_key, w_value, w_out, router.T], axis=1)
    weight_pieces = {step: trade(weight_rows, step, n_row) for step in steps if step % 2 == 0}
    for step in steps:
        if step % 2 == 1:
            weight_pieces[step] = trade(weight_pieces[step ^ 1], 1, n_row)
    weight_heads = jnp.zeros((D, weight_rows.shape[1]), BF16)
    for step in steps:
        weight_heads = lax.dynamic_update_slice(
            weight_heads, weight_pieces[step], (peers[step] * rows_local, 0)
        )
    w_qkv = weight_heads[:, : 3 * width_local]
    w_out_own = weight_heads[:, 3 * width_local : 4 * width_local]
    router_all = weight_heads[:, 4 * width_local :]

    def owned_at(peer):
        return (peer * per_device // unit_split, 0, (peer % unit_split) * unit_count)

    all_weights = (w_gate, w_up, w_down)
    all_parts = [(which, e) for which in range(3) for e in range(per_device)]
    owned = {}
    w_in = [jnp.zeros((D, 2 * unit_count), BF16) for e in range(per_device)]
    w_back = [jnp.zeros((D, unit_count), BF16) for e in range(per_device)]

    def slices(parts):
        pieces = []
        for step in steps if parts else ():
            first, _, unit = owned_at(peers[step])
            held = [
                lax.dynamic_slice(
                    all_weights[which], (first + e, 0, unit), (1, rows_local, unit_count)
                )
                for which, e in parts
            ]
            pieces.append(jnp.concatenate(held))
        return pieces

    def to_owner(parts, pieces, *earlier):
        pieces = after(pieces, *earlier)
        pieces = [
            None if step == 1 else trade(pieces[step], step, n_row) for step in steps
        ]
        pieces[1] = jnp.stack([near_pieces[all_parts.index(part)] for part in parts])
        for i, (which, e) in enumerate(parts):
            for step in steps:
                at = (peers[step] * rows_local, unit_count if which == 1 else 0)
                if which < 2:
                    w_in[e] = lax.dynamic_update_slice(w_in[e], pieces[step][i], at)
                else:
                    w_back[e] = lax.dynamic_update_slice(w_back[e], pieces[step][i], at)
        return pieces

    def tied(value):
        value, w_in[:], w_back[:] = lax.optimization_barrier((value, w_in[:], w_back[:]))
        return value

    first_parts, second_parts = all_parts[:per_device], all_parts[per_device : per_device + 1]
    third_parts = all_parts[per_device + 1 : 2 * per_device + 1]
    last_parts = all_parts[2 * per_device + 1 :]
    near_pieces = trade(slices(all_parts)[1], 1, n_row)
    first_pieces = to_owner(first_parts, slices(first_parts))
    second_pieces = after(slices(second_parts), *w_in)
    later = [slices(parts) for parts in (third_parts, last_parts)]
    far_bases = far[::2]
    gathered, second_pieces, later, cot_b, inverse, near_pieces = tied(
        (gathered, second_pieces, later, cot_b, inverse, near_pieces)
    )
    gains = gathered[tok_count : tok_count + 6].astype(F32).reshape(2, 3, D).sum(axis=1)

    expert_ids = jnp.arange(E, dtype=jnp.int32)
    routes_t = routes.T
    chosen = jnp.any(routes_t[None] == expert_ids[:, None, None], axis=1)
    own_ids = col * local_experts + jnp.arange(local_experts, dtype=jnp.int32)
    own_chosen = jnp.any(routes_t[None] == own_ids[:, None, None], axis=1)
    earlier = (places[:, None] < places[None, :]).astype(BF16)
    rank = plain_dot(own_chosen.astype(BF16), earlier).astype(jnp.int32)
    slot_rank = jnp.where(own_chosen, rank, -1)
    slots = jnp.arange(capacity, dtype=jnp.int32)

    def of_peer(table, step, e):
        return lax.dynamic_slice_in_dim(table, owned_at(peers[step])[0] + e, 1, 0)

    hits = [
        [of_peer(slot_rank, step, e) == slots[:, None] for step in steps]
        for e in range(per_device)
    ]
    picks = [[hit.astype(BF16) for hit in hits[e]] for e in range(per_device)]

    far_ranks = {base: trade(slot_rank.astype(F32), base, n_row) for base in far_bases}

    def swap_small(pieces):
        table = jnp.zeros((n_row,) + pieces[0].shape, pieces[0].dtype)
        for step in steps:
            table = jnp.where(
                jnp.arange(n_row).reshape((-1,) + (1,) * pieces[0].ndim) == peers[step],
                pieces[step][None],
                table,
            )
        table = lax.all_to_all(table, "row", 0, 0, tiled=True)
        return [lax.dynamic_index_in_dim(table, peers[step], 0, False) for step in steps]

    cosine, sine = rope_tables(position)
    q_gain, k_gain = query_gain[None], key_gain[None]
    normed1, scale_in, raw_qk, query_rot, key_rot, values_b = project(
        gathered, gains[:1], weight_heads, q_gain, k_gain, cosine, sine, width_local
    )
    seg_q, seg_k = segment[:, None], jnp.where(key_mask == 1, segment, -1)[None]
    attended_b, log_totals = attend(query_rot, key_rot, values_b, seg_q, seg_k)

    half = D // 2
    out_half = lax.dynamic_slice_in_dim(w_out_own, core * half, half, 0)
    out_half_all = gather_features(after(out_half, *first_pieces[:-1]))

    to_owner(second_parts, second_pieces)
    far_cots = [trade(cot_b, base, n_row) for base in far_bases]
    attended_b = tied(attended_b)
    attended_all = gather_features(after(attended_b, out_half_all))
    third_pieces = to_owner(third_parts, later[0], attended_b, far_cots)
    other_half = trade(after(out_half_all, *w_back), 1, n_row)
    cot_alls = {
        base: gather_features(after(cot, third_pieces[2])) for base, cot in zip(far_bases, far_cots)
    }
    attended_all = tied(attended_all)
    if last_parts:
        to_owner(last_parts, later[1], w_back[0])
    normed2, scale_mid, mixed = run_branch(
        core, col, gathered, attended_all, out_half_all, other_half, gains[1:], feat_local
    )
    cot_alls[0] = gather_features(after(cot_b, normed2))
    normed2 = tied(normed2)
    column_start = col * feat_local

    all_rows = [[None] * n_row for e in range(per_device)]

    def send_rows(e, held, values):
        rows = [plain_dot(picks[e][step], values, BF16) for step in held]
        for step, row_piece in zip(held, rows):
            all_rows[e][step] = trade(row_piece, step, n_row)
        return rows

    sent = [send_rows(0, far, normed2)]
    near_values = after(normed2, sent)
    sent += [send_rows(e, near, near_values) for e in range(per_device)]

    def grad_rows_of(base, cots):
        if not base:
            wanted = [of_peer(slot_rank, step, e) for step in near for e in range(per_device)]
            rows = pick(jnp.concatenate(wanted), cots, capacity)
            return [rows[:per_device], rows[per_device:]]
        table = far_ranks[base]
        halves = []
        for step in near:
            held = []
            for e in range(per_device):
                hit = (of_peer(table, step, e) == slots[:, None].astype(F32)).astype(BF16)
                held.append(plain_dot(hit, cots, BF16))
            halves.append(held)
        return halves

    grad_rows_at = {}

    def hand_on(base, halves):
        grad_rows_at[base] = halves[0]
        grad_rows_at[base + 1] = [trade(piece, 1, n_row) for piece in halves[1]]

    logits = lax.dot_general(
        router_all, after(normed2, sent), (((0,), (1,)), ((), ())), preferred_element_type=F32
    )
    top_logit = jnp.max(jnp.where(chosen, logits, -jnp.inf), axis=0, keepdims=True)
    raised = jnp.where(chosen, jnp.exp(logits - top_logit), 0.0)
    gate_probs = raised / jnp.sum(raised, axis=0, keepdims=True)
    own_probs = lax.dynamic_slice_in_dim(gate_probs, col * local_experts, local_experts, 0)

    slot_gates = []
    for step in steps:
        held = [
            jnp.sum(jnp.where(hits[e][step], of_peer(own_probs, step, e), 0.0), axis=1)
            for e in range(per_device)
        ]
        slot_gates.append(jnp.stack(held))
    slot_gates = swap_small(slot_gates)

    all_rows[0], slot_gates, later_rows = lax.optimization_barrier(
        (all_rows[0], slot_gates, normed2)
    )
    for e in range(1, per_device):
        sent.append(send_rows(e, far, later_rows))
    far_cots = after([cot_alls[base] for base in far_bases], sent, later_rows)
    for base, cots in zip(far_bases, far_cots):
        hand_on(base, grad_rows_of(base, cots))

    both = range(per_device)
    calls, grads_back = {}, [[None] * n_row for e in range(per_device)]

    def gates_of(e, step):
        return jnp.concatenate([slot_gates[step][e], slot_gates[step + 1][e]])[:, None]

    def expert_call(e, step, gates):
        xs = [all_rows[e][step], all_rows[e][step + 1]]
        cs = [grad_rows_at[step][e], grad_rows_at[step + 1][e]]
        act, grad_pre, sums, *back = run_expert(xs, cs, gates, w_in[e], w_back[e])
        calls[e, step] = [xs, cs, [act], [grad_pre], [sums], back]

    def send_back(e, step):
        for i, piece in enumerate(calls[e, step][-1]):
            grads_back[e][step + i] = trade(piece, step + i, n_row)

    def far_calls(e):
        return [calls[e, step] for step in far_bases]

    for step in far_bases:
        expert_call(0, step, gates_of(0, step))
        send_back(0, step)
    for e in range(1, per_device):
        all_rows[e] = after(all_rows[e], far_calls(0))
        for step in far_bases:
            expert_call(e, step, gates_of(e, step))
    every = [(e, step) for e in range(per_device) for step in steps]
    ranks = jnp.concatenate([of_peer(slot_rank, step, e) for e, step in every])
    near_gates = [gates_of(e, 0) for e in both]
    near_cots, near_gates, ranks, _ = lax.optimization_barrier(
        (cot_alls[0], near_gates, ranks, [far_calls(e) for e in both])
    )
    near_halves = grad_rows_of(0, near_cots)
    for e in range(1, per_device):
        held, grads_back[e - 1], near_halves = lax.optimization_barrier(
            (far_calls(e), grads_back[e - 1], near_halves)
        )
        for step, call in zip(far_bases, held):
            calls[e, step] = call
            send_back(e, step)
    hand_on(0, near_halves)
    for e in range(per_device):
        expert_call(e, 0, near_gates[e])
        send_back(e, 0)
    last_near = (per_device - 1, 0)
    calls[last_near], grads_back[-1] = lax.optimization_barrier((calls[last_near], grads_back[-1]))

    def joined(e, which):
        return jnp.concatenate([piece for step in steps[::2] for piece in calls[e, step][which]])

    scalars = [joined(e, 4) for e in range(per_device)]
    scalars = jnp.stack(scalars)
    scalars_back = swap_small(
        [scalars[:, step * capacity : (step + 1) * capacity] for step in steps]
    )
    grad_normed2_part = combine(ranks, [grads_back[e][step] for e, step in every])

    calls = after(calls, grad_normed2_part)
    branch_back, weight_grads = [], []
    for e in range(per_device):
        rows, grad_rows, act, grad_pre = (joined(e, which) for which in range(4))
        out = contract_last(act, w_back[e], BF16)
        branch_back.append(
            trade_all([out[step * capacity : (step + 1) * capacity] for step in steps])
        )
        grad_in = contract_first(rows, grad_pre, BF16)
        weight_grads.append(
            (
                grad_in[:, :unit_count],
                grad_in[:, unit_count:],
                contract_first(grad_rows, act, BF16),
            )
        )
    grad_normed2 = scatter_partial(grad_normed2_part).astype(F32)

    grad_own = jnp.zeros((local_experts, tok_count), F32)
    inner_own = jnp.zeros((1, tok_count), F32)
    own_rows = jnp.arange(local_experts, dtype=jnp.int32)[:, None]
    for e in range(per_device):
        for step in steps:
            expert = owned_at(peers[step])[0] + e
            back = scalars_back[step][e]
            spread = jnp.sum(jnp.where(hits[e][step], back[:, :1], 0.0), axis=0, keepdims=True)
            grad_own = grad_own + jnp.where(own_rows == expert, spread, 0.0)
            inner_own = inner_own + jnp.sum(
                jnp.where(hits[e][step], back[:, 1:], 0.0), axis=0, keepdims=True
            )
    small = jnp.concatenate([grad_own, inner_own], axis=0)
    small, branch_back[0] = lax.optimization_barrier((small, branch_back[0]))
    small = lax.all_to_all(
        jnp.broadcast_to(small.astype(BF16)[None], (n_col,) + small.shape), "col", 0, 0, tiled=True
    )
    small, branch_back = lax.optimization_barrier((small, branch_back))
    small = small.astype(F32)
    grad_gates = small[:, :local_experts].reshape(E, tok_count)
    grad_logits = gate_probs * (
        grad_gates - jnp.sum(gate_probs * grad_gates, axis=0, keepdims=True)
    )
    grad_logits = grad_logits.astype(BF16)
    inner_mid = jnp.sum(small[:, local_experts], axis=0) + jnp.sum(
        grad_logits.astype(F32) * logits, axis=0
    )
    inner_mid = (inner_mid / D)[:, None]
    grad_router = lax.dot_general(
        normed2, grad_logits, (((0,), (1,)), ((), ())), preferred_element_type=F32
    )
    router_local = lax.dynamic_slice_in_dim(router_all, column_start, feat_local, 0)
    grad_unit_mid = grad_normed2 + lax.dot_general(
        grad_logits, router_local, (((0,), (1,)), ((), ())), preferred_element_type=F32
    )
    unit_mid = mixed * scale_mid
    grad_norm2 = jnp.sum(grad_unit_mid * unit_mid, axis=0)
    scaled_mid = grad_unit_mid * norm2_gain
    grad_mixed = cot_b.astype(F32) + scale_mid * (scaled_mid - unit_mid * inner_mid)
    def held_slices(which, experts):
        return [
            jnp.stack(
                [
                    lax.dynamic_slice_in_dim(
                        weight_grads[e][which], peers[step] * rows_local, rows_local, 0
                    )
                    for e in experts
                ]
            )
            for step in steps
        ]

    def to_holders(pieces, *earlier):
        return trade_all(after(pieces, *earlier))

    gate_slices, up_slices = held_slices(0, both), held_slices(1, both)
    grad_mixed_b, gate_slices, up_slices = lax.optimization_barrier(
        (grad_mixed.astype(BF16), gate_slices, up_slices)
    )
    grad_branch = gather_features(grad_mixed_b)
    gate_pieces = to_holders(gate_slices)

    def to_rows(pieces):
        flat, places = [], []
        for e, held in enumerate(pieces):
            for step in steps:
                first, _, unit = owned_at(peers[step])
                flat.append(held[step])
                places += [first + e, unit]
        return place(jnp.stack(places), flat, local_experts, hidden_units)

    def sum_cores(grad):
        parts = [
            lax.dynamic_slice_in_dim(grad, peers[step] * rows_local, rows_local, 0)
            for step in steps
        ]
        other = trade(jnp.stack(parts[1::2]), 1, n_row).astype(F32)
        sums = [part.astype(F32) + other[i] for i, part in enumerate(parts[::2])]
        return [sums[0]] + [part.astype(grad.dtype) for part in sums[1:]]

    def sum_chips(sums):
        total = sums[0]
        for part, base in zip(sums[1:], far_bases):
            total = total + trade(part, base, n_row).astype(F32)
        return total

    def sum_groups(grad, *earlier):
        return sum_chips(sum_cores(after(grad, *earlier)))

    combined_part = combine(ranks, [branch_back[e][step] for e, step in every])
    grad_branch, gate_pieces, combined_part = lax.optimization_barrier(
        (grad_branch, gate_pieces, combined_part)
    )
    up_pieces = to_holders(up_slices, gate_pieces)

    combined = scatter_partial(combined_part)

    grad_w_out = contract_first(grad_branch, attended_b, BF16)
    grad_w_gate = to_rows([gate_pieces])
    grad_attended = plain_dot(after(grad_branch, grad_w_gate), w_out_own, BF16)
    grad_q, grad_k, grad_v, grad_query_gain, grad_key_gain = attend_back(
        query_rot, key_rot, values_b, grad_attended, log_totals, seg_q, seg_k, raw_qk,
        q_gain, k_gain, cosine, sine,
    )
    grad_qkv = jnp.concatenate([grad_q, grad_k, grad_v], axis=1)
    grad_w_out = sum_groups(grad_w_out)
    grad_router = sum_groups(grad_router, grad_branch).T
    down_slices = [held_slices(2, [e]) for e in range(per_device)]
    grad_qkv, up_pieces, combined, down_slices, grad_w_out, grad_router = (
        lax.optimization_barrier(
            (grad_qkv, up_pieces, combined, down_slices, grad_w_out, grad_router)
        )
    )
    down_pieces = [to_holders(down_slices[0])]
    grad_normed1_part = through_heads(grad_qkv, weight_heads)
    grad_unit_in = scatter_partial(grad_normed1_part)
    output = (mixed + combined.astype(F32)).astype(BF16)[inverse]
    grad_w_up = to_rows([up_pieces])
    grad_normed1_part, down_pieces, output, grad_w_up = lax.optimization_barrier(
        (grad_normed1_part, down_pieces, output, grad_w_up)
    )
    down_pieces += [to_holders(held, down_pieces) for held in down_slices[1:]]
    inner_in = jnp.sum(
        grad_qkv.astype(F32) * jnp.concatenate([raw_qk, values_b.astype(F32)], axis=1), axis=1
    )
    packed = packed_b.astype(F32)
    unit_in = packed * scale_in
    unit_all = gathered[:tok_count].astype(F32) * scale_in
    grad_norm1 = jnp.sum(grad_normed1_part.astype(F32) * unit_all, axis=0)
    def for_all(vector):
        return jnp.broadcast_to(vector[None], (n_col,) + vector.shape)

    vectors = jnp.concatenate(
        [
            for_all(inner_in),
            for_all(grad_query_gain[0]),
            for_all(grad_key_gain[0]),
            grad_norm1.reshape(n_col, feat_local),
        ],
        axis=1,
    )
    heads_sums = sum_cores(contract_first(normed1, grad_qkv, BF16))
    vectors, heads_sums = lax.optimization_barrier((vectors, heads_sums))
    vectors = jnp.sum(lax.all_to_all(vectors, "col", 0, 0, tiled=True), axis=0)
    vectors, down_pieces, heads_sums = lax.optimization_barrier(
        (vectors, down_pieces, heads_sums)
    )
    inner_in = vectors[:tok_count, None] / D
    vectors = jnp.concatenate([vectors[tok_count:], grad_norm2])
    vectors = sum(trade(vectors, step, n_row) for step in steps)
    grad_heads = sum_chips(heads_sums)
    grad_unit_in, vectors, inner_in, grad_heads = lax.optimization_barrier(
        (grad_unit_in, vectors, inner_in, grad_heads)
    )
    grad_unit_in = grad_unit_in.astype(F32)
    scaled_in = grad_unit_in * norm1_gain
    grad_input = (grad_mixed + scale_in * (scaled_in - unit_in * inner_in))[inverse]

    grad_w_query, grad_w_key, grad_w_value = (
        grad_heads[:, i * width_local : (i + 1) * width_local] for i in range(3)
    )
    grad_w_down = to_rows(down_pieces)

    grad_query_gain, grad_key_gain = vectors[:DH], vectors[DH : 2 * DH]
    grad_norm1 = vectors[2 * DH : 2 * DH + feat_local]
    grad_norm2 = vectors[2 * DH + feat_local :]
    return (
        output,
        grad_input,
        grad_norm1,
        grad_query_gain,
        grad_key_gain,
        grad_w_query,
        grad_w_key,
        grad_w_value,
        grad_w_out,
        grad_norm2,
        grad_router,
        grad_w_gate,
        grad_w_up,
        grad_w_down,
    )


def solution(mesh):
    return jax.shard_map(
        body,
        mesh=mesh,
        in_specs=(
            P("row", "col"),
            P("row", None),
            P("row", None),
            P("row"),
            P("row", None),
            P("col"),
            P(),
            P(),
            P("row", "col"),
            P("row", "col"),
            P("row", "col"),
            P("row", "col"),
            P("col"),
            P(None, "row"),
            P("col", "row", None),
            P("col", "row", None),
            P("col", "row", None),
            P("row", "col"),
        ),
        out_specs=(
            P("row", "col"),
            P("row", "col"),
            P("col"),
            P(),
            P(),
            P("row", "col"),
            P("row", "col"),
            P("row", "col"),
            P("row", "col"),
            P("col"),
            P(None, "row"),
            P("col", "row", None),
            P("col", "row", None),
            P("col", "row", None),
        ),
        check_vma=False,
    )
```

```python
import jax
import jax.numpy as jnp
from jax import lax
from jax.experimental import pallas as pl
from jax.experimental.pallas import tpu as pltpu
from jax.sharding import PartitionSpec as P

D = 2048
DH = 128
E = 64
TOP = 8


EPSILON = 1e-06
ROPE_BASE = 10000.0
BF16 = jnp.bfloat16
F32 = jnp.float32


def layout(seq_lengths, tok_count):
    seq_ends = jnp.cumsum(seq_lengths)
    seq_starts = seq_ends - seq_lengths
    places = jnp.arange(tok_count, dtype=jnp.int32)
    segment = jnp.sum((places[:, None] >= seq_ends[None, :]).astype(jnp.int32), axis=1)
    member = segment[:, None] == jnp.arange(seq_lengths.shape[0], dtype=jnp.int32)[None, :]
    offset = jnp.sum(jnp.where(member, seq_starts[None, :], 0), axis=1)
    return (segment, places - offset)


def rope_tables(position):
    half_dim = DH // 2
    frequency = ROPE_BASE ** (-2.0 * jnp.arange(half_dim, dtype=F32) / DH)
    angles = position.astype(F32)[:, None] * frequency[None, :]
    cosine, sine = jnp.cos(angles), jnp.sin(angles)
    return jnp.concatenate([cosine, cosine], 1), jnp.concatenate([-sine, sine], 1)


def gather_features(local_rows):
    return lax.all_gather(local_rows, "col", axis=1, tiled=True)


def scatter_partial(partial_rows):
    return lax.psum_scatter(partial_rows, "col", scatter_dimension=1, tiled=True)


def trade(value, step, n_row):
    if step == 0:
        return value
    return lax.ppermute(value, "row", [(r, r ^ step) for r in range(n_row)])


def trade_all(pieces):
    return [trade(piece, step, len(pieces)) for step, piece in enumerate(pieces)]


def contract_last(left_op, right_op, kind=F32):
    return lax.dot_general(
        left_op, right_op, (((1,), (1,)), ((), ())), preferred_element_type=F32
    ).astype(kind)


def contract_first(left_op, right_op, kind=F32):
    return lax.dot_general(
        left_op, right_op, (((0,), (0,)), ((), ())), preferred_element_type=F32
    ).astype(kind)


def plain_dot(left_op, right_op, kind=F32):
    return jnp.dot(left_op, right_op, preferred_element_type=F32).astype(kind)


def after(value, *earlier):
    return lax.optimization_barrier((value, *earlier))[0]


def thirds(values):
    high = lax.reduce_precision(values, 8, 7)
    middle = lax.reduce_precision(values - high, 8, 7)
    return jnp.stack([high, middle, values - high - middle]).astype(BF16)


def cost(flops, moved):
    return pl.CostEstimate(flops=flops, bytes_accessed=moved, transcendentals=0)


def rope(values, cosine, sine):
    return values * cosine + pltpu.roll(values, DH // 2, 1) * sine


def rope_back(grad, cosine, sine):
    return grad * cosine + pltpu.roll(grad * sine, DH // 2, 1)


def project_kernel(x_ref, gain_ref, w_ref, qg_ref, kg_ref, cos_ref, sin_ref, *outs):
    normed_ref, scale_ref, raw_ref, q_ref, k_ref, v_ref = outs
    x = x_ref[...].astype(F32)
    scale = lax.rsqrt(jnp.mean(x * x, axis=1, keepdims=True) + EPSILON)
    normed = (x * scale * gain_ref[...]).astype(BF16)
    normed_ref[...] = normed
    scale_ref[...] = scale
    width = q_ref.shape[1]
    qkv = jnp.dot(normed, w_ref[:, : 3 * width], preferred_element_type=F32)
    raw_ref[...] = qkv[:, : 2 * width]
    v_ref[...] = qkv[:, 2 * width :].astype(BF16)
    cosine, sine = cos_ref[...], sin_ref[...]
    for part, gain, out in ((0, qg_ref, q_ref), (1, kg_ref, k_ref)):
        for h in range(width // DH):
            head = qkv[:, part * width + h * DH : part * width + (h + 1) * DH]
            size = lax.rsqrt(jnp.mean(head * head, axis=1, keepdims=True) + EPSILON)
            out[:, h * DH : (h + 1) * DH] = rope(head * size * gain[...], cosine, sine).astype(BF16)


def project(x, gain, w, q_gain, k_gain, cosine, sine, width, block=256):
    rows = cosine.shape[0]
    by_rows = lambda n: pl.BlockSpec((block, n), lambda i: (i, 0))
    whole = lambda a: pl.BlockSpec(a.shape, lambda i: (0, 0))
    return pl.pallas_call(
        project_kernel,
        name="project",
        grid=(rows // block,),
        in_specs=[
            by_rows(D),
            whole(gain),
            whole(w),
            whole(q_gain),
            whole(k_gain),
            by_rows(DH),
            by_rows(DH),
        ],
        out_specs=[by_rows(n) for n in (D, 1, 2 * width, width, width, width)],
        out_shape=[
            jax.ShapeDtypeStruct((rows, D), BF16),
            jax.ShapeDtypeStruct((rows, 1), F32),
            jax.ShapeDtypeStruct((rows, 2 * width), F32),
            jax.ShapeDtypeStruct((rows, width), BF16),
            jax.ShapeDtypeStruct((rows, width), BF16),
            jax.ShapeDtypeStruct((rows, width), BF16),
        ],
        cost_estimate=cost(1000, 1000),
    )(x, gain, w, q_gain, k_gain, cosine, sine)


def masked_scores(q, k, seg_q, seg_k, first):
    scores = lax.dot_general(q, k, (((1,), (1,)), ((), ())), preferred_element_type=F32)
    rows = first + lax.broadcasted_iota(jnp.int32, scores.shape, 0)
    columns = lax.broadcasted_iota(jnp.int32, scores.shape, 1)
    allowed = (seg_q == seg_k) | (rows == columns)
    return jnp.where(allowed, scores * DH ** (-0.5), -1e30)


def attend_kernel(q_ref, k_ref, v_ref, seg_q_ref, seg_k_ref, out_ref, log_ref):
    first = pl.program_id(1) * q_ref.shape[0]
    scores = masked_scores(q_ref[...], k_ref[...], seg_q_ref[...], seg_k_ref[...], first)
    top = jnp.max(scores, axis=1, keepdims=True)
    terms = jnp.exp(scores - top)
    total = jnp.sum(terms, axis=1, keepdims=True)
    weights = (terms * (1.0 / total)).astype(BF16)
    out_ref[...] = jnp.dot(weights, v_ref[...], preferred_element_type=F32).astype(BF16)
    log_ref[0] = top + jnp.log(total)


def attend(q, k, v, seg_q, seg_k, block=256):
    rows, width = q.shape
    heads = width // DH
    by_rows = pl.BlockSpec((block, DH), lambda h, i: (i, h))
    whole = pl.BlockSpec((rows, DH), lambda h, i: (0, h))
    return pl.pallas_call(
        attend_kernel,
        name="attend",
        grid=(heads, rows // block),
        in_specs=[
            by_rows,
            whole,
            whole,
            pl.BlockSpec((block, 1), lambda h, i: (i, 0)),
            pl.BlockSpec((1, rows), lambda h, i: (0, 0)),
        ],
        out_specs=[by_rows, pl.BlockSpec((1, block, 1), lambda h, i: (h, i, 0))],
        out_shape=[
            jax.ShapeDtypeStruct((rows, width), BF16),
            jax.ShapeDtypeStruct((heads, rows, 1), F32),
        ],
        cost_estimate=cost(1000, 1000),
    )(q, k, v, seg_q, seg_k)


def head_back(grad, raw, gain, cosine, sine):
    grad = rope_back(grad, cosine, sine)
    size = lax.rsqrt(jnp.mean(raw * raw, axis=1, keepdims=True) + EPSILON)
    unit = raw * size
    grad_gain = jnp.sum(grad * unit, axis=0, keepdims=True)
    grad = grad * gain
    return size * (grad - unit * jnp.mean(grad * unit, axis=1, keepdims=True)), grad_gain


def attend_back_kernel(
    q_ref, k_ref, v_ref, grad_ref, log_ref, seg_q_ref, seg_k_ref, raw_q_ref, raw_k_ref,
    qg_ref, kg_ref, cos_q_ref, sin_q_ref, cos_ref, sin_ref,
    dq_ref, dk_ref, dv_ref, dqg_ref, dkg_ref, sum_k, sum_v,
):
    head, i = pl.program_id(0), pl.program_id(1)

    @pl.when((head == 0) & (i == 0))
    def _():
        dqg_ref[...] = jnp.zeros_like(dqg_ref)
        dkg_ref[...] = jnp.zeros_like(dkg_ref)

    @pl.when(i == 0)
    def _():
        sum_k[...] = jnp.zeros_like(sum_k)
        sum_v[...] = jnp.zeros_like(sum_v)

    q, k, grad = q_ref[...], k_ref[...], grad_ref[...]
    scores = masked_scores(q, k, seg_q_ref[...], seg_k_ref[...], i * q.shape[0])
    probs = jnp.exp(scores - log_ref[0])
    sum_v[...] += lax.dot_general(
        probs.astype(BF16), grad, (((0,), (0,)), ((), ())), preferred_element_type=F32
    )
    grad_probs = lax.dot_general(
        grad, v_ref[...], (((1,), (1,)), ((), ())), preferred_element_type=F32
    )
    inner = jnp.sum(probs * grad_probs, axis=1, keepdims=True)
    grad_scores = (probs * (grad_probs - inner)).astype(BF16)
    sum_k[...] += lax.dot_general(
        grad_scores, q, (((0,), (0,)), ((), ())), preferred_element_type=F32
    )
    grad_q = jnp.dot(grad_scores, k, preferred_element_type=F32) * DH ** (-0.5)
    grad_q, grad_gain = head_back(
        grad_q, raw_q_ref[...], qg_ref[...], cos_q_ref[...], sin_q_ref[...]
    )
    dq_ref[...] = grad_q.astype(BF16)
    dqg_ref[...] += grad_gain

    @pl.when(i == pl.num_programs(1) - 1)
    def _():
        grad_k, gain_k = head_back(
            sum_k[...] * DH ** (-0.5), raw_k_ref[...], kg_ref[...], cos_ref[...], sin_ref[...]
        )
        dk_ref[...] = grad_k.astype(BF16)
        dkg_ref[...] += gain_k
        dv_ref[...] = sum_v[...].astype(BF16)


def attend_back(q, k, v, grad, logs, seg_q, seg_k, raw, q_gain, k_gain, cosine, sine, block=256):
    rows, width = q.shape
    heads = width // DH
    by_rows = pl.BlockSpec((block, DH), lambda h, i: (i, h))
    whole = pl.BlockSpec((rows, DH), lambda h, i: (0, h))
    gain = pl.BlockSpec((1, DH), lambda h, i: (0, 0))
    return pl.pallas_call(
        attend_back_kernel,
        name="attend_back",
        grid=(heads, rows // block),
        in_specs=[
            by_rows,
            whole,
            whole,
            by_rows,
            pl.BlockSpec((1, block, 1), lambda h, i: (h, i, 0)),
            pl.BlockSpec((block, 1), lambda h, i: (i, 0)),
            pl.BlockSpec((1, rows), lambda h, i: (0, 0)),
            by_rows,
            pl.BlockSpec((rows, DH), lambda h, i: (0, heads + h)),
            gain,
            gain,
            pl.BlockSpec((block, DH), lambda h, i: (i, 0)),
            pl.BlockSpec((block, DH), lambda h, i: (i, 0)),
            pl.BlockSpec((rows, DH), lambda h, i: (0, 0)),
            pl.BlockSpec((rows, DH), lambda h, i: (0, 0)),
        ],
        out_specs=[by_rows, whole, whole, gain, gain],
        out_shape=[
            jax.ShapeDtypeStruct((rows, width), BF16),
            jax.ShapeDtypeStruct((rows, width), BF16),
            jax.ShapeDtypeStruct((rows, width), BF16),
            jax.ShapeDtypeStruct((1, DH), F32),
            jax.ShapeDtypeStruct((1, DH), F32),
        ],
        scratch_shapes=[pltpu.VMEM((rows, DH), F32), pltpu.VMEM((rows, DH), F32)],
        cost_estimate=cost(1000, 1000),
    )(q, k, v, grad, logs, seg_q, seg_k, raw, raw, q_gain, k_gain, cosine, sine, cosine, sine)


def branch_kernel(
    at_ref, x_ref, att_ref, own_ref, other_ref, gain_ref, normed_ref, scale_ref, mixed_ref, total
):
    half = own_ref.shape[0]
    own = contract_last(att_ref[...], own_ref[...])
    other = contract_last(att_ref[...], other_ref[...])
    second = at_ref[0] == 1
    total[:, :half] = x_ref[:, :half].astype(F32) + jnp.where(second, other, own)
    total[:, half:] = x_ref[:, half:].astype(F32) + jnp.where(second, own, other)
    mixed = total[...]
    scale = lax.rsqrt(jnp.mean(mixed * mixed, axis=1, keepdims=True) + EPSILON)
    normed_ref[...] = (mixed * scale * gain_ref[...]).astype(BF16)
    scale_ref[...] = scale
    width = mixed_ref.shape[1]
    mixed_ref[...] = total[:, pl.ds(pl.multiple_of(at_ref[1] * width, 128), width)]


def run_branch(core, col, x, attended, own, other, gain, width, block=256):
    rows = attended.shape[0]
    by_rows = lambda n: pl.BlockSpec((block, n), lambda i, at: (i, 0))
    whole = lambda a: pl.BlockSpec(a.shape, lambda i, at: (0, 0))
    return pl.pallas_call(
        branch_kernel,
        name="branch",
        grid_spec=pltpu.PrefetchScalarGridSpec(
            num_scalar_prefetch=1,
            grid=(rows // block,),
            in_specs=[by_rows(D), by_rows(D), whole(own), whole(other), whole(gain)],
            out_specs=[by_rows(D), by_rows(1), by_rows(width)],
            scratch_shapes=[pltpu.VMEM((block, D), F32)],
        ),
        out_shape=[
            jax.ShapeDtypeStruct((rows, D), BF16),
            jax.ShapeDtypeStruct((rows, 1), F32),
            jax.ShapeDtypeStruct((rows, width), F32),
        ],
        cost_estimate=cost(1000, 1000),
    )(jnp.stack([core, col]), x, attended, own, other, gain)


def expert_kernel(
    x0_ref, x1_ref, c0_ref, c1_ref, gate_ref, w_ref, wd_ref,
    act_ref, grad_ref, sums_ref, dx0_ref, dx1_ref,
):
    width = act_ref.shape[1]
    slot_gate = gate_ref[...]
    rows = jnp.concatenate([x0_ref[...], x1_ref[...]], axis=0)
    pre = jnp.dot(rows, w_ref[...], preferred_element_type=F32)
    gate, up = pre[:, :width], pre[:, width:]
    cots = jnp.concatenate([c0_ref[...], c1_ref[...]], axis=0)
    grad = jnp.dot(cots, wd_ref[...], preferred_element_type=F32)
    opened = 1.0 / (1.0 + jnp.exp(-gate))
    silu = gate * opened
    act = silu * up
    act_ref[...] = (slot_gate * act).astype(BF16)
    grad_gate = jnp.sum(act * grad, axis=1, keepdims=True)
    grad = slot_gate * grad
    dgate = (grad * up * opened * (1.0 + gate * (1.0 - opened))).astype(BF16)
    dup = (grad * silu).astype(BF16)
    grad_ref[:, :width] = dgate
    grad_ref[:, width:] = dup
    inner = jnp.sum(dgate.astype(F32) * gate + dup.astype(F32) * up, axis=1, keepdims=True)
    sums_ref[:, 0:1] = grad_gate
    sums_ref[:, 1:2] = inner
    back = contract_last(grad_ref[...], w_ref[...], BF16)
    dx0_ref[...] = back[: dx0_ref.shape[0]]
    dx1_ref[...] = back[dx0_ref.shape[0] :]


def run_expert(xs, cs, slot_gate, w, wd):
    capacity, width = xs[0].shape[0], wd.shape[1]
    slots = 2 * capacity
    operands = [*xs, *cs, slot_gate, w, wd]
    outs = [(slots, width, BF16), (slots, 2 * width, BF16), (slots, 2, F32)]
    outs += [(capacity, D, BF16)] * 2
    whole = lambda shape: pl.BlockSpec(shape, lambda i: (0, 0), pipeline_mode=pl.Buffered(1))
    return pl.pallas_call(
        expert_kernel,
        name="expert",
        grid=(1,),
        in_specs=[whole(a.shape) for a in operands],
        out_specs=[pl.BlockSpec(out[:2], lambda i: (0, 0)) for out in outs],
        out_shape=[jax.ShapeDtypeStruct(out[:2], out[2]) for out in outs],
        cost_estimate=cost(1000, 1000),
    )(*operands)


def through_heads_kernel(grad_ref, w_ref, out_ref):
    width = grad_ref.shape[1]
    out_ref[...] = contract_last(grad_ref[...], w_ref[:, :width], BF16)


def through_heads(grad, w, block=768):
    rows, width = grad.shape
    return pl.pallas_call(
        through_heads_kernel,
        name="through_heads",
        grid=(rows // block,),
        in_specs=[
            pl.BlockSpec((block, width), lambda i: (i, 0)),
            pl.BlockSpec(w.shape, lambda i: (0, 0)),
        ],
        out_specs=pl.BlockSpec((block, D), lambda i: (i, 0)),
        out_shape=jax.ShapeDtypeStruct((rows, D), BF16),
        cost_estimate=cost(1000, 1000),
    )(grad, w)


def pick_kernel(rank_ref, value_ref, *refs):
    hits_ref = refs[-1]
    pieces = refs[:-1]
    capacity = pieces[0].shape[0]

    @pl.when(pl.program_id(0) == 0)
    def _():
        slots = lax.broadcasted_iota(jnp.int32, (capacity, hits_ref.shape[1]), 0)
        for i in range(len(pieces)):
            hits = (slots == rank_ref[i : i + 1, :]).astype(BF16)
            hits_ref[i * capacity : (i + 1) * capacity, :] = hits

    rows = jnp.dot(hits_ref[...], value_ref[...], preferred_element_type=F32).astype(BF16)
    for i, piece in enumerate(pieces):
        piece[...] = rows[i * capacity : (i + 1) * capacity]


def pick(ranks, values, capacity, block=512):
    pieces, rows = ranks.shape
    by_width = lambda n: pl.BlockSpec((n, block), lambda j: (0, j))
    return pl.pallas_call(
        pick_kernel,
        name="pick",
        grid=(D // block,),
        in_specs=[pl.BlockSpec(ranks.shape, lambda j: (0, 0)), by_width(rows)],
        out_specs=[by_width(capacity)] * pieces,
        out_shape=[jax.ShapeDtypeStruct((capacity, D), BF16)] * pieces,
        scratch_shapes=[pltpu.VMEM((pieces * capacity, rows), BF16)],
        cost_estimate=cost(1000, 1000),
    )(ranks, values)


def combine_kernel(*refs):
    rank_ref, out_ref = refs[0], refs[-1]
    pieces = refs[1:-1]
    total = 0.0
    for i, piece in enumerate(pieces):
        shape = (piece.shape[0], out_ref.shape[0])
        slots = lax.broadcasted_iota(jnp.int32, shape, 0)
        hits = (slots == rank_ref[i : i + 1, :]).astype(BF16)
        total = total + contract_first(hits, piece[...])
    out_ref[...] = total.astype(BF16)


def combine(ranks, pieces, block=768):
    rows = ranks.shape[1]
    width = 1024
    whole = lambda a: pl.BlockSpec((a.shape[0], width), lambda j, i: (0, j))
    return pl.pallas_call(
        combine_kernel,
        name="combine",
        grid=(D // width, rows // block),
        in_specs=[pl.BlockSpec((len(pieces), block), lambda j, i: (0, i))]
        + [whole(piece) for piece in pieces],
        out_specs=pl.BlockSpec((block, width), lambda j, i: (i, j)),
        out_shape=jax.ShapeDtypeStruct((rows, D), BF16),
        cost_estimate=cost(1000, 1000),
    )(ranks, *pieces)


def place_kernel(at_ref, *refs):
    out_ref = refs[-1]
    for i, piece in enumerate(refs[:-1]):
        experts, _, units = piece.shape
        first, unit = at_ref[2 * i], pl.multiple_of(at_ref[2 * i + 1], 128)
        for e in range(experts):
            out_ref[first + e, :, pl.ds(unit, units)] = piece[e].astype(F32)


def place(places, pieces, experts, units, block=64):
    rows = pieces[0].shape[1]
    spec = lambda a: pl.BlockSpec((a.shape[0], block, a.shape[2]), lambda i, at: (0, i, 0))
    return pl.pallas_call(
        place_kernel,
        name="place",
        grid_spec=pltpu.PrefetchScalarGridSpec(
            num_scalar_prefetch=1,
            grid=(rows // block,),
            in_specs=[spec(piece) for piece in pieces],
            out_specs=pl.BlockSpec((experts, block, units), lambda i, at: (0, i, 0)),
        ),
        out_shape=jax.ShapeDtypeStruct((experts, rows, units), F32),
        cost_estimate=cost(1000, 1000),
    )(places, *pieces)


def body(
    hidden_in,
    token_order,
    lengths,
    key_mask,
    routes,
    norm1_gain,
    query_gain,
    key_gain,
    w_query,
    w_key,
    w_value,
    w_out,
    norm2_gain,
    router,
    w_gate,
    w_up,
    w_down,
    cotangent,
):
    tok_count, feat_local = hidden_in.shape
    n_row = D // w_query.shape[0]
    n_col = D // feat_local
    local_experts, _, hidden_units = w_gate.shape
    per_device = max(1, local_experts // n_row)
    unit_split = max(1, n_row // local_experts)
    capacity = 5 * tok_count * TOP // (4 * E)
    col = lax.axis_index("col")
    row = lax.axis_index("row")
    core = row % 2
    steps = range(n_row)
    peers = [row ^ step for step in steps]
    near, far = list(steps)[:2], list(steps)[2:]
    rows_local = D // n_row
    unit_count = hidden_units // unit_split
    places = jnp.arange(tok_count, dtype=jnp.int32)
    order_row = token_order[0]
    inverse = jnp.zeros((tok_count,), jnp.int32).at[order_row].set(places)
    segment, position = layout(lengths[0], tok_count)

    packed_b = hidden_in[order_row]
    gains_b = jnp.concatenate([thirds(norm1_gain), thirds(norm2_gain)])
    gathered = gather_features(jnp.concatenate([packed_b, jnp.pad(gains_b, ((0, 10), (0, 0)))]))
    cot_b = cotangent[order_row]

    width_local = w_query.shape[1]
    head_count = width_local // DH
    weight_rows = jnp.concatenate([w_query, w_key, w_value, w_out, router.T], axis=1)
    weight_pieces = {step: trade(weight_rows, step, n_row) for step in steps if step % 2 == 0}
    for step in steps:
        if step % 2 == 1:
            weight_pieces[step] = trade(weight_pieces[step ^ 1], 1, n_row)
    weight_heads = jnp.zeros((D, weight_rows.shape[1]), BF16)
    for step in steps:
        weight_heads = lax.dynamic_update_slice(
            weight_heads, weight_pieces[step], (peers[step] * rows_local, 0)
        )
    w_qkv = weight_heads[:, : 3 * width_local]
    w_out_own = weight_heads[:, 3 * width_local : 4 * width_local]
    router_all = weight_heads[:, 4 * width_local :]

    def owned_at(peer):
        return (peer * per_device // unit_split, 0, (peer % unit_split) * unit_count)

    all_weights = (w_gate, w_up, w_down)
    all_parts = [(which, e) for which in range(3) for e in range(per_device)]
    owned = {}
    w_in = [jnp.zeros((D, 2 * unit_count), BF16) for e in range(per_device)]
    w_back = [jnp.zeros((D, unit_count), BF16) for e in range(per_device)]

    def slices(parts):
        pieces = []
        for step in steps if parts else ():
            first, _, unit = owned_at(peers[step])
            held = [
                lax.dynamic_slice(
                    all_weights[which], (first + e, 0, unit), (1, rows_local, unit_count)
                )
                for which, e in parts
            ]
            pieces.append(jnp.concatenate(held))
        return pieces

    def to_owner(parts, pieces, *earlier):
        pieces = after(pieces, *earlier)
        pieces = [
            None if step == 1 else trade(pieces[step], step, n_row) for step in steps
        ]
        pieces[1] = jnp.stack([near_pieces[all_parts.index(part)] for part in parts])
        for i, (which, e) in enumerate(parts):
            for step in steps:
                at = (peers[step] * rows_local, unit_count if which == 1 else 0)
                if which < 2:
                    w_in[e] = lax.dynamic_update_slice(w_in[e], pieces[step][i], at)
                else:
                    w_back[e] = lax.dynamic_update_slice(w_back[e], pieces[step][i], at)
        return pieces

    def tied(value):
        value, w_in[:], w_back[:] = lax.optimization_barrier((value, w_in[:], w_back[:]))
        return value

    first_parts, second_parts = all_parts[:per_device], all_parts[per_device : per_device + 1]
    third_parts = all_parts[per_device + 1 : 2 * per_device + 1]
    last_parts = all_parts[2 * per_device + 1 :]
    near_pieces = trade(slices(all_parts)[1], 1, n_row)
    first_pieces = to_owner(first_parts, slices(first_parts))
    second_pieces = after(slices(second_parts), *w_in)
    later = [slices(parts) for parts in (third_parts, last_parts)]
    far_bases = far[::2]
    gathered, second_pieces, later, cot_b, inverse, near_pieces = tied(
        (gathered, second_pieces, later, cot_b, inverse, near_pieces)
    )
    gains = gathered[tok_count : tok_count + 6].astype(F32).reshape(2, 3, D).sum(axis=1)

    expert_ids = jnp.arange(E, dtype=jnp.int32)
    routes_t = routes.T
    chosen = jnp.any(routes_t[None] == expert_ids[:, None, None], axis=1)
    own_ids = col * local_experts + jnp.arange(local_experts, dtype=jnp.int32)
    own_chosen = jnp.any(routes_t[None] == own_ids[:, None, None], axis=1)
    earlier = (places[:, None] < places[None, :]).astype(BF16)
    rank = plain_dot(own_chosen.astype(BF16), earlier).astype(jnp.int32)
    slot_rank = jnp.where(own_chosen, rank, -1)
    slots = jnp.arange(capacity, dtype=jnp.int32)

    def of_peer(table, step, e):
        return lax.dynamic_slice_in_dim(table, owned_at(peers[step])[0] + e, 1, 0)

    hits = [
        [of_peer(slot_rank, step, e) == slots[:, None] for step in steps]
        for e in range(per_device)
    ]
    picks = [[hit.astype(BF16) for hit in hits[e]] for e in range(per_device)]

    far_ranks = {base: trade(slot_rank.astype(F32), base, n_row) for base in far_bases}

    def swap_small(pieces):
        table = jnp.zeros((n_row,) + pieces[0].shape, pieces[0].dtype)
        for step in steps:
            table = jnp.where(
                jnp.arange(n_row).reshape((-1,) + (1,) * pieces[0].ndim) == peers[step],
                pieces[step][None],
                table,
            )
        table = lax.all_to_all(table, "row", 0, 0, tiled=True)
        return [lax.dynamic_index_in_dim(table, peers[step], 0, False) for step in steps]

    cosine, sine = rope_tables(position)
    q_gain, k_gain = query_gain[None], key_gain[None]
    normed1, scale_in, raw_qk, query_rot, key_rot, values_b = project(
        gathered, gains[:1], weight_heads, q_gain, k_gain, cosine, sine, width_local
    )
    seg_q, seg_k = segment[:, None], jnp.where(key_mask == 1, segment, -1)[None]
    attended_b, log_totals = attend(query_rot, key_rot, values_b, seg_q, seg_k)

    half = D // 2
    out_half = lax.dynamic_slice_in_dim(w_out_own, core * half, half, 0)
    out_half_all = gather_features(after(out_half, *first_pieces[:-1]))

    to_owner(second_parts, second_pieces)
    far_cots = [trade(cot_b, base, n_row) for base in far_bases]
    attended_b = tied(attended_b)
    attended_all = gather_features(after(attended_b, out_half_all))
    third_pieces = to_owner(third_parts, later[0], attended_b, far_cots)
    other_half = trade(after(out_half_all, *w_back), 1, n_row)
    cot_alls = {
        base: gather_features(after(cot, third_pieces[2])) for base, cot in zip(far_bases, far_cots)
    }
    attended_all = tied(attended_all)
    if last_parts:
        to_owner(last_parts, later[1], w_back[0])
    normed2, scale_mid, mixed = run_branch(
        core, col, gathered, attended_all, out_half_all, other_half, gains[1:], feat_local
    )
    cot_alls[0] = gather_features(after(cot_b, normed2))
    normed2 = tied(normed2)
    column_start = col * feat_local

    all_rows = [[None] * n_row for e in range(per_device)]

    def send_rows(e, held, values):
        rows = [plain_dot(picks[e][step], values, BF16) for step in held]
        for step, row_piece in zip(held, rows):
            all_rows[e][step] = trade(row_piece, step, n_row)
        return rows

    sent = [send_rows(0, far, normed2)]
    near_values = after(normed2, sent)
    sent += [send_rows(e, near, near_values) for e in range(per_device)]

    def grad_rows_of(base, cots):
        if not base:
            wanted = [of_peer(slot_rank, step, e) for step in near for e in range(per_device)]
            rows = pick(jnp.concatenate(wanted), cots, capacity)
            return [rows[:per_device], rows[per_device:]]
        table = far_ranks[base]
        halves = []
        for step in near:
            held = []
            for e in range(per_device):
                hit = (of_peer(table, step, e) == slots[:, None].astype(F32)).astype(BF16)
                held.append(plain_dot(hit, cots, BF16))
            halves.append(held)
        return halves

    grad_rows_at = {}

    def hand_on(base, halves):
        grad_rows_at[base] = halves[0]
        grad_rows_at[base + 1] = [trade(piece, 1, n_row) for piece in halves[1]]

    logits = lax.dot_general(
        router_all, after(normed2, sent), (((0,), (1,)), ((), ())), preferred_element_type=F32
    )
    top_logit = jnp.max(jnp.where(chosen, logits, -jnp.inf), axis=0, keepdims=True)
    raised = jnp.where(chosen, jnp.exp(logits - top_logit), 0.0)
    gate_probs = raised / jnp.sum(raised, axis=0, keepdims=True)
    own_probs = lax.dynamic_slice_in_dim(gate_probs, col * local_experts, local_experts, 0)

    slot_gates = []
    for step in steps:
        held = [
            jnp.sum(jnp.where(hits[e][step], of_peer(own_probs, step, e), 0.0), axis=1)
            for e in range(per_device)
        ]
        slot_gates.append(jnp.stack(held))
    slot_gates = swap_small(slot_gates)

    all_rows[0], slot_gates, later_rows = lax.optimization_barrier(
        (all_rows[0], slot_gates, normed2)
    )
    for e in range(1, per_device):
        sent.append(send_rows(e, far, later_rows))
    far_cots = after([cot_alls[base] for base in far_bases], sent, later_rows)
    for base, cots in zip(far_bases, far_cots):
        hand_on(base, grad_rows_of(base, cots))

    both = range(per_device)
    calls, grads_back = {}, [[None] * n_row for e in range(per_device)]

    def gates_of(e, step):
        return jnp.concatenate([slot_gates[step][e], slot_gates[step + 1][e]])[:, None]

    def expert_call(e, step, gates):
        xs = [all_rows[e][step], all_rows[e][step + 1]]
        cs = [grad_rows_at[step][e], grad_rows_at[step + 1][e]]
        act, grad_pre, sums, *back = run_expert(xs, cs, gates, w_in[e], w_back[e])
        calls[e, step] = [xs, cs, [act], [grad_pre], [sums], back]

    def send_back(e, step):
        for i, piece in enumerate(calls[e, step][-1]):
            grads_back[e][step + i] = trade(piece, step + i, n_row)

    def far_calls(e):
        return [calls[e, step] for step in far_bases]

    for step in far_bases:
        expert_call(0, step, gates_of(0, step))
        send_back(0, step)
    for e in range(1, per_device):
        all_rows[e] = after(all_rows[e], far_calls(0))
        for step in far_bases:
            expert_call(e, step, gates_of(e, step))
    every = [(e, step) for e in range(per_device) for step in steps]
    ranks = jnp.concatenate([of_peer(slot_rank, step, e) for e, step in every])
    near_gates = [gates_of(e, 0) for e in both]
    near_cots, near_gates, ranks, _ = lax.optimization_barrier(
        (cot_alls[0], near_gates, ranks, [far_calls(e) for e in both])
    )
    near_halves = grad_rows_of(0, near_cots)
    for e in range(1, per_device):
        held, grads_back[e - 1], near_halves = lax.optimization_barrier(
            (far_calls(e), grads_back[e - 1], near_halves)
        )
        for step, call in zip(far_bases, held):
            calls[e, step] = call
            send_back(e, step)
    hand_on(0, near_halves)
    for e in range(per_device):
        expert_call(e, 0, near_gates[e])
        send_back(e, 0)
    last_near = (per_device - 1, 0)
    calls[last_near], grads_back[-1] = lax.optimization_barrier((calls[last_near], grads_back[-1]))

    def joined(e, which):
        return jnp.concatenate([piece for step in steps[::2] for piece in calls[e, step][which]])

    grad_normed2_part = combine(ranks, [grads_back[e][step] for e, step in every])

    calls = after(calls, grad_normed2_part)
    scalars = [joined(e, 4) for e in range(per_device)]
    scalars = jnp.stack(scalars)
    scalars_back = swap_small(
        [scalars[:, step * capacity : (step + 1) * capacity] for step in steps]
    )
    branch_back, weight_grads = [], []
    for e in range(per_device):
        rows, grad_rows, act, grad_pre = (joined(e, which) for which in range(4))
        out = contract_last(act, w_back[e], BF16)
        branch_back.append(
            trade_all([out[step * capacity : (step + 1) * capacity] for step in steps])
        )
        grad_in = contract_first(rows, grad_pre, BF16)
        weight_grads.append(
            (
                grad_in[:, :unit_count],
                grad_in[:, unit_count:],
                contract_first(grad_rows, act, BF16),
            )
        )
    grad_normed2 = scatter_partial(grad_normed2_part).astype(F32)

    grad_own = jnp.zeros((local_experts, tok_count), F32)
    inner_own = jnp.zeros((1, tok_count), F32)
    own_rows = jnp.arange(local_experts, dtype=jnp.int32)[:, None]
    for e in range(per_device):
        for step in steps:
            expert = owned_at(peers[step])[0] + e
            back = scalars_back[step][e]
            spread = jnp.sum(jnp.where(hits[e][step], back[:, :1], 0.0), axis=0, keepdims=True)
            grad_own = grad_own + jnp.where(own_rows == expert, spread, 0.0)
            inner_own = inner_own + jnp.sum(
                jnp.where(hits[e][step], back[:, 1:], 0.0), axis=0, keepdims=True
            )
    small = jnp.concatenate([grad_own, inner_own], axis=0)
    small, branch_back[0] = lax.optimization_barrier((small, branch_back[0]))
    small = lax.all_to_all(
        jnp.broadcast_to(small.astype(BF16)[None], (n_col,) + small.shape), "col", 0, 0, tiled=True
    )
    small, branch_back = lax.optimization_barrier((small, branch_back))
    small = small.astype(F32)
    grad_gates = small[:, :local_experts].reshape(E, tok_count)
    grad_logits = gate_probs * (
        grad_gates - jnp.sum(gate_probs * grad_gates, axis=0, keepdims=True)
    )
    grad_logits = grad_logits.astype(BF16)
    inner_mid = jnp.sum(small[:, local_experts], axis=0) + jnp.sum(
        grad_logits.astype(F32) * logits, axis=0
    )
    inner_mid = (inner_mid / D)[:, None]
    grad_router = lax.dot_general(
        normed2, grad_logits, (((0,), (1,)), ((), ())), preferred_element_type=F32
    )
    router_local = lax.dynamic_slice_in_dim(router_all, column_start, feat_local, 0)
    grad_unit_mid = grad_normed2 + lax.dot_general(
        grad_logits, router_local, (((0,), (1,)), ((), ())), preferred_element_type=F32
    )
    unit_mid = mixed * scale_mid
    grad_norm2 = jnp.sum(grad_unit_mid * unit_mid, axis=0)
    scaled_mid = grad_unit_mid * norm2_gain
    grad_mixed = cot_b.astype(F32) + scale_mid * (scaled_mid - unit_mid * inner_mid)
    def held_slices(which, experts):
        return [
            jnp.stack(
                [
                    lax.dynamic_slice_in_dim(
                        weight_grads[e][which], peers[step] * rows_local, rows_local, 0
                    )
                    for e in experts
                ]
            )
            for step in steps
        ]

    def to_holders(pieces, *earlier):
        return trade_all(after(pieces, *earlier))

    gate_slices, up_slices = held_slices(0, both), held_slices(1, both)
    grad_mixed_b, gate_slices, up_slices = lax.optimization_barrier(
        (grad_mixed.astype(BF16), gate_slices, up_slices)
    )
    grad_branch = gather_features(grad_mixed_b)
    gate_pieces = to_holders(gate_slices)

    def to_rows(pieces):
        flat, places = [], []
        for e, held in enumerate(pieces):
            for step in steps:
                first, _, unit = owned_at(peers[step])
                flat.append(held[step])
                places += [first + e, unit]
        return place(jnp.stack(places), flat, local_experts, hidden_units)

    def sum_cores(grad):
        parts = [
            lax.dynamic_slice_in_dim(grad, peers[step] * rows_local, rows_local, 0)
            for step in steps
        ]
        other = trade(jnp.stack(parts[1::2]), 1, n_row).astype(F32)
        sums = [part.astype(F32) + other[i] for i, part in enumerate(parts[::2])]
        return [sums[0]] + [part.astype(grad.dtype) for part in sums[1:]]

    def sum_chips(sums):
        total = sums[0]
        for part, base in zip(sums[1:], far_bases):
            total = total + trade(part, base, n_row).astype(F32)
        return total

    def sum_groups(grad, *earlier):
        return sum_chips(sum_cores(after(grad, *earlier)))

    combined_part = combine(ranks, [branch_back[e][step] for e, step in every])
    grad_branch, gate_pieces, combined_part = lax.optimization_barrier(
        (grad_branch, gate_pieces, combined_part)
    )
    up_pieces = to_holders(up_slices, gate_pieces)

    combined = scatter_partial(combined_part)

    grad_w_out = contract_first(grad_branch, attended_b, BF16)
    grad_w_gate = to_rows([gate_pieces])
    grad_attended = plain_dot(after(grad_branch, grad_w_gate), w_out_own, BF16)
    grad_q, grad_k, grad_v, grad_query_gain, grad_key_gain = attend_back(
        query_rot, key_rot, values_b, grad_attended, log_totals, seg_q, seg_k, raw_qk,
        q_gain, k_gain, cosine, sine,
    )
    grad_qkv = jnp.concatenate([grad_q, grad_k, grad_v], axis=1)
    grad_w_out = sum_groups(grad_w_out)
    grad_router = sum_groups(grad_router, grad_branch).T
    down_slices = [held_slices(2, [e]) for e in range(per_device)]
    grad_qkv, up_pieces, combined, down_slices, grad_w_out, grad_router = (
        lax.optimization_barrier(
            (grad_qkv, up_pieces, combined, down_slices, grad_w_out, grad_router)
        )
    )
    down_pieces = [to_holders(down_slices[0])]
    grad_normed1_part = through_heads(grad_qkv, weight_heads)
    grad_unit_in = scatter_partial(grad_normed1_part)
    output = (mixed + combined.astype(F32)).astype(BF16)[inverse]
    grad_w_up = to_rows([up_pieces])
    grad_normed1_part, down_pieces, output, grad_w_up = lax.optimization_barrier(
        (grad_normed1_part, down_pieces, output, grad_w_up)
    )
    down_pieces += [to_holders(held, down_pieces) for held in down_slices[1:]]
    inner_in = jnp.sum(
        grad_qkv.astype(F32) * jnp.concatenate([raw_qk, values_b.astype(F32)], axis=1), axis=1
    )
    packed = packed_b.astype(F32)
    unit_in = packed * scale_in
    unit_all = gathered[:tok_count].astype(F32) * scale_in
    grad_norm1 = jnp.sum(grad_normed1_part.astype(F32) * unit_all, axis=0)
    def for_all(vector):
        return jnp.broadcast_to(vector[None], (n_col,) + vector.shape)

    vectors = jnp.concatenate(
        [
            for_all(inner_in),
            for_all(grad_query_gain[0]),
            for_all(grad_key_gain[0]),
            grad_norm1.reshape(n_col, feat_local),
        ],
        axis=1,
    )
    heads_sums = sum_cores(contract_first(normed1, grad_qkv, BF16))
    vectors, heads_sums = lax.optimization_barrier((vectors, heads_sums))
    vectors = jnp.sum(lax.all_to_all(vectors, "col", 0, 0, tiled=True), axis=0)
    vectors, down_pieces, heads_sums = lax.optimization_barrier(
        (vectors, down_pieces, heads_sums)
    )
    inner_in = vectors[:tok_count, None] / D
    vectors = jnp.concatenate([vectors[tok_count:], grad_norm2])
    vectors = sum(trade(vectors, step, n_row) for step in steps)
    grad_heads = sum_chips(heads_sums)
    grad_unit_in, vectors, inner_in, grad_heads = lax.optimization_barrier(
        (grad_unit_in, vectors, inner_in, grad_heads)
    )
    grad_unit_in = grad_unit_in.astype(F32)
    scaled_in = grad_unit_in * norm1_gain
    grad_input = (grad_mixed + scale_in * (scaled_in - unit_in * inner_in))[inverse]

    grad_w_query, grad_w_key, grad_w_value = (
        grad_heads[:, i * width_local : (i + 1) * width_local] for i in range(3)
    )
    grad_w_down = to_rows(down_pieces)

    grad_query_gain, grad_key_gain = vectors[:DH], vectors[DH : 2 * DH]
    grad_norm1 = vectors[2 * DH : 2 * DH + feat_local]
    grad_norm2 = vectors[2 * DH + feat_local :]
    return (
        output,
        grad_input,
        grad_norm1,
        grad_query_gain,
        grad_key_gain,
        grad_w_query,
        grad_w_key,
        grad_w_value,
        grad_w_out,
        grad_norm2,
        grad_router,
        grad_w_gate,
        grad_w_up,
        grad_w_down,
    )


def solution(mesh):
    return jax.shard_map(
        body,
        mesh=mesh,
        in_specs=(
            P("row", "col"),
            P("row", None),
            P("row", None),
            P("row"),
            P("row", None),
            P("col"),
            P(),
            P(),
            P("row", "col"),
            P("row", "col"),
            P("row", "col"),
            P("row", "col"),
            P("col"),
            P(None, "row"),
            P("col", "row", None),
            P("col", "row", None),
            P("col", "row", None),
            P("row", "col"),
        ),
        out_specs=(
            P("row", "col"),
            P("row", "col"),
            P("col"),
            P(),
            P(),
            P("row", "col"),
            P("row", "col"),
            P("row", "col"),
            P("row", "col"),
            P("col"),
            P(None, "row"),
            P("col", "row", None),
            P("col", "row", None),
            P("col", "row", None),
        ),
        check_vma=False,
    )
```
